128 devices in a mesh: shot: 4 (over y_lo, core), gx: 4 (over z), gy: 8 (over x, y_hi).
Axes of the slice: x: 4, y: 4 (y_hi: 2, y_lo: 2; y = y_hi * 2 + y_lo), z: 4, core: 2. Of those that a mesh axis runs over, the one named last changes fastest.
Arguments:
- model_tiles: float32 [256, 256, 128], P(('shot', 'gx'), 'gy'), may hold values from 0.2 to 0.45
- owner_map: int32 [16], replicated, may hold values from 0 to 15, each once
- offsets: int32 [4], P('shot'), may hold values from 0 to 12
- field_now: float32 [4, 2, 64, 256, 128], P('shot', None, 'gx', 'gy'), may hold values from -6 to 6
- field_prev: float32 [4, 2, 64, 256, 128], P('shot', None, 'gx', 'gy'), may hold values from -6 to 6
- sources: int32 [4, 2, 3], P('shot'), may hold values from 0 to 255, as said below
- wavelet: float32 [4, 2, 8], P('shot'), may hold values from -6 to 6
- receivers: int32 [4, 256, 3], P('shot'), may hold values from 0 to 255, as said below
Outputs:
- out_now: float32 [4, 2, 64, 256, 128], P('shot', None, 'gx', 'gy')
- out_prev: float32 [4, 2, 64, 256, 128], P('shot', None, 'gx', 'gy')
- traces: float32 [4, 2, 256, 8], P('shot')
The draws below stay inside these ranges and needn't reach their ends.
Inputs may be any that keep to these rules, and one draw needn't show every extreme that they name: `sources`: each row is a cell of the group's aperture: first entry below 64, second below 256, third below 128. `receivers`: each row is a cell of the group's aperture: first entry below 64, second below 256, third below 128.
All inputs are finite; a program needn't handle non-finite values.
Results may differ from the reference program's by a relative error of at most 0.0003.
Values sent between devices are 32-bit elements; how exact they have to be, the bound alone decides.
A program may use at most 128 MiB of HBM per device.

```python
import jax
import jax.numpy as jnp
from jax import lax

BX = 16
BZ = 128
SHOTS = 2
STEPS = 8
RECS = 256
GROUPS = 4
TCOLS = 16
NXA = 64
NYA = 256
N_GX = 4


def cell_points(key, amount):
    key_x, key_y, key_z = jax.random.split(key, 3)
    along_x = jax.random.randint(key_x, (GROUPS, amount), 0, NXA, dtype=jnp.int32)
    along_y = jax.random.randint(key_y, (GROUPS, amount), 0, NYA, dtype=jnp.int32)
    along_z = jax.random.randint(key_z, (GROUPS, amount), 0, BZ, dtype=jnp.int32)
    points = jnp.stack([along_x, along_y, along_z], axis=-1)
    points = points.at[0, 0].set(jnp.array([NXA - 1, NYA - 1, BZ - 1], dtype=jnp.int32))
    points = points.at[0, amount - 1].set(jnp.zeros((3,), jnp.int32))
    return points


def draw_sources(key, part):
    return cell_points(jax.random.fold_in(key, 11), SHOTS)


def draw_receivers(key, part):
    return cell_points(jax.random.fold_in(key, 23), RECS)


def place_ends(drawn, stream_key, least, largest):
    extent = drawn.shape
    spot = [jax.random.randint(jax.random.fold_in(stream_key, axis), (), 0, extent[axis]) for axis in range(len(extent))]
    drawn = drawn.at[tuple(spot)].set(least)
    longest = extent.index(max(extent))
    spot[longest] = (spot[longest] + 1) % extent[longest]
    return drawn.at[tuple(spot)].set(largest)


def levels(rng, dims, cuts, least, high):
    loudness, own = 1.0, jax.random.fold_in(rng, 6)
    for dim, parts in cuts:
        steps = jnp.exp(jax.random.uniform(jax.random.fold_in(own, dim), (parts,), jnp.float32, least / len(cuts), high / len(cuts)))
        loudness = loudness * jnp.repeat(steps, dims[dim] // parts).reshape([-1 if axis == dim else 1 for axis in range(len(dims))])
    return loudness


def scatter_about(rng, extent, scale, most, shards=(), held_as=jnp.bfloat16):
    result = scale * jax.random.normal(rng, extent, jnp.float32)
    if shards:
        result = result * levels(rng, extent, shards, -0.22, 0.18)
    return jnp.clip(result, -most, most).astype(held_as)


def setup_inputs(seed: int = 0) -> dict:
    keys = jax.random.split(jax.random.key(seed), 9)
    model_tiles = jnp.clip(0.2 + 0.24999999 * jax.random.uniform(keys[0], (TCOLS * BX, NYA, BZ), jnp.float32) ** levels(keys[0], (TCOLS * BX, NYA, BZ), ((0, 16), (1, 8)), -0.2, 0.2), 0.2, 0.45)
    owner_map = jax.random.permutation(keys[1], TCOLS).astype(jnp.int32)
    offsets = place_ends(jax.random.randint(keys[2], (GROUPS,), 0, TCOLS - N_GX + 1), jax.random.fold_in(keys[2], 1), 0, TCOLS - N_GX).astype(jnp.int32)
    field_now = scatter_about(keys[3], (GROUPS, SHOTS, NXA, NYA, BZ), 1.0, 6.0, ((0, 4), (2, 4), (3, 8)), jnp.float32)
    field_prev = scatter_about(keys[4], (GROUPS, SHOTS, NXA, NYA, BZ), 1.0, 6.0, ((0, 4), (2, 4), (3, 8)), jnp.float32)
    sources = draw_sources(jax.random.fold_in(keys[8], 71), 0)
    wavelet = scatter_about(keys[6], (GROUPS, SHOTS, STEPS), 1.0, 6.0, ((0, 4),), jnp.float32)
    receivers = draw_receivers(jax.random.fold_in(keys[8], 71), 0)
    return {"model_tiles": model_tiles, "owner_map": owner_map, "offsets": offsets, "field_now": field_now, "field_prev": field_prev, "sources": sources, "wavelet": wavelet, "receivers": receivers}


center_weight = -2.5
near_weight = 4.0 / 3.0
far_weight = -1.0 / 12.0
damp_peak = 0.3


def laplace(padded):
    middle = padded[:, 2:-2, 2:-2, 2:-2]
    along_x = center_weight * middle + near_weight * (padded[:, 3:-1, 2:-2, 2:-2] + padded[:, 1:-3, 2:-2, 2:-2]) + far_weight * (padded[:, 4:, 2:-2, 2:-2] + padded[:, :-4, 2:-2, 2:-2])
    along_y = center_weight * middle + near_weight * (padded[:, 2:-2, 3:-1, 2:-2] + padded[:, 2:-2, 1:-3, 2:-2]) + far_weight * (padded[:, 2:-2, 4:, 2:-2] + padded[:, 2:-2, :-4, 2:-2])
    along_z = center_weight * middle + near_weight * (padded[:, 2:-2, 2:-2, 3:-1] + padded[:, 2:-2, 2:-2, 1:-3]) + far_weight * (padded[:, 2:-2, 2:-2, 4:] + padded[:, 2:-2, 2:-2, :-4])
    return along_x + along_y + along_z


def damping(x_cells, y_cells, width, x_total, y_total):
    x_depth = jnp.maximum(width - jnp.minimum(x_cells + 1, x_total - x_cells), 0).astype(jnp.float32) / width
    y_depth = jnp.maximum(width - jnp.minimum(y_cells + 1, y_total - y_cells), 0).astype(jnp.float32) / width
    return damp_peak * (x_depth[:, None] * x_depth[:, None] + y_depth[None, :] * y_depth[None, :])


def injection(x_cells, y_cells, z_cells, source_cells, amplitude):
    on_x = (x_cells[None, :] == source_cells[:, 0:1]).astype(jnp.float32)
    on_y = (y_cells[None, :] == source_cells[:, 1:2]).astype(jnp.float32)
    on_z = (z_cells[None, :] == source_cells[:, 2:3]).astype(jnp.float32)
    return amplitude[:, None, None, None] * on_x[:, :, None, None] * on_y[:, None, :, None] * on_z[:, None, None, :]


def advance(padded, previous, coef, damp, inject):
    middle = padded[:, 2:-2, 2:-2, 2:-2]
    return (2.0 * middle - (1.0 - damp) * previous + coef * laplace(padded) + inject) / (1.0 + damp)


def reference(model_tiles, owner_map, offsets, field_now, field_prev, sources, wavelet, receivers):
    blocks = model_tiles.reshape(TCOLS, BX, NYA, BZ)
    model = jnp.take(blocks, owner_map.astype(jnp.int32), axis=0).reshape(TCOLS * BX, NYA, BZ)
    x_cells = jnp.arange(NXA, dtype=jnp.int32)
    y_cells = jnp.arange(NYA, dtype=jnp.int32)
    z_cells = jnp.arange(BZ, dtype=jnp.int32)
    damp = damping(x_cells, y_cells, BX, NXA, NYA)[:, :, None]
    now_list = []
    prev_list = []
    trace_list = []
    for group in range(GROUPS):
        speed = lax.dynamic_slice_in_dim(model, (offsets[group] * BX).astype(jnp.int32), NXA, 0)
        coef = speed * speed
        current = field_now[group]
        previous = field_prev[group]
        samples = []
        for step in range(STEPS):
            padded = jnp.pad(current, ((0, 0), (2, 2), (2, 2), (2, 2)))
            inject = injection(x_cells, y_cells, z_cells, sources[group], wavelet[group, :, step])
            fresh = advance(padded, previous, coef, damp, inject)
            samples.append(fresh[:, receivers[group, :, 0], receivers[group, :, 1], receivers[group, :, 2]])
            previous = current
            current = fresh
        now_list.append(current)
        prev_list.append(previous)
        trace_list.append(jnp.stack(samples, axis=-1))
    return jnp.stack(now_list), jnp.stack(prev_list), jnp.stack(trace_list)
```

```python
import jax
import jax.numpy as jnp
from jax import lax
from jax.experimental import pallas as pl
from jax.experimental.pallas import tpu as pltpu
from jax.sharding import PartitionSpec as P

STEPS = 8
SHOTS = 2
NS, NX, NY = 4, 4, 8
GROUP = NS * NX
PEERS = NX * NY
BX, BY, BZ = 16, 32, 128
AX, AY = NX * BX, NY * BY
RECS = 256
PX, PY = BX + 8, BY + 16
X0, Y0 = 4, 8
MESH = pl.DeviceIdType.MESH
F32 = jnp.float32


def loop(n, body, start=0):
    lax.fori_loop(start, n, lambda k, c: (body(k), c)[1], 0)


def kernel(
    tiles, owner, offset, now, prev, sources, wavelet, receivers,
    out_now, out_prev, out_traces,
    U, MT, R, SEL, SELH, EDGE, YM, CO, KC, KA, K2, INV, EY,
    YS, YR, CS, CR, PS, PR, OFS, OFR, OFM, OH, IDL, XB, TS, TR,
    in_sem, off_s, off_r, a_s, a_r, b_s, b_r, bh_s, bh_r, e_s, e_r,
    h_s, h_r, p_s, p_r, t_s, t_r,
):
    s = lax.axis_index("shot")
    i = lax.axis_index("gx")
    j = lax.axis_index("gy")
    me = s * NX + i
    mine = i * NY + j

    def member(d, row):
        return (d // NX, lax.rem(d, NX), row)

    def peer(q):
        return (s, q // NY, lax.rem(q, NY))

    def send(src, dst, ssem, rsem, dev):
        return pltpu.make_async_remote_copy(
            src_ref=src, dst_ref=dst, send_sem=ssem, recv_sem=rsem,
            device_id=dev, device_id_type=MESH,
        )

    inner_x = pl.ds(X0, BX)
    inner_y = pl.ds(Y0, BY)
    has = [i > 0, i < NX - 1, j > 0, j < NY - 1]

    cp_mt = pltpu.make_async_copy(tiles, MT, in_sem.at[0])
    cp_now = pltpu.make_async_copy(now.at[0], U.at[0, :, inner_x, inner_y, :], in_sem.at[1])
    cp_prev = pltpu.make_async_copy(prev.at[0], U.at[2, :, inner_x, inner_y, :], in_sem.at[2])
    cp_mt.start()
    cp_now.start()
    cp_prev.start()

    side_planes = jnp.zeros((4, PY, BZ), F32)
    side_rows = jnp.zeros((8, BZ), F32)
    for b in range(3):
        for sh in range(SHOTS):
            U[b, sh, 0:4] = side_planes
            U[b, sh, PX - 4 : PX] = side_planes

    def zero_rows(x):
        for b in range(3):
            for sh in range(SHOTS):
                U[b, sh, X0 + x, 0:8] = side_rows
                U[b, sh, X0 + x, PY - 8 : PY] = side_rows
        CO[X0 + x, 0:8] = side_rows
        CO[X0 + x, PY - 8 : PY] = side_rows

    loop(BX, zero_rows)
    CO[0:4] = side_planes
    CO[PX - 4 : PX] = side_planes

    barrier = pltpu.get_barrier_semaphore()

    def greet(dev):
        pl.semaphore_signal(barrier, inc=1, device_id=dev, device_id_type=MESH)

    loop(GROUP, lambda r: greet(member(lax.rem(me + r, GROUP), j)), 1)

    @pl.when(has[2])
    def _():
        loop(GROUP, lambda d: greet(member(d, j - 1)))

    @pl.when(has[3])
    def _():
        loop(GROUP, lambda d: greet(member(d, j + 1)))

    def far(row):
        @pl.when((row > j + 1) | (row < j - 1))
        def _():
            for ii in range(NX):
                greet((s, ii, row))

    loop(NY, far)
    near = has[2].astype(jnp.int32) + has[3].astype(jnp.int32)
    pl.semaphore_wait(barrier, GROUP - 1 + GROUP * near + NX * (NY - 1 - near))

    OFS[...] = jnp.full((1, BZ), offset[0], jnp.int32)

    def off_copy(r):
        return send(OFS, OFR.at[s], off_s.at[r], off_r.at[s], (lax.rem(s + r, NS), i, j))

    for r in range(1, NS):
        off_copy(r).start()
    OFR[s] = jnp.full((1, BZ), offset[0], jnp.int32)

    cp_mt.wait()

    def a_copy(r):
        d = lax.rem(me + r, GROUP)
        return send(MT.at[d], R.at[me], a_s.at[r], a_r.at[me], member(d, j))

    loop(GROUP, lambda r: a_copy(r).start(), 1)
    R[me] = MT[me]

    def pack(buf, depth, store):
        def one(x):
            for sh in range(SHOTS):
                store[0, sh * BX + x] = U[buf, sh, X0 + x, pl.ds(Y0, depth)]
                store[1, sh * BX + x] = U[buf, sh, X0 + x, pl.ds(Y0 + BY - depth, depth)]

        loop(BX, one)

    def unpack(buf, depth, store):
        def one(x):
            for sh in range(SHOTS):
                @pl.when(has[2])
                def _():
                    U[buf, sh, X0 + x, pl.ds(Y0 - depth, depth)] = store[0, sh * BX + x]

                @pl.when(has[3])
                def _():
                    U[buf, sh, X0 + x, pl.ds(Y0 + BY, depth)] = store[1, sh * BX + x]

        loop(BX, one)

    corners = [(-1, -1), (-1, 1), (1, -1), (1, 1)]

    def halo_list(buf, slot):
        ends = [pl.ds(X0, 4), pl.ds(X0 + BX - 4, 4)]
        lands = [pl.ds(X0 + BX, 4), pl.ds(X0 - 4, 4)]
        found = []
        for n, dx in ((0, -1), (1, 1)):
            found.append((
                has[n], U.at[buf, :, ends[n], inner_y, :], U.at[buf, :, lands[n], inner_y, :],
                n, 1 - n, (s, i + dx, j),
            ))
        for n, dy in ((0, -1), (1, 1)):
            found.append((
                has[2 + n], YS.at[n], YR.at[slot, 1 - n], 2 + n, 3 - n, (s, i, j + dy),
            ))
        for n, (dx, dy) in enumerate(corners):
            ok = has[0 if dx < 0 else 1] & has[2 if dy < 0 else 3]
            found.append((
                ok, CS.at[n], CR.at[slot, 3 - n], 4 + n, 7 - n, (s, i + dx, j + dy),
            ))
        return found

    def halo_send(buf, slot):
        pack(buf, 4, YS)
        for n, (dx, dy) in enumerate(corners):
            for sh in range(SHOTS):
                for k in range(2):
                    x = X0 + k if dx < 0 else X0 + BX - 2 + k
                    y = Y0 if dy < 0 else Y0 + BY - 2
                    CS[n, sh * 4 + k * 2 : sh * 4 + k * 2 + 2] = U[buf, sh, x, y : y + 2]
        for ok, src, dst, n, m, dev in halo_list(buf, slot):
            @pl.when(ok)
            def _():
                send(src, dst, h_s.at[slot, n], h_r.at[slot, m], dev).start()

    def halo_wait(buf, slot):
        copies = halo_list(buf, slot)
        opposite = [1, 0, 3, 2, 7, 6, 5, 4]
        for n in range(8):
            ok, src, dst, _, m, dev = copies[n]
            back = copies[opposite[n]]

            @pl.when(ok)
            def _():
                send(src, dst, h_s.at[slot, n], h_r.at[slot, m], dev).wait_send()
                send(back[1], back[2], h_s.at[slot, n], h_r.at[slot, n], dev).wait_recv()

        unpack(buf, 4, YR.at[slot])
        for n, (dx, dy) in enumerate(corners):
            @pl.when(copies[4 + n][0])
            def _():
                for sh in range(SHOTS):
                    for k in range(2):
                        x = X0 - 2 + k if dx < 0 else X0 + BX + k
                        y = Y0 - 2 if dy < 0 else Y0 + BY
                        U[buf, sh, x, y : y + 2] = CR[slot, n, sh * 4 + k * 2 : sh * 4 + k * 2 + 2]

    cp_now.wait()
    halo_send(0, 0)
    cp_prev.wait()
    pack(2, 2, PS)
    prev_ends = [pl.ds(X0, 2), pl.ds(X0 + BX - 2, 2)]
    prev_lands = [pl.ds(X0 + BX, 2), pl.ds(X0 - 2, 2)]
    prev_list = []
    for n, dx in ((0, -1), (1, 1)):
        prev_list.append((
            has[n], U.at[2, :, prev_ends[n], inner_y, :], U.at[2, :, prev_lands[n], inner_y, :],
            n, 1 - n, (s, i + dx, j),
        ))
    for n, dy in ((0, -1), (1, 1)):
        prev_list.append((has[2 + n], PS.at[n], PR.at[1 - n], 2 + n, 3 - n, (s, i, j + dy)))
    for ok, src, dst, n, m, dev in prev_list:
        @pl.when(ok)
        def _():
            send(src, dst, p_s.at[n], p_r.at[m], dev).start()

    rows = lax.broadcasted_iota(jnp.int32, (8, BZ), 0)
    lanes = lax.broadcasted_iota(jnp.int32, (8, BZ), 1)
    first_lane = (lanes > 0).astype(F32)
    second_lane = (lanes > 1).astype(F32)
    last_lane = (lanes < BZ - 1).astype(F32)
    last_two = (lanes < BZ - 2).astype(F32)

    def weight(cell, total):
        return jnp.maximum(16 - jnp.minimum(cell + 1, total - cell), 0).astype(F32) / 16.0

    def damping_tables(x):
        wx = weight(jnp.full((8, BZ), i * BX + x - X0, jnp.int32), AX)
        for q in range(5):
            at = pl.ds(Y0 - 4 + 8 * q, 8)
            wy = weight(rows + (j * BY - 4 + 8 * q), AY)
            d = 0.3 * (wx * wx + wy * wy)
            inv = 1.0 / (1.0 + d)
            INV[x, at] = inv
            K2[x, at] = (1.0 - d) * inv

    loop(X0 + BX + 2, damping_tables, X0 - 2)

    for sh in range(SHOTS):
        wx = weight(jnp.full((8, BZ), sources[0, sh, 0], jnp.int32), AX)
        for q in range(5):
            cells = rows + (j * BY - 4 + 8 * q)
            wy = weight(cells, AY)
            inv = 1.0 / (1.0 + 0.3 * (wx * wx + wy * wy))
            hit = (cells == sources[0, sh, 1]) & (lanes == sources[0, sh, 2])
            EY[sh, pl.ds(Y0 - 4 + 8 * q, 8)] = jnp.where(hit, inv, 0.0)

    rx = receivers[0, :, 0:1] - i * BX
    ry = receivers[0, :, 1:2] - j * BY
    rz = receivers[0, :, 2:3]
    here = (rx >= 0) & (rx < BX) & (ry >= 0) & (ry < BY)
    ids = jnp.where(here, rx * BY + ry + 1, 0).astype(F32)
    deep = lax.broadcasted_iota(jnp.int32, (RECS, 2 * BZ), 1)
    deep = jnp.where(deep >= BZ, deep - BZ, deep)
    OH[...] = jnp.where(deep == rz, 1.0, 0.0).astype(jnp.bfloat16)
    square = (RECS, RECS)
    eye = lax.broadcasted_iota(jnp.int32, square, 0) == lax.broadcasted_iota(jnp.int32, square, 1)
    IDL[...] = jnp.sum(jnp.where(eye, ids, 0.0), axis=0, keepdims=True)

    for r in range(1, NS):
        off_copy(r).wait_send()
        other = lax.rem(s + r, NS)
        send(OFS, OFR.at[other], off_s.at[r], off_r.at[other], (other, i, j)).wait_recv()
    cp_off = pltpu.make_async_copy(OFR, OFM, in_sem.at[0])
    cp_off.start()
    cp_off.wait()

    def a_wait(r):
        a_copy(r).wait_send()
        d = lax.rem(me + r, GROUP)
        send(MT.at[d], R.at[d], a_s.at[r], a_r.at[d], member(d, j)).wait_recv()

    loop(GROUP, a_wait, 1)

    tail = me >= GROUP - 2
    head = me < 2
    shift = jnp.where(tail, -1, 1)

    def choose(d):
        column = OFM[d // NX, 0, 0] + lax.rem(d, NX)
        plane = R[owner[column]]
        SEL[d] = plane
        EDGE[0, d] = plane[BY - 2 : BY]
        EDGE[1, d] = plane[0:2]
        SELH[d] = R[owner[jnp.clip(column + shift, 0, GROUP - 1)]]

    loop(GROUP, choose)

    def b_copy(r):
        d = lax.rem(me + r, GROUP)
        return send(
            SEL.at[d], CO.at[X0 + me, inner_y, :], b_s.at[r], b_r.at[me], member(d, j)
        )

    halo_plane = jnp.where(tail, me - (GROUP - 2) + X0 - 2, X0 + BX + jnp.minimum(me, 1))
    halo_slot = jnp.where(tail, me - (GROUP - 2), 2 + jnp.minimum(me, 1))

    def bh_copy(r):
        d = lax.rem(me + r, GROUP)
        return send(
            SELH.at[d], CO.at[halo_plane, inner_y, :], bh_s.at[r], bh_r.at[halo_slot], member(d, j)
        )

    def bh_ok(d):
        c = lax.rem(d, NX)
        return (tail & (c > 0)) | (head & (c < NX - 1))

    def edge_copy(side, d):
        row = j + 1 if side == 0 else j - 1
        return send(
            EDGE.at[side, d], YM.at[side, me], e_s.at[side, d], e_r.at[side, me], member(d, row)
        )

    loop(GROUP, lambda r: b_copy(r).start(), 1)

    def bh_start(r):
        @pl.when(bh_ok(lax.rem(me + r, GROUP)))
        def _():
            bh_copy(r).start()

    loop(GROUP, bh_start, 1)
    for side, ok in ((0, has[3]), (1, has[2])):
        @pl.when(ok)
        def _():
            loop(GROUP, lambda d: edge_copy(side, d).start())

    CO[X0 + me, inner_y] = SEL[me]

    @pl.when(bh_ok(me))
    def _():
        CO[halo_plane, inner_y] = SELH[me]

    halo_wait(0, 0)
    for n in range(4):
        ok, src, dst, _, m, dev = prev_list[n]
        back = prev_list[[1, 0, 3, 2][n]]

        @pl.when(ok)
        def _():
            send(src, dst, p_s.at[n], p_r.at[m], dev).wait_send()
            send(back[1], back[2], p_s.at[n], p_r.at[n], dev).wait_recv()

    unpack(2, 2, PR)

    def b_wait(r):
        b_copy(r).wait_send()
        d = lax.rem(me + r, GROUP)
        send(
            SEL.at[d], CO.at[X0 + d, inner_y, :], b_s.at[r], b_r.at[d], member(d, j)
        ).wait_recv()

        @pl.when(bh_ok(d))
        def _():
            bh_copy(r).wait_send()

    loop(GROUP, b_wait, 1)
    for slot in range(4):
        source = GROUP - 2 + slot if slot < 2 else slot - 2
        plane = X0 - 2 + slot if slot < 2 else X0 + BX + slot - 2
        edge = has[0] if slot < 2 else has[1]

        @pl.when(edge & (me != source))
        def _():
            send(
                SELH.at[0], CO.at[plane, inner_y, :], bh_s.at[0], bh_r.at[slot], member(source, j)
            ).wait_recv()

    for side, to, back in ((0, has[3], has[2]), (1, has[2], has[3])):
        @pl.when(to)
        def _():
            loop(GROUP, lambda d: edge_copy(side, d).wait_send())

        @pl.when(back)
        def _():
            row = j - 1 if side == 0 else j + 1

            def one(d):
                send(
                    EDGE.at[side, d], YM.at[side, d], e_s.at[side, d], e_r.at[side, d],
                    member(d, row),
                ).wait_recv()

            loop(GROUP, one)

            def put(x):
                CO[X0 + x, pl.ds(Y0 - 2 if side == 0 else Y0 + BY, 2)] = YM[side, x]

            loop(BX, put)

    def model_tables(x):
        for q in range(5):
            at = pl.ds(Y0 - 4 + 8 * q, 8)
            speed = CO[x, at]
            inv = INV[x, at]
            scaled = speed * speed * inv
            KC[x, at] = 2.0 * inv - 7.5 * scaled
            KA[x, at] = (4.0 / 3.0) * scaled

    loop(X0 + BX + 2, model_tables, X0 - 2)

    def advance(read, write_from, write, x_lo, x_hi, y_lo, count, step):
        def plane(x):
            on = [
                jnp.where(sources[0, sh, 0] == i * BX + x - X0, wavelet[0, sh, step], 0.0)
                for sh in range(SHOTS)
            ]
            for q in range(count):
                y = y_lo + 8 * q
                at = pl.ds(y, 8)
                kc, ka, k2 = KC[x, at], KA[x, at], K2[x, at]
                for sh in range(SHOTS):
                    c = U[read, sh, x, at]
                    a = (U[read, sh, x + 1, at] + U[read, sh, x - 1, at]) + (
                        U[read, sh, x, pl.ds(y + 1, 8)] + U[read, sh, x, pl.ds(y - 1, 8)]
                    )
                    b = (U[read, sh, x + 2, at] + U[read, sh, x - 2, at]) + (
                        U[read, sh, x, pl.ds(y + 2, 8)] + U[read, sh, x, pl.ds(y - 2, 8)]
                    )
                    a = a + (
                        pltpu.roll(c, 1, 1) * first_lane + pltpu.roll(c, BZ - 1, 1) * last_lane
                    )
                    b = b + (
                        pltpu.roll(c, 2, 1) * second_lane + pltpu.roll(c, BZ - 2, 1) * last_two
                    )
                    fresh = (kc * c - k2 * U[write_from, sh, x, at]) + ka * (a - 0.0625 * b)
                    U[write, sh, x, at] = fresh + EY[sh, at] * on[sh]

        loop(x_hi, plane, x_lo)

    def outer_step(even, step):
        advance(even, 2, 2, X0 - 2, X0 + BX + 2, Y0 - 4, 5, step)

    def inner_step(even, odd_out, step):
        advance(2, even, odd_out, X0, X0 + BX, Y0, 4, step)

    row_ids = lax.broadcasted_iota(jnp.int32, (BX * BY, RECS), 0).astype(F32) + 1.0

    def sample(buf, step):
        def split(x):
            for sh in range(SHOTS):
                v = U[buf, sh, X0 + x, inner_y]
                high = v.astype(jnp.bfloat16)
                low = (v - high.astype(F32)).astype(jnp.bfloat16)
                at = pl.ds(pl.multiple_of((sh * BX + x) * BY, BY), BY)
                XB[at, 0:BZ] = high
                XB[at, BZ : 2 * BZ] = low

        loop(BX, split)
        for sh in range(SHOTS):
            picked = lax.dot_general(
                XB[sh * BX * BY : (sh + 1) * BX * BY], OH[...], (((1,), (1,)), ((), ())),
                preferred_element_type=F32,
            )
            got = jnp.sum(jnp.where(row_ids == IDL[...], picked, 0.0), axis=0, keepdims=True)
            TS[step, 2 * sh : 2 * sh + 1] = got[:, 0:128]
            TS[step, 2 * sh + 1 : 2 * sh + 2] = got[:, 128:256]

    def trace_copy(pair, r):
        at = pl.ds(2 * pair, 2)
        return send(
            TS.at[at], TR.at[mine, at], t_s.at[pair, r], t_r.at[pair, mine],
            peer(lax.rem(mine + r, PEERS)),
        )

    def trace_wait(pair, r):
        trace_copy(pair, r).wait_send()
        q = lax.rem(mine + r, PEERS)
        at = pl.ds(2 * pair, 2)
        send(TS.at[at], TR.at[q, at], t_s.at[pair, r], t_r.at[pair, q], peer(q)).wait_recv()

    def two_steps(pair):
        even = lax.rem(pair, 2)
        later = 1 - even
        outer_step(even, 2 * pair)
        inner_step(even, later, 2 * pair + 1)
        halo_send(later, later)
        sample(2, 2 * pair)
        sample(later, 2 * pair + 1)
        loop(PEERS, lambda r: trace_copy(pair, r).start(), 1)
        halo_wait(later, later)

    pairs = STEPS // 2
    loop(pairs - 1, two_steps)
    last = pairs - 1
    even = last % 2
    later = 1 - even
    outer_step(even, 2 * last)
    cp_out_prev = pltpu.make_async_copy(
        U.at[2, :, inner_x, inner_y, :], out_prev.at[0], in_sem.at[2]
    )
    cp_out_prev.start()
    inner_step(even, later, 2 * last + 1)
    cp_out_now = pltpu.make_async_copy(
        U.at[later, :, inner_x, inner_y, :], out_now.at[0], in_sem.at[1]
    )
    cp_out_now.start()
    sample(2, 2 * last)
    sample(later, 2 * last + 1)
    loop(PEERS, lambda r: trace_copy(last, r).start(), 1)
    out_traces[...] = TS[...]
    for pair in range(pairs):
        loop(PEERS, lambda r: trace_wait(pair, r), 1)

    def add(r):
        out_traces[...] += TR[lax.rem(mine + r, PEERS)]

    loop(PEERS, add, 1)
    cp_out_prev.wait()
    cp_out_now.wait()


def window(tiles, owner, offset, now, prev, sources, wavelet, receivers):
    any_spec = pl.BlockSpec(memory_space=pl.ANY)
    smem = pl.BlockSpec(memory_space=pltpu.SMEM)
    vmem = pl.BlockSpec(memory_space=pltpu.VMEM)
    buf = pltpu.VMEM
    dma = pltpu.SemaphoreType.DMA
    padded = (PX, PY, BZ)
    out_now, out_prev, traces = pl.pallas_call(
        kernel,
        out_shape=(
            jax.ShapeDtypeStruct(now.shape, F32),
            jax.ShapeDtypeStruct(prev.shape, F32),
            jax.ShapeDtypeStruct((STEPS, 2 * SHOTS, 128), F32),
        ),
        in_specs=[any_spec, smem, smem, any_spec, any_spec, smem, smem, vmem],
        out_specs=(any_spec, any_spec, vmem),
        scratch_shapes=[
            buf((3, SHOTS) + padded, F32),
            buf((BX, BY, BZ), F32),
            buf((GROUP, BY, BZ), F32),
            buf((GROUP, BY, BZ), F32),
            buf((GROUP, BY, BZ), F32),
            buf((2, GROUP, 2, BZ), F32),
            buf((2, GROUP, 2, BZ), F32),
            buf(padded, F32),
            buf(padded, F32),
            buf(padded, F32),
            buf(padded, F32),
            buf(padded, F32),
            buf((SHOTS, PY, BZ), F32),
            buf((2, SHOTS * BX, 4, BZ), F32),
            buf((2, 2, SHOTS * BX, 4, BZ), F32),
            buf((4, 8, BZ), F32),
            buf((2, 4, 8, BZ), F32),
            buf((2, SHOTS * BX, 2, BZ), F32),
            buf((2, SHOTS * BX, 2, BZ), F32),
            buf((1, BZ), jnp.int32),
            buf((NS, 1, BZ), jnp.int32),
            pltpu.SMEM((NS, 1, BZ), jnp.int32),
            buf((RECS, 2 * BZ), jnp.bfloat16),
            buf((1, RECS), F32),
            buf((SHOTS * BX * BY, 2 * BZ), jnp.bfloat16),
            buf((STEPS, 2 * SHOTS, 128), F32),
            buf((PEERS, STEPS, 2 * SHOTS, 128), F32),
            dma((3,)), dma((NS,)), dma((NS,)),
            dma((GROUP,)), dma((GROUP,)), dma((GROUP,)), dma((GROUP,)),
            dma((GROUP,)), dma((4,)), dma((2, GROUP)), dma((2, GROUP)),
            dma((2, 8)), dma((2, 8)), dma((4,)), dma((4,)),
            dma((STEPS // 2, PEERS)), dma((STEPS // 2, PEERS)),
        ],
        compiler_params=pltpu.CompilerParams(collective_id=0, has_side_effects=True),
    )(tiles, owner, offset, now, prev, sources, wavelet, receivers)
    traces = traces.reshape(STEPS, SHOTS, RECS)
    return out_now, out_prev, jnp.transpose(traces, (1, 2, 0))[None]


def solution(mesh):
    return jax.shard_map(
        window,
        mesh=mesh,
        in_specs=(
            P(("shot", "gx"), "gy", None),
            P(),
            P("shot"),
            P("shot", None, "gx", "gy", None),
            P("shot", None, "gx", "gy", None),
            P("shot", None, None),
            P("shot", None, None),
            P("shot", None, None),
        ),
        out_specs=(
            P("shot", None, "gx", "gy", None),
            P("shot", None, "gx", "gy", None),
            P("shot", None, None, None),
        ),
        check_vma=False,
    )
```

```python
import jax
import jax.numpy as jnp
from jax import lax
from jax.experimental import pallas as pl
from jax.experimental.pallas import tpu as pltpu
from jax.sharding import PartitionSpec as P

STEPS = 8
SHOTS = 2
NS, NX, NY = 4, 4, 8
GROUP = NS * NX
PEERS = NX * NY
BX, BY, BZ = 16, 32, 128
AX, AY = NX * BX, NY * BY
RECS = 256
PX, PY = BX + 8, BY + 16
X0, Y0 = 4, 8
MESH = pl.DeviceIdType.MESH
F32 = jnp.float32


def loop(n, body, start=0):
    lax.fori_loop(start, n, lambda k, c: (body(k), c)[1], 0)


def kernel(
    tiles, owner, offset, now, prev, sources, wavelet, receivers,
    out_now, out_prev, out_traces,
    U, MT, R, SEL, SELH, EDGE, YM, CO, KC, KA, K2, INV, EY,
    YS, YR, CS, CR, PS, PR, OFS, OFR, OFM, OH, IDL, XB, TS, TR,
    in_sem, off_s, off_r, a_sem, b_sem, bh_s, bh_r, e_sem,
    h_s, h_r, p_s, p_r, t_sem,
):
    s = lax.axis_index("shot")
    i = lax.axis_index("gx")
    j = lax.axis_index("gy")
    me = s * NX + i
    mine = i * NY + j

    def member(d, row):
        return (d >> 2, d & (NX - 1), row)

    def peer(q):
        return (s, q >> 3, q & (NY - 1))

    def other(r):
        return (me + r) & (GROUP - 1)

    def all_of(ref, sem):
        pltpu.make_async_copy(ref, ref, sem).wait()

    def send(src, dst, ssem, rsem, dev):
        return pltpu.make_async_remote_copy(
            src_ref=src, dst_ref=dst, send_sem=ssem, recv_sem=rsem,
            device_id=dev, device_id_type=MESH,
        )

    inner_x = pl.ds(X0, BX)
    inner_y = pl.ds(Y0, BY)
    has = [i > 0, i < NX - 1, j > 0, j < NY - 1]

    cp_mt = pltpu.make_async_copy(tiles, MT, in_sem.at[0])
    cp_now = pltpu.make_async_copy(now.at[0], U.at[0, :, inner_x, inner_y, :], in_sem.at[1])
    cp_prev = pltpu.make_async_copy(prev.at[0], U.at[2, :, inner_x, inner_y, :], in_sem.at[2])
    cp_mt.start()
    cp_now.start()
    cp_prev.start()

    side_planes = jnp.zeros((4, PY, BZ), F32)
    side_rows = jnp.zeros((8, BZ), F32)
    for b in range(3):
        for sh in range(SHOTS):
            U[b, sh, 0:4] = side_planes
            U[b, sh, PX - 4 : PX] = side_planes

    def zero_rows(x):
        for b in range(3):
            for sh in range(SHOTS):
                U[b, sh, X0 + x, 0:8] = side_rows
                U[b, sh, X0 + x, PY - 8 : PY] = side_rows
        CO[X0 + x, 0:8] = side_rows
        CO[X0 + x, PY - 8 : PY] = side_rows

    loop(BX, zero_rows)
    CO[0:4] = side_planes
    CO[PX - 4 : PX] = side_planes

    barrier = pltpu.get_barrier_semaphore()

    def greet(dev):
        pl.semaphore_signal(barrier, inc=1, device_id=dev, device_id_type=MESH)

    loop(GROUP, lambda r: greet(member(other(r), j)), 1)

    @pl.when(has[2])
    def _():
        loop(GROUP, lambda d: greet(member(d, j - 1)))

    @pl.when(has[3])
    def _():
        loop(GROUP, lambda d: greet(member(d, j + 1)))

    def far(row):
        @pl.when((row > j + 1) | (row < j - 1))
        def _():
            for ii in range(NX):
                greet((s, ii, row))

    loop(NY, far)
    near = has[2].astype(jnp.int32) + has[3].astype(jnp.int32)
    pl.semaphore_wait(barrier, GROUP - 1 + GROUP * near + NX * (NY - 1 - near))

    OFS[...] = jnp.full((1, BZ), offset[0], jnp.int32)

    def off_copy(r):
        return send(OFS, OFR.at[s], off_s.at[r], off_r.at[s], ((s + r) & (NS - 1), i, j))

    for r in range(1, NS):
        off_copy(r).start()
    OFR[s] = jnp.full((1, BZ), offset[0], jnp.int32)

    cp_mt.wait()

    def a_start(r):
        d = other(r)
        send(MT.at[d], R.at[me], a_sem.at[0], a_sem.at[1], member(d, j)).start()

    loop(GROUP, a_start, 1)
    R[me] = MT[me]

    def pack(buf, depth, store):
        for x in range(BX):
            for sh in range(SHOTS):
                store[0, sh * BX + x] = U[buf, sh, X0 + x, pl.ds(Y0, depth)]
                store[1, sh * BX + x] = U[buf, sh, X0 + x, pl.ds(Y0 + BY - depth, depth)]

    def unpack(buf, depth, store):
        for side, y in ((0, Y0 - depth), (1, Y0 + BY)):
            @pl.when(has[2 + side])
            def _():
                for x in range(BX):
                    for sh in range(SHOTS):
                        U[buf, sh, X0 + x, pl.ds(y, depth)] = store[side, sh * BX + x]

    corners = [(-1, -1), (-1, 1), (1, -1), (1, 1)]

    def halo_list(buf, slot):
        ends = [pl.ds(X0, 4), pl.ds(X0 + BX - 4, 4)]
        lands = [pl.ds(X0 + BX, 4), pl.ds(X0 - 4, 4)]
        found = []
        for n, dx in ((0, -1), (1, 1)):
            found.append((
                has[n], U.at[buf, :, ends[n], inner_y, :], U.at[buf, :, lands[n], inner_y, :],
                n, 1 - n, (s, i + dx, j),
            ))
        for n, dy in ((0, -1), (1, 1)):
            found.append((
                has[2 + n], YS.at[n], YR.at[slot, 1 - n], 2 + n, 3 - n, (s, i, j + dy),
            ))
        for n, (dx, dy) in enumerate(corners):
            ok = has[0 if dx < 0 else 1] & has[2 if dy < 0 else 3]
            found.append((
                ok, CS.at[n], CR.at[slot, 3 - n], 4 + n, 7 - n, (s, i + dx, j + dy),
            ))
        return found

    def halo_send(buf, slot):
        pack(buf, 4, YS)
        for n, (dx, dy) in enumerate(corners):
            for sh in range(SHOTS):
                for k in range(2):
                    x = X0 + k if dx < 0 else X0 + BX - 2 + k
                    y = Y0 if dy < 0 else Y0 + BY - 2
                    CS[n, sh * 4 + k * 2 : sh * 4 + k * 2 + 2] = U[buf, sh, x, y : y + 2]
        for ok, src, dst, n, m, dev in halo_list(buf, slot):
            @pl.when(ok)
            def _():
                send(src, dst, h_s.at[slot, n], h_r.at[slot, m], dev).start()

    def halo_wait(buf, slot):
        copies = halo_list(buf, slot)
        opposite = [1, 0, 3, 2, 7, 6, 5, 4]
        for n in range(8):
            ok, src, dst, _, m, dev = copies[n]
            back = copies[opposite[n]]

            @pl.when(ok)
            def _():
                send(src, dst, h_s.at[slot, n], h_r.at[slot, m], dev).wait_send()
                send(back[1], back[2], h_s.at[slot, n], h_r.at[slot, n], dev).wait_recv()

        unpack(buf, 4, YR.at[slot])
        for n, (dx, dy) in enumerate(corners):
            @pl.when(copies[4 + n][0])
            def _():
                for sh in range(SHOTS):
                    for k in range(2):
                        x = X0 - 2 + k if dx < 0 else X0 + BX + k
                        y = Y0 - 2 if dy < 0 else Y0 + BY
                        U[buf, sh, x, y : y + 2] = CR[slot, n, sh * 4 + k * 2 : sh * 4 + k * 2 + 2]

    cp_now.wait()
    halo_send(0, 0)
    cp_prev.wait()
    pack(2, 2, PS)
    prev_ends = [pl.ds(X0, 2), pl.ds(X0 + BX - 2, 2)]
    prev_lands = [pl.ds(X0 + BX, 2), pl.ds(X0 - 2, 2)]
    prev_list = []
    for n, dx in ((0, -1), (1, 1)):
        prev_list.append((
            has[n], U.at[2, :, prev_ends[n], inner_y, :], U.at[2, :, prev_lands[n], inner_y, :],
            n, 1 - n, (s, i + dx, j),
        ))
    for n, dy in ((0, -1), (1, 1)):
        prev_list.append((has[2 + n], PS.at[n], PR.at[1 - n], 2 + n, 3 - n, (s, i, j + dy)))
    for ok, src, dst, n, m, dev in prev_list:
        @pl.when(ok)
        def _():
            send(src, dst, p_s.at[n], p_r.at[m], dev).start()

    rows = lax.broadcasted_iota(jnp.int32, (8, BZ), 0)
    lanes = lax.broadcasted_iota(jnp.int32, (8, BZ), 1)
    first_lane = (lanes > 0).astype(F32)
    second_lane = (lanes > 1).astype(F32)
    last_lane = (lanes < BZ - 1).astype(F32)
    last_two = (lanes < BZ - 2).astype(F32)

    def weight(cell, total):
        return jnp.maximum(16 - jnp.minimum(cell + 1, total - cell), 0).astype(F32) / 16.0

    def damping_tables(x):
        wx = weight(jnp.full((8, BZ), i * BX + x - X0, jnp.int32), AX)
        for q in range(5):
            at = pl.ds(Y0 - 4 + 8 * q, 8)
            wy = weight(rows + (j * BY - 4 + 8 * q), AY)
            d = 0.3 * (wx * wx + wy * wy)
            inv = 1.0 / (1.0 + d)
            INV[x, at] = inv
            K2[x, at] = (1.0 - d) * inv

    loop(X0 + BX + 2, damping_tables, X0 - 2)

    for sh in range(SHOTS):
        wx = weight(jnp.full((8, BZ), sources[0, sh, 0], jnp.int32), AX)
        for q in range(5):
            cells = rows + (j * BY - 4 + 8 * q)
            wy = weight(cells, AY)
            inv = 1.0 / (1.0 + 0.3 * (wx * wx + wy * wy))
            hit = (cells == sources[0, sh, 1]) & (lanes == sources[0, sh, 2])
            EY[sh, pl.ds(Y0 - 4 + 8 * q, 8)] = jnp.where(hit, inv, 0.0)

    rx = receivers[0] - i * BX
    ry = receivers[1] - j * BY
    here = (rx >= 0) & (rx < BX) & (ry >= 0) & (ry < BY)
    IDL[...] = jnp.where(here, rx * BY + ry, -1)
    deep = lax.broadcasted_iota(jnp.int32, (2 * BZ, RECS), 0) & (BZ - 1)
    OH[...] = jnp.where(deep == receivers[2], 1.0, 0.0).astype(jnp.bfloat16)

    for r in range(1, NS):
        off_copy(r).wait_send()
        shot = (s + r) & (NS - 1)
        send(OFS, OFR.at[shot], off_s.at[r], off_r.at[shot], (shot, i, j)).wait_recv()
    cp_off = pltpu.make_async_copy(OFR, OFM, in_sem.at[0])
    cp_off.start()
    cp_off.wait()
    all_of(MT.at[pl.ds(0, GROUP - 1)], a_sem.at[0])
    all_of(R.at[pl.ds(0, GROUP - 1)], a_sem.at[1])

    tail = me >= GROUP - 2
    head = me < 2
    shift = jnp.where(tail, -1, 1)
    firsts = [OFM[k, 0, 0] for k in range(NS)]
    for d in range(GROUP):
        plane = R[owner[firsts[d // NX] + d % NX]]
        SEL[d] = plane
        EDGE[0, d] = plane[BY - 2 : BY]
        EDGE[1, d] = plane[0:2]
    for d in range(GROUP):
        column = jnp.clip(firsts[d // NX] + d % NX + shift, 0, GROUP - 1)
        SELH[d] = R[owner[column]]

    halo_plane = jnp.where(tail, me - (GROUP - 2) + X0 - 2, X0 + BX + jnp.minimum(me, 1))
    halo_slot = jnp.where(tail, me - (GROUP - 2), 2 + jnp.minimum(me, 1))

    def bh_copy(r):
        d = other(r)
        return send(
            SELH.at[d], CO.at[halo_plane, inner_y, :], bh_s.at[r], bh_r.at[halo_slot], member(d, j)
        )

    def bh_ok(d):
        c = d & (NX - 1)
        return (tail & (c > 0)) | (head & (c < NX - 1))

    def b_start(r):
        d = other(r)
        send(
            SEL.at[d], CO.at[X0 + me, inner_y, :], b_sem.at[0], b_sem.at[1], member(d, j)
        ).start()

    loop(GROUP, b_start, 1)

    @pl.when(tail | head)
    def _():
        def bh_start(r):
            @pl.when(bh_ok(other(r)))
            def _():
                bh_copy(r).start()

        loop(GROUP, bh_start, 1)

    for side, ok in ((0, has[3]), (1, has[2])):
        @pl.when(ok)
        def _():
            row = j + 1 if side == 0 else j - 1

            def edge_start(d):
                send(
                    EDGE.at[side, d], YM.at[side, me], e_sem.at[0, side], e_sem.at[1, side],
                    member(d, row),
                ).start()

            loop(GROUP, edge_start)

    CO[X0 + me, inner_y] = SEL[me]

    @pl.when(bh_ok(me))
    def _():
        CO[halo_plane, inner_y] = SELH[me]

    halo_wait(0, 0)
    for n in range(4):
        ok, src, dst, _, m, dev = prev_list[n]
        back = prev_list[[1, 0, 3, 2][n]]

        @pl.when(ok)
        def _():
            send(src, dst, p_s.at[n], p_r.at[m], dev).wait_send()
            send(back[1], back[2], p_s.at[n], p_r.at[n], dev).wait_recv()

    unpack(2, 2, PR)

    all_of(SEL.at[pl.ds(0, GROUP - 1)], b_sem.at[0])
    all_of(CO.at[pl.ds(0, GROUP - 1), inner_y, :], b_sem.at[1])

    @pl.when(tail | head)
    def _():
        def bh_wait(r):
            @pl.when(bh_ok(other(r)))
            def _():
                bh_copy(r).wait_send()

        loop(GROUP, bh_wait, 1)

    for slot in range(4):
        source = GROUP - 2 + slot if slot < 2 else slot - 2
        plane = X0 - 2 + slot if slot < 2 else X0 + BX + slot - 2
        edge = has[0] if slot < 2 else has[1]

        @pl.when(edge & (me != source))
        def _():
            send(
                SELH.at[0], CO.at[plane, inner_y, :], bh_s.at[0], bh_r.at[slot], member(source, j)
            ).wait_recv()

    for side, to, back in ((0, has[3], has[2]), (1, has[2], has[3])):
        @pl.when(to)
        def _():
            all_of(EDGE.at[side], e_sem.at[0, side])

        @pl.when(back)
        def _():
            all_of(YM.at[side], e_sem.at[1, side])
            for x in range(BX):
                CO[X0 + x, pl.ds(Y0 - 2 if side == 0 else Y0 + BY, 2)] = YM[side, x]

    def model_tables(x):
        for q in range(5):
            at = pl.ds(Y0 - 4 + 8 * q, 8)
            speed = CO[x, at]
            inv = INV[x, at]
            scaled = speed * speed * inv
            KC[x, at] = 2.0 * inv - 7.5 * scaled
            KA[x, at] = (4.0 / 3.0) * scaled

    loop(X0 + BX + 2, model_tables, X0 - 2)

    def advance(read, write_from, write, x_lo, x_hi, y_lo, count, step):
        def planes(block):
            first = x_lo + 4 * block
            done = []
            on = [
                [
                    jnp.where(sources[0, sh, 0] == i * BX + first + k - X0, wavelet[0, sh, step], 0.0)
                    for sh in range(SHOTS)
                ]
                for k in range(4)
            ]
            for q in range(count):
                y = y_lo + 8 * q
                at = pl.ds(y, 8)
                for k in range(4):
                    x = first + k
                    kc, ka, k2 = KC[x, at], KA[x, at], K2[x, at]
                    for sh in range(SHOTS):
                        c = U[read, sh, x, at]
                        a = (U[read, sh, x + 1, at] + U[read, sh, x - 1, at]) + (
                            U[read, sh, x, pl.ds(y + 1, 8)] + U[read, sh, x, pl.ds(y - 1, 8)]
                        )
                        b = (U[read, sh, x + 2, at] + U[read, sh, x - 2, at]) + (
                            U[read, sh, x, pl.ds(y + 2, 8)] + U[read, sh, x, pl.ds(y - 2, 8)]
                        )
                        a = a + (
                            pltpu.roll(c, 1, 1) * first_lane
                            + pltpu.roll(c, BZ - 1, 1) * last_lane
                        )
                        b = b + (
                            pltpu.roll(c, 2, 1) * second_lane
                            + pltpu.roll(c, BZ - 2, 1) * last_two
                        )
                        fresh = (kc * c - k2 * U[write_from, sh, x, at]) + ka * (a - 0.0625 * b)
                        done.append((sh, x, at, fresh + EY[sh, at] * on[k][sh]))
            for sh, x, at, fresh in done:
                U[write, sh, x, at] = fresh

        loop((x_hi - x_lo) // 4, planes)

    def outer_step(even, step):
        advance(even, 2, 2, X0 - 2, X0 + BX + 2, Y0 - 4, 5, step)

    def inner_step(even, odd_out, step):
        advance(2, even, odd_out, X0, X0 + BX, Y0, 4, step)

    row_ids = lax.broadcasted_iota(jnp.int32, (BX * BY, RECS), 0)

    def sample(buf, pair, half):
        def split(block):
            for k in range(4):
                for sh in range(SHOTS):
                    x = 4 * block + k
                    v = U[buf, sh, X0 + x, inner_y]
                    high = v.astype(jnp.bfloat16)
                    low = (v - high.astype(F32)).astype(jnp.bfloat16)
                    at = pl.ds(pl.multiple_of((sh * BX + x) * BY, BY), BY)
                    XB[at, 0:BZ] = high
                    XB[at, BZ : 2 * BZ] = low

        loop(BX // 4, split)
        for sh in range(SHOTS):
            picked = jnp.dot(
                XB[sh * BX * BY : (sh + 1) * BX * BY], OH[...], preferred_element_type=F32
            )
            got = jnp.sum(jnp.where(row_ids == IDL[...], picked, 0.0), axis=0, keepdims=True)
            row = 4 * half + 2 * sh
            TS[pair, row : row + 1] = got[:, 0:128]
            TS[pair, row + 1 : row + 2] = got[:, 128:256]

    def trace_send(pair):
        def one(r):
            send(
                TS.at[pair], TR.at[pair, mine], t_sem.at[0, pair], t_sem.at[1, pair],
                peer((mine + r) & (PEERS - 1)),
            ).start()

        loop(PEERS, one, 1)
        TR[pair, mine] = TS[pair]

    def two_steps(pair):
        even = lax.rem(pair, 2)
        later = 1 - even
        outer_step(even, 2 * pair)
        inner_step(even, later, 2 * pair + 1)
        halo_send(later, later)
        sample(2, pair, 0)
        sample(later, pair, 1)
        trace_send(pair)
        halo_wait(later, later)

    pairs = STEPS // 2
    loop(pairs - 1, two_steps)
    last = pairs - 1
    even = last % 2
    later = 1 - even
    outer_step(even, 2 * last)
    cp_out_prev = pltpu.make_async_copy(
        U.at[2, :, inner_x, inner_y, :], out_prev.at[0], in_sem.at[2]
    )
    cp_out_prev.start()
    inner_step(even, later, 2 * last + 1)
    cp_out_now = pltpu.make_async_copy(
        U.at[later, :, inner_x, inner_y, :], out_now.at[0], in_sem.at[1]
    )
    cp_out_now.start()
    sample(2, last, 0)
    sample(later, last, 1)
    trace_send(last)
    for pair in range(pairs):
        all_of(TR.at[pair, pl.ds(0, PEERS - 1)], t_sem.at[0, pair])
        all_of(TR.at[pair, pl.ds(0, PEERS - 1)], t_sem.at[1, pair])
        total = TR[pair, 0]
        for q in range(1, PEERS):
            total = total + TR[pair, q]
        for row in range(8):
            half, sh, part = row // 4, (row // 2) % 2, row % 2
            out_traces[sh, 2 * pair + half : 2 * pair + half + 1, 128 * part : 128 * part + 128] = (
                total[row : row + 1]
            )
    cp_out_prev.wait()
    cp_out_now.wait()


def window(tiles, owner, offset, now, prev, sources, wavelet, receivers):
    any_spec = pl.BlockSpec(memory_space=pl.ANY)
    smem = pl.BlockSpec(memory_space=pltpu.SMEM)
    vmem = pl.BlockSpec(memory_space=pltpu.VMEM)
    buf = pltpu.VMEM
    dma = pltpu.SemaphoreType.DMA
    padded = (PX, PY, BZ)
    out_now, out_prev, traces = pl.pallas_call(
        kernel,
        out_shape=(
            jax.ShapeDtypeStruct(now.shape, F32),
            jax.ShapeDtypeStruct(prev.shape, F32),
            jax.ShapeDtypeStruct((SHOTS, STEPS, RECS), F32),
        ),
        in_specs=[any_spec, smem, smem, any_spec, any_spec, smem, smem, vmem],
        out_specs=(any_spec, any_spec, vmem),
        scratch_shapes=[
            buf((3, SHOTS) + padded, F32),
            buf((BX, BY, BZ), F32),
            buf((GROUP, BY, BZ), F32),
            buf((GROUP, BY, BZ), F32),
            buf((GROUP, BY, BZ), F32),
            buf((2, GROUP, 2, BZ), F32),
            buf((2, GROUP, 2, BZ), F32),
            buf(padded, F32),
            buf(padded, F32),
            buf(padded, F32),
            buf(padded, F32),
            buf(padded, F32),
            buf((SHOTS, PY, BZ), F32),
            buf((2, SHOTS * BX, 4, BZ), F32),
            buf((2, 2, SHOTS * BX, 4, BZ), F32),
            buf((4, 8, BZ), F32),
            buf((2, 4, 8, BZ), F32),
            buf((2, SHOTS * BX, 2, BZ), F32),
            buf((2, SHOTS * BX, 2, BZ), F32),
            buf((1, BZ), jnp.int32),
            buf((NS, 1, BZ), jnp.int32),
            pltpu.SMEM((NS, 1, BZ), jnp.int32),
            buf((2 * BZ, RECS), jnp.bfloat16),
            buf((1, RECS), jnp.int32),
            buf((SHOTS * BX * BY, 2 * BZ), jnp.bfloat16),
            buf((STEPS // 2, 8, 128), F32),
            buf((STEPS // 2, PEERS, 8, 128), F32),
            dma((3,)), dma((NS,)), dma((NS,)), dma((2,)), dma((2,)),
            dma((GROUP,)), dma((4,)), dma((2, 2)),
            dma((2, 8)), dma((2, 8)), dma((4,)), dma((4,)), dma((2, STEPS // 2)),
        ],
        compiler_params=pltpu.CompilerParams(collective_id=0, has_side_effects=True),
    )(tiles, owner, offset, now, prev, sources, wavelet, jnp.transpose(receivers, (2, 0, 1)))
    return out_now, out_prev, jnp.transpose(traces, (0, 2, 1))[None]


def solution(mesh):
    return jax.shard_map(
        window,
        mesh=mesh,
        in_specs=(
            P(("shot", "gx"), "gy", None),
            P(),
            P("shot"),
            P("shot", None, "gx", "gy", None),
            P("shot", None, "gx", "gy", None),
            P("shot", None, None),
            P("shot", None, None),
            P("shot", None, None),
        ),
        out_specs=(
            P("shot", None, "gx", "gy", None),
            P("shot", None, "gx", "gy", None),
            P("shot", None, None, None),
        ),
        check_vma=False,
    )
```

```python
import jax
import jax.numpy as jnp
from jax import lax
from jax.experimental import pallas as pl
from jax.experimental.pallas import tpu as pltpu
from jax.sharding import PartitionSpec as P

STEPS = 8
SHOTS = 2
NS, NX, NY = 4, 4, 8
GROUP = NS * NX
PEERS = NX * NY
BX, BY, BZ = 16, 32, 128
AX, AY = NX * BX, NY * BY
RECS = 256
PX, PY = BX + 8, BY + 16
X0, Y0 = 4, 8
MESH = pl.DeviceIdType.MESH
F32 = jnp.float32


def loop(n, body, start=0):
    lax.fori_loop(start, n, lambda k, c: (body(k), c)[1], 0)


def kernel(
    tiles, owner, offset, now, prev, sources, wavelet, receivers,
    out_now, out_prev, out_traces,
    E0, E1, O, MT, R, SEL, SELH, EDGE, YM, CO, KC, KA, K2, INV, EY,
    YS, YR, CS, CR, PS, PR, OFS, OFR, OFM, OH, IDL, XB, TS, TR,
    in_sem, off_s, off_r, a_sem, b_sem, bh_s, bh_r, e_sem,
    h_s, h_r, p_s, p_r, t_sem,
):
    s = lax.axis_index("shot")
    i = lax.axis_index("gx")
    j = lax.axis_index("gy")
    me = s * NX + i
    mine = i * NY + j

    def member(r):
        return (s ^ (r >> 2), i ^ (r & 3), j)

    def all_of(ref, sem):
        pltpu.make_async_copy(ref, ref, sem).wait()

    def send(src, dst, ssem, rsem, dev):
        return pltpu.make_async_remote_copy(
            src_ref=src, dst_ref=dst, send_sem=ssem, recv_sem=rsem,
            device_id=dev, device_id_type=MESH,
        )

    inner_x = pl.ds(X0, BX)
    inner_y = pl.ds(Y0, BY)
    has = [i > 0, i < NX - 1, j > 0, j < NY - 1]

    cp_mt = pltpu.make_async_copy(tiles, MT, in_sem.at[0])
    cp_now = pltpu.make_async_copy(now.at[0], E0.at[:, inner_x, inner_y, :], in_sem.at[1])
    cp_prev = pltpu.make_async_copy(prev.at[0], O.at[:, inner_x, inner_y, :], in_sem.at[2])
    cp_mt.start()
    cp_now.start()
    cp_prev.start()

    barrier = pltpu.get_barrier_semaphore()

    def greet(dev):
        pl.semaphore_signal(barrier, inc=1, device_id=dev, device_id_type=MESH)

    for r in range(1, NY):
        greet((s, i, j ^ r))
    for r in range(1, GROUP):
        greet(member(r))
    pl.semaphore_wait(barrier, GROUP + NY - 2)

    OFS[...] = jnp.full((1, BZ), offset[0], jnp.int32)

    def off_copy(r):
        return send(OFS, OFR.at[s], off_s.at[r], off_r.at[s], (s ^ r, i, j))

    for r in range(1, NS):
        off_copy(r).start()
    OFR[s] = jnp.full((1, BZ), offset[0], jnp.int32)

    cp_mt.wait()
    for r in range(1, GROUP):
        send(MT.at[me ^ r], R.at[me], a_sem.at[0], a_sem.at[1], member(r)).start()
    R[me] = MT[me]

    def pack(buf, depth, store):
        for x in range(BX):
            for sh in range(SHOTS):
                store[0, sh * BX + x] = buf[sh, X0 + x, pl.ds(Y0, depth)]
                store[1, sh * BX + x] = buf[sh, X0 + x, pl.ds(Y0 + BY - depth, depth)]

    def unpack(buf, depth, store):
        for side, y in ((0, Y0 - depth), (1, Y0 + BY)):
            @pl.when(has[2 + side])
            def _():
                for x in range(BX):
                    for sh in range(SHOTS):
                        buf[sh, X0 + x, pl.ds(y, depth)] = store[side, sh * BX + x]

    corners = [(-1, -1), (-1, 1), (1, -1), (1, 1)]

    def halo_list(buf, slot):
        ends = [pl.ds(X0, 4), pl.ds(X0 + BX - 4, 4)]
        lands = [pl.ds(X0 + BX, 4), pl.ds(X0 - 4, 4)]
        found = []
        for n, dx in ((0, -1), (1, 1)):
            found.append((
                has[n], buf.at[:, ends[n], inner_y, :], buf.at[:, lands[n], inner_y, :],
                n, 1 - n, (s, i + dx, j),
            ))
        for n, dy in ((0, -1), (1, 1)):
            found.append((
                has[2 + n], YS.at[n], YR.at[slot, 1 - n], 2 + n, 3 - n, (s, i, j + dy),
            ))
        for n, (dx, dy) in enumerate(corners):
            ok = has[0 if dx < 0 else 1] & has[2 if dy < 0 else 3]
            found.append((
                ok, CS.at[n], CR.at[slot, 3 - n], 4 + n, 7 - n, (s, i + dx, j + dy),
            ))
        return found

    def start_some(copies, slot):
        for ok, src, dst, n, m, dev in copies:
            @pl.when(ok)
            def _():
                send(src, dst, h_s.at[slot, n], h_r.at[slot, m], dev).start()

    def send_sides(buf, slot):
        start_some(halo_list(buf, slot)[0:2], slot)

    def send_rows(buf, slot):
        pack(buf, 4, YS)
        start_some(halo_list(buf, slot)[2:4], slot)

    def send_corners(buf, slot):
        for n, (dx, dy) in enumerate(corners):
            for sh in range(SHOTS):
                for k in range(2):
                    x = X0 + k if dx < 0 else X0 + BX - 2 + k
                    y = Y0 if dy < 0 else Y0 + BY - 2
                    CS[n, sh * 4 + k * 2 : sh * 4 + k * 2 + 2] = buf[sh, x, y : y + 2]
        start_some(halo_list(buf, slot)[4:8], slot)

    def halo_wait(buf, slot):
        copies = halo_list(buf, slot)
        opposite = [1, 0, 3, 2, 7, 6, 5, 4]
        for n in range(8):
            ok, src, dst, _, m, dev = copies[n]
            back = copies[opposite[n]]

            @pl.when(ok)
            def _():
                send(src, dst, h_s.at[slot, n], h_r.at[slot, m], dev).wait_send()
                send(back[1], back[2], h_s.at[slot, n], h_r.at[slot, n], dev).wait_recv()

        unpack(buf, 4, YR.at[slot])
        for n, (dx, dy) in enumerate(corners):
            @pl.when(copies[4 + n][0])
            def _():
                for sh in range(SHOTS):
                    for k in range(2):
                        x = X0 - 2 + k if dx < 0 else X0 + BX + k
                        y = Y0 - 2 if dy < 0 else Y0 + BY
                        buf[sh, x, y : y + 2] = CR[slot, n, sh * 4 + k * 2 : sh * 4 + k * 2 + 2]

    cp_now.wait()
    send_rows(E0, 0)
    send_sides(E0, 0)
    cp_prev.wait()
    pack(O, 2, PS)
    prev_ends = [pl.ds(X0, 2), pl.ds(X0 + BX - 2, 2)]
    prev_lands = [pl.ds(X0 + BX, 2), pl.ds(X0 - 2, 2)]
    prev_list = []
    for n, dx in ((0, -1), (1, 1)):
        prev_list.append((
            has[n], O.at[:, prev_ends[n], inner_y, :], O.at[:, prev_lands[n], inner_y, :],
            n, 1 - n, (s, i + dx, j),
        ))
    for n, dy in ((0, -1), (1, 1)):
        prev_list.append((has[2 + n], PS.at[n], PR.at[1 - n], 2 + n, 3 - n, (s, i, j + dy)))
    for ok, src, dst, n, m, dev in prev_list:
        @pl.when(ok)
        def _():
            send(src, dst, p_s.at[n], p_r.at[m], dev).start()

    for n, first in ((0, 0), (1, PX - 4)):
        @pl.when(jnp.logical_not(has[n]))
        def _():
            blank = jnp.zeros((4, PY, BZ), F32)
            for buf in (E0, E1, O):
                for sh in range(SHOTS):
                    buf[sh, first : first + 4] = blank
            CO[first : first + 4] = blank

    for n, first in ((2, 0), (3, PY - 8)):
        @pl.when(jnp.logical_not(has[n]))
        def _():
            blank = jnp.zeros((8, BZ), F32)

            def one(x):
                for buf in (E0, E1, O):
                    for sh in range(SHOTS):
                        buf[sh, x, first : first + 8] = blank
                CO[x, first : first + 8] = blank

            loop(PX, one)

    rows = lax.broadcasted_iota(jnp.int32, (8, BZ), 0)
    lanes = lax.broadcasted_iota(jnp.int32, (8, BZ), 1)
    first_lane = (lanes > 0).astype(F32)
    second_lane = (lanes > 1).astype(F32)
    last_lane = (lanes < BZ - 1).astype(F32)
    last_two = (lanes < BZ - 2).astype(F32)

    def weight(cell, total):
        return jnp.maximum(16 - jnp.minimum(cell + 1, total - cell), 0).astype(F32) / 16.0

    def damping_tables(x):
        wx = weight(jnp.full((8, BZ), i * BX + x - X0, jnp.int32), AX)
        for q in range(5):
            at = pl.ds(Y0 - 4 + 8 * q, 8)
            wy = weight(rows + (j * BY - 4 + 8 * q), AY)
            d = 0.3 * (wx * wx + wy * wy)
            inv = 1.0 / (1.0 + d)
            INV[x, at] = inv
            K2[x, at] = (1.0 - d) * inv

    loop(X0 + BX + 2, damping_tables, X0 - 2)

    for sh in range(SHOTS):
        wx = weight(jnp.full((8, BZ), sources[0, sh, 0], jnp.int32), AX)
        for q in range(5):
            cells = rows + (j * BY - 4 + 8 * q)
            wy = weight(cells, AY)
            inv = 1.0 / (1.0 + 0.3 * (wx * wx + wy * wy))
            hit = (cells == sources[0, sh, 1]) & (lanes == sources[0, sh, 2])
            EY[sh, pl.ds(Y0 - 4 + 8 * q, 8)] = jnp.where(hit, inv, 0.0)

    rx = receivers[0] - i * BX
    ry = receivers[1] - j * BY
    here = (rx >= 0) & (rx < BX) & (ry >= 0) & (ry < BY)
    IDL[...] = jnp.where(here, rx * BY + ry, -1)
    deep = lax.broadcasted_iota(jnp.int32, (2 * BZ, RECS), 0) & (BZ - 1)
    OH[...] = jnp.where(deep == receivers[2], 1.0, 0.0).astype(jnp.bfloat16)

    for r in range(1, NS):
        off_copy(r).wait_send()
        shot = s ^ r
        send(OFS, OFR.at[shot], off_s.at[r], off_r.at[shot], (shot, i, j)).wait_recv()
    cp_off = pltpu.make_async_copy(OFR, OFM, in_sem.at[0])
    cp_off.start()
    cp_off.wait()
    all_of(MT.at[pl.ds(0, GROUP - 1)], a_sem.at[0])
    all_of(R.at[pl.ds(0, GROUP - 1)], a_sem.at[1])

    send_corners(E0, 0)

    tail = me >= GROUP - 2
    head = me < 2
    shift = jnp.where(tail, -1, 1)
    firsts = [OFM[s ^ r, 0, 0] for r in range(NS)]
    columns = [firsts[r >> 2] + (i ^ (r & 3)) for r in range(GROUP)]
    for r in range(GROUP):
        plane = R[owner[columns[r]]]
        SEL[r] = plane
        EDGE[0, r] = plane[BY - 2 : BY]
        EDGE[1, r] = plane[0:2]
    halo_plane = jnp.where(tail, me - (GROUP - 2) + X0 - 2, X0 + BX + jnp.minimum(me, 1))
    halo_slot = jnp.where(tail, me - (GROUP - 2), 2 + jnp.minimum(me, 1))

    def bh_copy(r):
        return send(
            SELH.at[r], CO.at[halo_plane, inner_y, :], bh_s.at[r], bh_r.at[halo_slot], member(r)
        )

    def bh_ok(r):
        c = i ^ (r & 3)
        return (tail & (c > 0)) | (head & (c < NX - 1))

    for r in range(1, GROUP):
        send(SEL.at[r], CO.at[X0 + me, inner_y, :], b_sem.at[0], b_sem.at[1], member(r)).start()

    @pl.when(tail | head)
    def _():
        for r in range(GROUP):
            SELH[r] = R[owner[jnp.clip(columns[r] + shift, 0, GROUP - 1)]]
        for r in range(1, GROUP):
            @pl.when(bh_ok(r))
            def _():
                bh_copy(r).start()

    for side, ok in ((0, has[3]), (1, has[2])):
        @pl.when(ok)
        def _():
            row = j + 1 if side == 0 else j - 1
            for r in range(GROUP):
                send(
                    EDGE.at[side, r], YM.at[side, me], e_sem.at[0, side], e_sem.at[1, side],
                    (s ^ (r >> 2), i ^ (r & 3), row),
                ).start()

    CO[X0 + me, inner_y] = SEL[0]

    @pl.when(bh_ok(0))
    def _():
        CO[halo_plane, inner_y] = SELH[0]

    halo_wait(E0, 0)
    for n in range(4):
        ok, src, dst, _, m, dev = prev_list[n]
        back = prev_list[[1, 0, 3, 2][n]]

        @pl.when(ok)
        def _():
            send(src, dst, p_s.at[n], p_r.at[m], dev).wait_send()
            send(back[1], back[2], p_s.at[n], p_r.at[n], dev).wait_recv()

    unpack(O, 2, PR)

    all_of(SEL.at[pl.ds(0, GROUP - 1)], b_sem.at[0])
    all_of(CO.at[pl.ds(0, GROUP - 1), inner_y, :], b_sem.at[1])

    @pl.when(tail | head)
    def _():
        for r in range(1, GROUP):
            @pl.when(bh_ok(r))
            def _():
                bh_copy(r).wait_send()

    for slot in range(4):
        source = GROUP - 2 + slot if slot < 2 else slot - 2
        plane = X0 - 2 + slot if slot < 2 else X0 + BX + slot - 2
        edge = has[0] if slot < 2 else has[1]

        @pl.when(edge & (me != source))
        def _():
            send(
                SELH.at[0], CO.at[plane, inner_y, :], bh_s.at[0], bh_r.at[slot],
                (source >> 2, source & 3, j),
            ).wait_recv()

    for side, to, back in ((0, has[3], has[2]), (1, has[2], has[3])):
        @pl.when(to)
        def _():
            all_of(EDGE.at[side], e_sem.at[0, side])

        @pl.when(back)
        def _():
            all_of(YM.at[side], e_sem.at[1, side])
            for x in range(BX):
                CO[X0 + x, pl.ds(Y0 - 2 if side == 0 else Y0 + BY, 2)] = YM[side, x]

    def model_tables(x):
        for q in range(5):
            at = pl.ds(Y0 - 4 + 8 * q, 8)
            speed = CO[x, at]
            inv = INV[x, at]
            scaled = speed * speed * inv
            KC[x, at] = 2.0 * inv - 7.5 * scaled
            KA[x, at] = (4.0 / 3.0) * scaled

    loop(X0 + BX + 2, model_tables, X0 - 2)

    def advance(read, before, write, first, stride, blocks, wide, tiles, step, lift=(0, 0)):
        def planes(block):
            x_first = first + stride * block
            for k in range(wide):
                x = x_first + k
                on = [
                    jnp.where(sources[0, sh, 0] == i * BX + x - X0, wavelet[0, sh, step], 0.0)
                    for sh in range(SHOTS)
                ]
                for y in tiles:
                    at = pl.ds(y, 8)
                    kc, ka, k2 = KC[x, at], KA[x, at], K2[x, at]
                    for sh in range(SHOTS):
                        c = read[sh, x, at]
                        a = (read[sh, x + 1, at] + read[sh, x - 1, at]) + (
                            read[sh, x, pl.ds(y + 1, 8)] + read[sh, x, pl.ds(y - 1, 8)]
                        )
                        b = (read[sh, x + 2, at] + read[sh, x - 2, at]) + (
                            read[sh, x, pl.ds(y + 2, 8)] + read[sh, x, pl.ds(y - 2, 8)]
                        )
                        a = a + (
                            pltpu.roll(c, 1, 1) * first_lane
                            + pltpu.roll(c, BZ - 1, 1) * last_lane
                        )
                        b = b + (
                            pltpu.roll(c, 2, 1) * second_lane
                            + pltpu.roll(c, BZ - 2, 1) * last_two
                        )
                        fresh = (kc * c - k2 * before[sh, x, at]) + ka * (a - 0.0625 * b)
                        fresh = fresh + EY[sh, at] * on[sh]
                        write[sh, x - lift[0], pl.ds(y - lift[1], 8)] = fresh

        loop(blocks, planes)

    wide_tiles = [Y0 - 4 + 8 * q for q in range(5)]
    own_tiles = [Y0 + 8 * q for q in range(4)]

    def outer_middle(even, step):
        advance(even, O, O, X0 + 2, 4, 3, 4, wide_tiles[1:4], step)

    def outer_ring(even, step):
        advance(even, O, O, X0 - 2, BX, 2, 4, wide_tiles, step)
        advance(even, O, O, X0 + 2, 4, 3, 4, [wide_tiles[0], wide_tiles[4]], step)

    row_ids = lax.broadcasted_iota(jnp.int32, (BX * BY, RECS), 0)

    def sample(buf, pair, half, corner=(X0, Y0)):
        def split(block):
            for k in range(4):
                for sh in range(SHOTS):
                    x = 4 * block + k
                    v = buf[sh, corner[0] + x, pl.ds(corner[1], BY)]
                    high = v.astype(jnp.bfloat16)
                    low = (v - high.astype(F32)).astype(jnp.bfloat16)
                    at = pl.ds(pl.multiple_of((sh * BX + x) * BY, BY), BY)
                    XB[at, 0:BZ] = high
                    XB[at, BZ : 2 * BZ] = low

        loop(BX // 4, split)
        for sh in range(SHOTS):
            picked = jnp.dot(
                XB[sh * BX * BY : (sh + 1) * BX * BY], OH[...], preferred_element_type=F32
            )
            got = jnp.sum(jnp.where(row_ids == IDL[...], picked, 0.0), axis=0, keepdims=True)
            row = 4 * half + 2 * sh
            TS[pair, row : row + 1] = got[:, 0:128]
            TS[pair, row + 1 : row + 2] = got[:, 128:256]

    def trace_send(pair):
        for r in range(1, PEERS):
            send(
                TS.at[pair], TR.at[pair, mine], t_sem.at[0, pair], t_sem.at[1, pair],
                (s, i ^ (r >> 3), j ^ (r & 7)),
            ).start()
        TR[pair, mine] = TS[pair]

    def trace_sum(pair):
        all_of(TR.at[pair, pl.ds(0, PEERS - 1)], t_sem.at[0, pair])
        all_of(TR.at[pair, pl.ds(0, PEERS - 1)], t_sem.at[1, pair])
        parts = [TR[pair, q] for q in range(PEERS)]
        while len(parts) > 1:
            parts = [a + b for a, b in zip(parts[0::2], parts[1::2])]
        for row in range(8):
            half, sh, part = row // 4, (row // 2) % 2, row % 2
            out_traces[sh, 2 * pair + half : 2 * pair + half + 1, 128 * part : 128 * part + 128] = (
                parts[0][row : row + 1]
            )

    pairs = STEPS // 2
    outer_middle(E0, 0)
    for pair in range(pairs):
        even, later = ((E0, E1), (E1, E0))[pair % 2]
        slot = (pair + 1) % 2
        step = 2 * pair + 1
        outer_ring(even, step - 1)
        if pair < pairs - 1:
            advance(O, even, later, X0, 12, 2, 4, own_tiles, step)
            send_sides(later, slot)
            send_corners(later, slot)
            advance(O, even, later, X0 + 4, 4, 2, 4, [own_tiles[0], own_tiles[3]], step)
            send_rows(later, slot)
            advance(O, even, later, X0 + 4, 4, 2, 4, own_tiles[1:3], step)
            sample(O, pair, 0)
            sample(later, pair, 1)
            trace_send(pair)
            outer_middle(later, step + 1)
            if pair:
                trace_sum(pair - 1)
            halo_wait(later, slot)
        else:
            cp_last = pltpu.make_async_copy(
                O.at[:, inner_x, inner_y, :], out_prev.at[0], in_sem.at[2]
            )
            cp_last.start()
            final = out_now.at[0]
            advance(O, even, final, X0, 4, 4, 4, own_tiles, step, (X0, Y0))
            sample(O, pair, 0)
            sample(final, pair, 1, (0, 0))
            trace_send(pair)
            trace_sum(pair - 1)
            trace_sum(pair)
            cp_last.wait()


def window(tiles, owner, offset, now, prev, sources, wavelet, receivers):
    any_spec = pl.BlockSpec(memory_space=pl.ANY)
    smem = pl.BlockSpec(memory_space=pltpu.SMEM)
    vmem = pl.BlockSpec(memory_space=pltpu.VMEM)
    buf = pltpu.VMEM
    dma = pltpu.SemaphoreType.DMA
    padded = (PX, PY, BZ)
    out_now, out_prev, traces = pl.pallas_call(
        kernel,
        out_shape=(
            pltpu.VMEM(now.shape, F32),
            pltpu.VMEM(prev.shape, F32),
            pltpu.VMEM((SHOTS, STEPS, RECS), F32),
        ),
        in_specs=[any_spec, smem, smem, any_spec, any_spec, smem, smem, vmem],
        out_specs=(vmem, vmem, vmem),
        scratch_shapes=[
            buf((SHOTS,) + padded, F32),
            buf((SHOTS,) + padded, F32),
            buf((SHOTS,) + padded, F32),
            buf((BX, BY, BZ), F32),
            buf((GROUP, BY, BZ), F32),
            buf((GROUP, BY, BZ), F32),
            buf((GROUP, BY, BZ), F32),
            buf((2, GROUP, 2, BZ), F32),
            buf((2, GROUP, 2, BZ), F32),
            buf(padded, F32),
            buf(padded, F32),
            buf(padded, F32),
            buf(padded, F32),
            buf(padded, F32),
            buf((SHOTS, PY, BZ), F32),
            buf((2, SHOTS * BX, 4, BZ), F32),
            buf((2, 2, SHOTS * BX, 4, BZ), F32),
            buf((4, 8, BZ), F32),
            buf((2, 4, 8, BZ), F32),
            buf((2, SHOTS * BX, 2, BZ), F32),
            buf((2, SHOTS * BX, 2, BZ), F32),
            buf((1, BZ), jnp.int32),
            buf((NS, 1, BZ), jnp.int32),
            pltpu.SMEM((NS, 1, BZ), jnp.int32),
            buf((2 * BZ, RECS), jnp.bfloat16),
            buf((1, RECS), jnp.int32),
            buf((SHOTS * BX * BY, 2 * BZ), jnp.bfloat16),
            buf((STEPS // 2, 8, 128), F32),
            buf((STEPS // 2, PEERS, 8, 128), F32),
            dma((3,)), dma((NS,)), dma((NS,)), dma((2,)), dma((2,)),
            dma((GROUP,)), dma((4,)), dma((2, 2)),
            dma((2, 8)), dma((2, 8)), dma((4,)), dma((4,)), dma((2, STEPS // 2)),
        ],
        compiler_params=pltpu.CompilerParams(collective_id=0, has_side_effects=True),
    )(tiles, owner, offset, now, prev, sources, wavelet, jnp.transpose(receivers, (2, 0, 1)))
    return out_now, out_prev, jnp.transpose(traces, (0, 2, 1))[None]


def solution(mesh):
    return jax.shard_map(
        window,
        mesh=mesh,
        in_specs=(
            P(("shot", "gx"), "gy", None),
            P(),
            P("shot"),
            P("shot", None, "gx", "gy", None),
            P("shot", None, "gx", "gy", None),
            P("shot", None, None),
            P("shot", None, None),
            P("shot", None, None),
        ),
        out_specs=(
            P("shot", None, "gx", "gy", None),
            P("shot", None, "gx", "gy", None),
            P("shot", None, None, None),
        ),
        check_vma=False,
    )
```

```python
import jax
import jax.numpy as jnp
from jax import lax
from jax.experimental import pallas as pl
from jax.experimental.pallas import tpu as pltpu
from jax.sharding import PartitionSpec as P

STEPS = 8
SHOTS = 2
NS, NX, NY = 4, 4, 8
GROUP = NS * NX
PEERS = NX * NY
BX, BY, BZ = 16, 32, 128
AX, AY = NX * BX, NY * BY
RECS = 256
PX, PY = BX + 8, BY + 16
X0, Y0 = 4, 8
MESH = pl.DeviceIdType.MESH
F32 = jnp.float32


def loop(n, body, start=0):
    lax.fori_loop(start, n, lambda k, c: (body(k), c)[1], 0)


def kernel(
    tiles, owner, offset, now, prev, sources, wavelet, receivers,
    out_now, out_prev, out_traces,
    E0, E1, O, MT, R, SEL, SELH, EDGE, YM, CO, KC, KA, K2, INV, EY,
    YS, YR, CS, CR, PS, PR, OFS, OFR, OFM, OH, IDL, XB, ACC, TS, TR,
    in_sem, off_s, off_r, a_sem, b_sem, bh_s, bh_r, e_sem,
    h_s, h_r, p_s, p_r, t_sem,
):
    s = lax.axis_index("shot")
    i = lax.axis_index("gx")
    j = lax.axis_index("gy")
    me = s * NX + i
    mine = i * NY + j

    def member(r):
        return (s ^ (r >> 2), i ^ (r & 3), j)

    def all_of(ref, sem):
        pltpu.make_async_copy(ref, ref, sem).wait()

    def send(src, dst, ssem, rsem, dev):
        return pltpu.make_async_remote_copy(
            src_ref=src, dst_ref=dst, send_sem=ssem, recv_sem=rsem,
            device_id=dev, device_id_type=MESH,
        )

    inner_x = pl.ds(X0, BX)
    inner_y = pl.ds(Y0, BY)
    has = [i > 0, i < NX - 1, j > 0, j < NY - 1]

    cp_mt = pltpu.make_async_copy(tiles, MT, in_sem.at[0])
    cp_now = pltpu.make_async_copy(now.at[0], E0.at[:, inner_x, inner_y, :], in_sem.at[1])
    cp_prev = pltpu.make_async_copy(prev.at[0], O.at[:, inner_x, inner_y, :], in_sem.at[2])
    cp_mt.start()
    cp_now.start()
    cp_prev.start()

    barrier = pltpu.get_barrier_semaphore()

    def greet(dev):
        pl.semaphore_signal(barrier, inc=1, device_id=dev, device_id_type=MESH)

    for r in range(1, NY):
        greet((s, i, j ^ r))
    for r in range(1, GROUP):
        greet(member(r))
    pl.semaphore_wait(barrier, GROUP + NY - 2)

    OFS[...] = jnp.full((1, BZ), offset[0], jnp.int32)

    def off_copy(r):
        return send(OFS, OFR.at[s], off_s.at[r], off_r.at[s], (s ^ r, i, j))

    for r in range(1, NS):
        off_copy(r).start()
    OFR[s] = jnp.full((1, BZ), offset[0], jnp.int32)

    cp_mt.wait()
    for r in range(1, GROUP):
        send(MT.at[me ^ r], R.at[me], a_sem.at[0], a_sem.at[1], member(r)).start()
    R[me] = MT[me]

    def pack(buf, depth, store):
        for x in range(BX):
            for sh in range(SHOTS):
                store[0, sh * BX + x] = buf[sh, X0 + x, pl.ds(Y0, depth)]
                store[1, sh * BX + x] = buf[sh, X0 + x, pl.ds(Y0 + BY - depth, depth)]

    def unpack(buf, depth, store):
        for side, y in ((0, Y0 - depth), (1, Y0 + BY)):
            @pl.when(has[2 + side])
            def _():
                for x in range(BX):
                    for sh in range(SHOTS):
                        buf[sh, X0 + x, pl.ds(y, depth)] = store[side, sh * BX + x]

    corners = [(-1, -1), (-1, 1), (1, -1), (1, 1)]

    def halo_list(buf, slot):
        ends = [pl.ds(X0, 4), pl.ds(X0 + BX - 4, 4)]
        lands = [pl.ds(X0 + BX, 4), pl.ds(X0 - 4, 4)]
        found = []
        for n, dx in ((0, -1), (1, 1)):
            found.append((
                has[n], buf.at[:, ends[n], inner_y, :], buf.at[:, lands[n], inner_y, :],
                n, 1 - n, (s, i + dx, j),
            ))
        for n, dy in ((0, -1), (1, 1)):
            found.append((
                has[2 + n], YS.at[n], YR.at[slot, 1 - n], 2 + n, 3 - n, (s, i, j + dy),
            ))
        for n, (dx, dy) in enumerate(corners):
            ok = has[0 if dx < 0 else 1] & has[2 if dy < 0 else 3]
            found.append((
                ok, CS.at[n], CR.at[slot, 3 - n], 4 + n, 7 - n, (s, i + dx, j + dy),
            ))
        return found

    def start_some(copies, slot):
        for ok, src, dst, n, m, dev in copies:
            @pl.when(ok)
            def _():
                send(src, dst, h_s.at[slot, n], h_r.at[slot, m], dev).start()

    def send_sides(buf, slot):
        start_some(halo_list(buf, slot)[0:2], slot)

    def send_rows(buf, slot):
        pack(buf, 4, YS)
        start_some(halo_list(buf, slot)[2:4], slot)

    def send_corners(buf, slot):
        for n, (dx, dy) in enumerate(corners):
            for sh in range(SHOTS):
                for k in range(2):
                    x = X0 + k if dx < 0 else X0 + BX - 2 + k
                    y = Y0 if dy < 0 else Y0 + BY - 2
                    CS[n, sh * 4 + k * 2 : sh * 4 + k * 2 + 2] = buf[sh, x, y : y + 2]
        start_some(halo_list(buf, slot)[4:8], slot)

    def wait_some(buf, slot, which):
        copies = halo_list(buf, slot)
        opposite = [1, 0, 3, 2, 7, 6, 5, 4]
        for n in which:
            ok, src, dst, _, m, dev = copies[n]
            back = copies[opposite[n]]

            @pl.when(ok)
            def _():
                send(src, dst, h_s.at[slot, n], h_r.at[slot, m], dev).wait_send()
                send(back[1], back[2], h_s.at[slot, n], h_r.at[slot, n], dev).wait_recv()

    def wait_rest(buf, slot):
        copies = halo_list(buf, slot)
        wait_some(buf, slot, range(2, 8))
        unpack(buf, 4, YR.at[slot])
        for n, (dx, dy) in enumerate(corners):
            @pl.when(copies[4 + n][0])
            def _():
                for sh in range(SHOTS):
                    for k in range(2):
                        x = X0 - 2 + k if dx < 0 else X0 + BX + k
                        y = Y0 - 2 if dy < 0 else Y0 + BY
                        buf[sh, x, y : y + 2] = CR[slot, n, sh * 4 + k * 2 : sh * 4 + k * 2 + 2]

    for n, first in ((0, 0), (1, PX - 4)):
        @pl.when(jnp.logical_not(has[n]))
        def _():
            blank = jnp.zeros((4, PY, BZ), F32)
            for buf in (E0, E1, O):
                for sh in range(SHOTS):
                    buf[sh, first : first + 4] = blank
            CO[first : first + 4] = blank

    for n, first in ((2, 0), (3, PY - 8)):
        @pl.when(jnp.logical_not(has[n]))
        def _():
            blank = jnp.zeros((8, BZ), F32)

            def one(x):
                for buf in (E0, E1, O):
                    for sh in range(SHOTS):
                        buf[sh, x, first : first + 8] = blank
                CO[x, first : first + 8] = blank

            loop(PX, one)

    rows = lax.broadcasted_iota(jnp.int32, (8, BZ), 0)
    lanes = lax.broadcasted_iota(jnp.int32, (8, BZ), 1)
    first_lane = (lanes > 0).astype(F32)
    second_lane = (lanes > 1).astype(F32)
    last_lane = (lanes < BZ - 1).astype(F32)
    last_two = (lanes < BZ - 2).astype(F32)

    def weight(cell, total):
        return jnp.maximum(16 - jnp.minimum(cell + 1, total - cell), 0).astype(F32) / 16.0

    def damping_tables(x):
        wx = weight(jnp.full((8, BZ), i * BX + x - X0, jnp.int32), AX)
        for q in range(5):
            at = pl.ds(Y0 - 4 + 8 * q, 8)
            wy = weight(rows + (j * BY - 4 + 8 * q), AY)
            d = 0.3 * (wx * wx + wy * wy)
            inv = 1.0 / (1.0 + d)
            INV[x, at] = inv
            K2[x, at] = (1.0 - d) * inv

    loop(X0 + BX + 2, damping_tables, X0 - 2)

    for sh in range(SHOTS):
        wx = weight(jnp.full((8, BZ), sources[0, sh, 0], jnp.int32), AX)
        for q in range(5):
            cells = rows + (j * BY - 4 + 8 * q)
            wy = weight(cells, AY)
            inv = 1.0 / (1.0 + 0.3 * (wx * wx + wy * wy))
            hit = (cells == sources[0, sh, 1]) & (lanes == sources[0, sh, 2])
            EY[sh, pl.ds(Y0 - 4 + 8 * q, 8)] = jnp.where(hit, inv, 0.0)

    rx = receivers[0] - i * BX
    ry = receivers[1] - j * BY
    here = (rx >= 0) & (rx < BX) & (ry >= 0) & (ry < BY)
    IDL[...] = jnp.where(here, rx * BY + ry, -1)
    deep = lax.broadcasted_iota(jnp.int32, (2 * BZ, RECS), 0) & (BZ - 1)
    OH[...] = jnp.where(deep == receivers[2], 1.0, 0.0).astype(jnp.bfloat16)

    for r in range(1, NS):
        off_copy(r).wait_send()
        shot = s ^ r
        send(OFS, OFR.at[shot], off_s.at[r], off_r.at[shot], (shot, i, j)).wait_recv()
    cp_now.wait()
    send_rows(E0, 0)
    send_sides(E0, 0)
    cp_prev.wait()
    pack(O, 2, PS)
    prev_ends = [pl.ds(X0, 2), pl.ds(X0 + BX - 2, 2)]
    prev_lands = [pl.ds(X0 + BX, 2), pl.ds(X0 - 2, 2)]
    prev_list = []
    for n, dx in ((0, -1), (1, 1)):
        prev_list.append((
            has[n], O.at[:, prev_ends[n], inner_y, :], O.at[:, prev_lands[n], inner_y, :],
            n, 1 - n, (s, i + dx, j),
        ))
    for n, dy in ((0, -1), (1, 1)):
        prev_list.append((has[2 + n], PS.at[n], PR.at[1 - n], 2 + n, 3 - n, (s, i, j + dy)))
    for ok, src, dst, n, m, dev in prev_list:
        @pl.when(ok)
        def _():
            send(src, dst, p_s.at[n], p_r.at[m], dev).start()

    cp_off = pltpu.make_async_copy(OFR, OFM, in_sem.at[0])
    cp_off.start()
    cp_off.wait()
    all_of(MT.at[pl.ds(0, GROUP - 1)], a_sem.at[0])
    all_of(R.at[pl.ds(0, GROUP - 1)], a_sem.at[1])

    send_corners(E0, 0)

    tail = me >= GROUP - 2
    head = me < 2
    shift = jnp.where(tail, -1, 1)
    firsts = [OFM[s ^ r, 0, 0] for r in range(NS)]
    columns = [firsts[r >> 2] + (i ^ (r & 3)) for r in range(GROUP)]
    for r in range(GROUP):
        plane = R[owner[columns[r]]]
        SEL[r] = plane
        EDGE[0, r] = plane[BY - 2 : BY]
        EDGE[1, r] = plane[0:2]
    halo_plane = jnp.where(tail, me - (GROUP - 2) + X0 - 2, X0 + BX + jnp.minimum(me, 1))
    halo_slot = jnp.where(tail, me - (GROUP - 2), 2 + jnp.minimum(me, 1))

    def bh_copy(r):
        return send(
            SELH.at[r], CO.at[halo_plane, inner_y, :], bh_s.at[r], bh_r.at[halo_slot], member(r)
        )

    def bh_ok(r):
        c = i ^ (r & 3)
        return (tail & (c > 0)) | (head & (c < NX - 1))

    for side, ok in ((0, has[3]), (1, has[2])):
        @pl.when(ok)
        def _():
            row = j + 1 if side == 0 else j - 1
            for r in range(GROUP):
                send(
                    EDGE.at[side, r], YM.at[side, me], e_sem.at[0, side], e_sem.at[1, side],
                    (s ^ (r >> 2), i ^ (r & 3), row),
                ).start()

    for r in range(1, GROUP):
        send(SEL.at[r], CO.at[X0 + me, inner_y, :], b_sem.at[0], b_sem.at[1], member(r)).start()

    @pl.when(tail | head)
    def _():
        for r in range(GROUP):
            SELH[r] = R[owner[jnp.clip(columns[r] + shift, 0, GROUP - 1)]]
        for r in range(1, GROUP):
            @pl.when(bh_ok(r))
            def _():
                bh_copy(r).start()

    CO[X0 + me, inner_y] = SEL[0]

    @pl.when(bh_ok(0))
    def _():
        CO[halo_plane, inner_y] = SELH[0]

    wait_some(E0, 0, range(2))
    wait_rest(E0, 0)
    for n in range(4):
        ok, src, dst, _, m, dev = prev_list[n]
        back = prev_list[[1, 0, 3, 2][n]]

        @pl.when(ok)
        def _():
            send(src, dst, p_s.at[n], p_r.at[m], dev).wait_send()
            send(back[1], back[2], p_s.at[n], p_r.at[n], dev).wait_recv()

    unpack(O, 2, PR)

    all_of(SEL.at[pl.ds(0, GROUP - 1)], b_sem.at[0])
    all_of(CO.at[pl.ds(0, GROUP - 1), inner_y, :], b_sem.at[1])

    @pl.when(tail | head)
    def _():
        for r in range(1, GROUP):
            @pl.when(bh_ok(r))
            def _():
                bh_copy(r).wait_send()

    for slot in range(4):
        source = GROUP - 2 + slot if slot < 2 else slot - 2
        plane = X0 - 2 + slot if slot < 2 else X0 + BX + slot - 2
        edge = has[0] if slot < 2 else has[1]

        @pl.when(edge & (me != source))
        def _():
            send(
                SELH.at[0], CO.at[plane, inner_y, :], bh_s.at[0], bh_r.at[slot],
                (source >> 2, source & 3, j),
            ).wait_recv()

    for side, to, back in ((0, has[3], has[2]), (1, has[2], has[3])):
        @pl.when(to)
        def _():
            all_of(EDGE.at[side], e_sem.at[0, side])

        @pl.when(back)
        def _():
            all_of(YM.at[side], e_sem.at[1, side])
            for x in range(BX):
                CO[X0 + x, pl.ds(Y0 - 2 if side == 0 else Y0 + BY, 2)] = YM[side, x]

    def model_tables(x):
        for q in range(5):
            at = pl.ds(Y0 - 4 + 8 * q, 8)
            speed = CO[x, at]
            inv = INV[x, at]
            scaled = speed * speed * inv
            KC[x, at] = 2.0 * inv - 7.5 * scaled
            KA[x, at] = (4.0 / 3.0) * scaled

    loop(X0 + BX + 2, model_tables, X0 - 2)

    def advance(
        read, before, write, first, stride, blocks, wide, tiles, step, lift=(0, 0), beside=None
    ):
        def planes(block):
            x_first = first + stride * block
            on = [
                [
                    jnp.where(
                        sources[0, sh, 0] == i * BX + x_first + k - X0, wavelet[0, sh, step], 0.0
                    )
                    for sh in range(SHOTS)
                ]
                for k in range(wide)
            ]
            for y in tiles:
                at = pl.ds(y, 8)
                line = [
                    {d: read[sh, x_first + d, at] for d in range(-2, wide + 2)} for sh in range(SHOTS)
                ]
                for k in range(wide):
                    x = x_first + k
                    kc, ka, k2 = KC[x, at], KA[x, at], K2[x, at]
                    for sh in range(SHOTS):
                        c = line[sh][k]
                        a = (line[sh][k + 1] + line[sh][k - 1]) + (
                            read[sh, x, pl.ds(y + 1, 8)] + read[sh, x, pl.ds(y - 1, 8)]
                        )
                        b = (line[sh][k + 2] + line[sh][k - 2]) + (
                            read[sh, x, pl.ds(y + 2, 8)] + read[sh, x, pl.ds(y - 2, 8)]
                        )
                        a = a + (
                            pltpu.roll(c, 1, 1) * first_lane
                            + pltpu.roll(c, BZ - 1, 1) * last_lane
                        )
                        b = b + (
                            pltpu.roll(c, 2, 1) * second_lane
                            + pltpu.roll(c, BZ - 2, 1) * last_two
                        )
                        fresh = (kc * c - k2 * before[sh, x, at]) + ka * (a - 0.0625 * b)
                        fresh = fresh + EY[sh, at] * on[k][sh]
                        write[sh, x - lift[0], pl.ds(y - lift[1], 8)] = fresh
            if beside is not None:
                beside(block)

        loop(blocks, planes)

    wide_tiles = [Y0 - 4 + 8 * q for q in range(5)]
    own_tiles = [Y0 + 8 * q for q in range(4)]

    ends = [wide_tiles[0], wide_tiles[4]]

    def outer_middle(even, step):
        advance(even, O, O, X0 + 2, 4, 3, 4, wide_tiles[1:4], step)

    def outer_sides(even, step):
        advance(even, O, O, X0 - 2, BX, 2, 4, wide_tiles[1:4], step)

    def outer_ends(even, step):
        advance(even, O, O, X0 - 2, 4, 5, 4, ends, step)

    row_ids = lax.broadcasted_iota(jnp.int32, (BX * BY, RECS), 0)

    def split(buf, block, corner):
        for sh in range(SHOTS):
            for k in range(4):
                x = 4 * block + k
                v = buf[sh, corner[0] + x, pl.ds(corner[1], BY)]
                high = v.astype(jnp.bfloat16)
                low = (v - high.astype(F32)).astype(jnp.bfloat16)
                at = pl.ds(pl.multiple_of((sh * BX + x) * BY, BY), BY)
                XB[at, 0:BZ] = high
                XB[at, BZ : 2 * BZ] = low

    def keep(pair, half, sh, got):
        row = 4 * half + 2 * sh
        TS[pair, row : row + 1] = got[:, 0:128]
        TS[pair, row + 1 : row + 2] = got[:, 128:256]

    def sample(buf, pair, half, corner=(X0, Y0)):
        loop(BX // 4, lambda block: split(buf, block, corner))
        for sh in range(SHOTS):
            picked = jnp.dot(
                XB[sh * BX * BY : (sh + 1) * BX * BY], OH[...], preferred_element_type=F32
            )
            got = jnp.sum(jnp.where(row_ids == IDL[...], picked, 0.0), axis=0, keepdims=True)
            keep(pair, half, sh, got)

    def sample_beside(buf):
        def some(block):
            split(buf, block, (X0, Y0))
            wanted = IDL[...] - 4 * BY * block
            for sh in range(SHOTS):
                at = pl.ds(pl.multiple_of((sh * BX + 4 * block) * BY, 4 * BY), 4 * BY)
                picked = jnp.dot(XB[at], OH[...], preferred_element_type=F32)
                hit = jnp.where(row_ids[: 4 * BY] == wanted, picked, 0.0)
                ACC[sh] += jnp.sum(hit.reshape(4 * BY // 8, 8, RECS), axis=0)

        return some

    def trace_send(pair):
        for r in range(1, PEERS):
            send(
                TS.at[pair], TR.at[pair, mine], t_sem.at[0, pair], t_sem.at[1, pair],
                (s, i ^ (r >> 3), j ^ (r & 7)),
            ).start()
        TR[pair, mine] = TS[pair]

    def trace_sum(pair):
        all_of(TR.at[pair, pl.ds(0, PEERS - 1)], t_sem.at[0, pair])
        all_of(TR.at[pair, pl.ds(0, PEERS - 1)], t_sem.at[1, pair])
        parts = [TR[pair, q] for q in range(PEERS)]
        while len(parts) > 1:
            parts = [a + b for a, b in zip(parts[0::2], parts[1::2])]
        for row in range(8):
            half, sh, part = row // 4, (row // 2) % 2, row % 2
            out_traces[sh, 2 * pair + half : 2 * pair + half + 1, 128 * part : 128 * part + 128] = (
                parts[0][row : row + 1]
            )

    pairs = STEPS // 2
    outer_middle(E0, 0)
    outer_sides(E0, 0)
    for pair in range(pairs):
        even, later = ((E0, E1), (E1, E0))[pair % 2]
        slot = (pair + 1) % 2
        step = 2 * pair + 1
        outer_ends(even, step - 1)
        if pair < pairs - 1:
            advance(O, even, later, X0, 4, 4, 4, [own_tiles[0], own_tiles[3]], step)
            send_rows(later, slot)
            send_corners(later, slot)
            advance(O, even, later, X0, 12, 2, 4, own_tiles[1:3], step)
            send_sides(later, slot)
            advance(O, even, later, X0 + 4, 4, 2, 4, own_tiles[1:3], step)
            sample(O, pair, 0)
            sample(later, pair, 1)
            trace_send(pair)
            outer_middle(later, step + 1)
            if pair:
                trace_sum(pair - 1)
            wait_some(later, slot, range(2))
            outer_sides(later, step + 1)
            wait_rest(later, slot)
        else:
            cp_last = pltpu.make_async_copy(
                O.at[:, inner_x, inner_y, :], out_prev.at[0], in_sem.at[2]
            )
            cp_last.start()
            final = out_now.at[0]
            ACC[...] = jnp.zeros_like(ACC)
            advance(
                O, even, final, X0, 4, 4, 4, own_tiles, step, (X0, Y0), sample_beside(O)
            )
            for sh in range(SHOTS):
                keep(pair, 0, sh, jnp.sum(ACC[sh], axis=0, keepdims=True))
            sample(final, pair, 1, (0, 0))
            trace_send(pair)
            trace_sum(pair - 1)
            trace_sum(pair)
            cp_last.wait()


def window(tiles, owner, offset, now, prev, sources, wavelet, receivers):
    any_spec = pl.BlockSpec(memory_space=pl.ANY)
    smem = pl.BlockSpec(memory_space=pltpu.SMEM)
    vmem = pl.BlockSpec(memory_space=pltpu.VMEM)
    buf = pltpu.VMEM
    dma = pltpu.SemaphoreType.DMA
    padded = (PX, PY, BZ)
    out_now, out_prev, traces = pl.pallas_call(
        kernel,
        out_shape=(
            pltpu.VMEM(now.shape, F32),
            pltpu.VMEM(prev.shape, F32),
            pltpu.VMEM((SHOTS, STEPS, RECS), F32),
        ),
        in_specs=[any_spec, smem, smem, any_spec, any_spec, smem, smem, vmem],
        out_specs=(vmem, vmem, vmem),
        scratch_shapes=[
            buf((SHOTS,) + padded, F32),
            buf((SHOTS,) + padded, F32),
            buf((SHOTS,) + padded, F32),
            buf((BX, BY, BZ), F32),
            buf((GROUP, BY, BZ), F32),
            buf((GROUP, BY, BZ), F32),
            buf((GROUP, BY, BZ), F32),
            buf((2, GROUP, 2, BZ), F32),
            buf((2, GROUP, 2, BZ), F32),
            buf(padded, F32),
            buf(padded, F32),
            buf(padded, F32),
            buf(padded, F32),
            buf(padded, F32),
            buf((SHOTS, PY, BZ), F32),
            buf((2, SHOTS * BX, 4, BZ), F32),
            buf((2, 2, SHOTS * BX, 4, BZ), F32),
            buf((4, 8, BZ), F32),
            buf((2, 4, 8, BZ), F32),
            buf((2, SHOTS * BX, 2, BZ), F32),
            buf((2, SHOTS * BX, 2, BZ), F32),
            buf((1, BZ), jnp.int32),
            buf((NS, 1, BZ), jnp.int32),
            pltpu.SMEM((NS, 1, BZ), jnp.int32),
            buf((2 * BZ, RECS), jnp.bfloat16),
            buf((1, RECS), jnp.int32),
            buf((SHOTS * BX * BY, 2 * BZ), jnp.bfloat16),
            buf((SHOTS, 8, RECS), F32),
            buf((STEPS // 2, 8, 128), F32),
            buf((STEPS // 2, PEERS, 8, 128), F32),
            dma((3,)), dma((NS,)), dma((NS,)), dma((2,)), dma((2,)),
            dma((GROUP,)), dma((4,)), dma((2, 2)),
            dma((2, 8)), dma((2, 8)), dma((4,)), dma((4,)), dma((2, STEPS // 2)),
        ],
        compiler_params=pltpu.CompilerParams(collective_id=0, has_side_effects=True),
    )(tiles, owner, offset, now, prev, sources, wavelet, jnp.transpose(receivers, (2, 0, 1)))
    return out_now, out_prev, jnp.transpose(traces, (0, 2, 1))[None]


def solution(mesh):
    return jax.shard_map(
        window,
        mesh=mesh,
        in_specs=(
            P(("shot", "gx"), "gy", None),
            P(),
            P("shot"),
            P("shot", None, "gx", "gy", None),
            P("shot", None, "gx", "gy", None),
            P("shot", None, None),
            P("shot", None, None),
            P("shot", None, None),
        ),
        out_specs=(
            P("shot", None, "gx", "gy", None),
            P("shot", None, "gx", "gy", None),
            P("shot", None, None, None),
        ),
        check_vma=False,
    )
```

```python
import jax
import jax.numpy as jnp
from jax import lax
from jax.experimental import pallas as pl
from jax.experimental.pallas import tpu as pltpu
from jax.sharding import PartitionSpec as P

STEPS = 8
SHOTS = 2
NS, NX, NY = 4, 4, 8
GROUP = NS * NX
PEERS = NX * NY
BX, BY, BZ = 16, 32, 128
AX, AY = NX * BX, NY * BY
RECS = 256
PX, PY = BX + 8, BY + 16
X0, Y0 = 4, 8
MESH = pl.DeviceIdType.MESH
F32 = jnp.float32


RING = (0, 1, 2, 1)
ROW_ORDER = sorted(range(1, GROUP), key=lambda r: -RING[r & 3] - (r >> 3))
SHOT_ORDER = sorted(
    range(1, PEERS), key=lambda r: -RING[r >> 3] - RING[(r & 7) >> 1] - 2 * (r & 1)
)


def loop(n, body, start=0):
    lax.fori_loop(start, n, lambda k, c: (body(k), c)[1], 0)


def kernel(
    tiles, owner, offset, now, prev, sources, wavelet, receivers,
    out_now, out_prev, out_traces,
    E0, E1, O, MT, R, SEL, SELH, EDGE, YM, CO, KC, KA, K2, INV, EY,
    YS, YR, CS, CR, PS, PR, OFS, OFR, OFM, OH, IDL, XB, ACC, TS, TR, TX, TY, TG, W,
    in_sem, off_s, off_r, a_sem, b_sem, bh_s, bh_r, e_sem,
    h_s, h_r, p_s, p_r, t_sem, x_sem, y_sem,
):
    s = lax.axis_index("shot")
    i = lax.axis_index("gx")
    j = lax.axis_index("gy")
    me = s * NX + i
    mine = i * NY + j

    def member(r):
        return (s ^ (r >> 2), i ^ (r & 3), j)

    def all_of(ref, sem):
        pltpu.make_async_copy(ref, ref, sem).wait()

    def send(src, dst, ssem, rsem, dev):
        return pltpu.make_async_remote_copy(
            src_ref=src, dst_ref=dst, send_sem=ssem, recv_sem=rsem,
            device_id=dev, device_id_type=MESH,
        )

    inner_x = pl.ds(X0, BX)
    inner_y = pl.ds(Y0, BY)
    has = [i > 0, i < NX - 1, j > 0, j < NY - 1]

    cp_mt = pltpu.make_async_copy(tiles, MT, in_sem.at[0])
    cp_now = pltpu.make_async_copy(now.at[0], E0.at[:, inner_x, inner_y, :], in_sem.at[1])
    cp_prev = pltpu.make_async_copy(prev.at[0], O.at[:, inner_x, inner_y, :], in_sem.at[2])
    cp_mt.start()
    cp_now.start()
    cp_prev.start()

    barrier = pltpu.get_barrier_semaphore()

    def greet(dev):
        pl.semaphore_signal(barrier, inc=1, device_id=dev, device_id_type=MESH)

    for r in range(1, NY):
        greet((s, i, j ^ r))
    for r in range(1, GROUP):
        greet(member(r))
    pl.semaphore_wait(barrier, GROUP + NY - 2)

    OFS[...] = jnp.full((1, BZ), offset[0], jnp.int32)

    def off_copy(r):
        return send(OFS, OFR.at[s], off_s.at[r], off_r.at[s], (s ^ r, i, j))

    for r in range(1, NS):
        off_copy(r).start()
    OFR[s] = jnp.full((1, BZ), offset[0], jnp.int32)

    cp_mt.wait()
    for r in ROW_ORDER:
        send(MT.at[me ^ r], R.at[me], a_sem.at[0], a_sem.at[1], member(r)).start()
    R[me] = MT[me]

    def pack(buf, depth, store):
        for x in range(BX):
            for sh in range(SHOTS):
                store[0, sh * BX + x] = buf[sh, X0 + x, pl.ds(Y0, depth)]
                store[1, sh * BX + x] = buf[sh, X0 + x, pl.ds(Y0 + BY - depth, depth)]

    def unpack(buf, depth, store):
        for side, y in ((0, Y0 - depth), (1, Y0 + BY)):
            @pl.when(has[2 + side])
            def _():
                for x in range(BX):
                    for sh in range(SHOTS):
                        buf[sh, X0 + x, pl.ds(y, depth)] = store[side, sh * BX + x]

    corners = [(-1, -1), (-1, 1), (1, -1), (1, 1)]

    def halo_list(buf, slot):
        ends = [pl.ds(X0, 4), pl.ds(X0 + BX - 4, 4)]
        lands = [pl.ds(X0 + BX, 4), pl.ds(X0 - 4, 4)]
        found = []
        for n, dx in ((0, -1), (1, 1)):
            found.append((
                has[n], buf.at[:, ends[n], inner_y, :], buf.at[:, lands[n], inner_y, :],
                n, 1 - n, (s, i + dx, j),
            ))
        for n, dy in ((0, -1), (1, 1)):
            found.append((
                has[2 + n], YS.at[n], YR.at[slot, 1 - n], 2 + n, 3 - n, (s, i, j + dy),
            ))
        for n, (dx, dy) in enumerate(corners):
            ok = has[0 if dx < 0 else 1] & has[2 if dy < 0 else 3]
            found.append((
                ok, CS.at[n], CR.at[slot, 3 - n], 4 + n, 7 - n, (s, i + dx, j + dy),
            ))
        return found

    def start_some(copies, slot):
        for ok, src, dst, n, m, dev in copies:
            @pl.when(ok)
            def _():
                send(src, dst, h_s.at[slot, n], h_r.at[slot, m], dev).start()

    def send_sides(buf, slot):
        start_some(halo_list(buf, slot)[0:2], slot)

    def send_rows(buf, slot):
        pack(buf, 4, YS)
        start_some(halo_list(buf, slot)[2:4], slot)

    def send_corners(buf, slot):
        for n, (dx, dy) in enumerate(corners):
            for sh in range(SHOTS):
                for k in range(2):
                    x = X0 + k if dx < 0 else X0 + BX - 2 + k
                    y = Y0 if dy < 0 else Y0 + BY - 2
                    CS[n, sh * 4 + k * 2 : sh * 4 + k * 2 + 2] = buf[sh, x, y : y + 2]
        start_some(halo_list(buf, slot)[4:8], slot)

    def wait_some(buf, slot, which):
        copies = halo_list(buf, slot)
        opposite = [1, 0, 3, 2, 7, 6, 5, 4]
        for n in which:
            ok, src, dst, _, m, dev = copies[n]
            back = copies[opposite[n]]

            @pl.when(ok)
            def _():
                send(src, dst, h_s.at[slot, n], h_r.at[slot, m], dev).wait_send()
                send(back[1], back[2], h_s.at[slot, n], h_r.at[slot, n], dev).wait_recv()

    def wait_rest(buf, slot):
        copies = halo_list(buf, slot)
        wait_some(buf, slot, range(2, 8))
        unpack(buf, 4, YR.at[slot])
        for n, (dx, dy) in enumerate(corners):
            @pl.when(copies[4 + n][0])
            def _():
                for sh in range(SHOTS):
                    for k in range(2):
                        x = X0 - 2 + k if dx < 0 else X0 + BX + k
                        y = Y0 - 2 if dy < 0 else Y0 + BY
                        buf[sh, x, y : y + 2] = CR[slot, n, sh * 4 + k * 2 : sh * 4 + k * 2 + 2]

    for n, first in ((0, 0), (1, PX - 4)):
        @pl.when(jnp.logical_not(has[n]))
        def _():
            blank = jnp.zeros((4, PY, BZ), F32)
            for buf in (E0, E1, O):
                for sh in range(SHOTS):
                    buf[sh, first : first + 4] = blank
            CO[first : first + 4] = blank

    for n, first in ((2, 0), (3, PY - 8)):
        @pl.when(jnp.logical_not(has[n]))
        def _():
            blank = jnp.zeros((8, BZ), F32)

            def one(x):
                for buf in (E0, E1, O):
                    for sh in range(SHOTS):
                        buf[sh, x, first : first + 8] = blank
                CO[x, first : first + 8] = blank

            loop(PX, one)

    rows = lax.broadcasted_iota(jnp.int32, (8, BZ), 0)
    lanes = lax.broadcasted_iota(jnp.int32, (8, BZ), 1)
    first_lane = (lanes > 0).astype(F32)
    second_lane = (lanes > 1).astype(F32)
    last_lane = (lanes < BZ - 1).astype(F32)
    last_two = (lanes < BZ - 2).astype(F32)

    def weight(cell, total):
        return jnp.maximum(16 - jnp.minimum(cell + 1, total - cell), 0).astype(F32) / 16.0

    def damping_tables(x):
        wx = weight(jnp.full((8, BZ), i * BX + x - X0, jnp.int32), AX)
        for q in range(5):
            at = pl.ds(Y0 - 4 + 8 * q, 8)
            wy = weight(rows + (j * BY - 4 + 8 * q), AY)
            d = 0.3 * (wx * wx + wy * wy)
            inv = 1.0 / (1.0 + d)
            INV[x, at] = inv
            K2[x, at] = (1.0 - d) * inv

    loop(X0 + BX + 2, damping_tables, X0 - 2)

    for sh in range(SHOTS):
        wx = weight(jnp.full((8, BZ), sources[0, sh, 0], jnp.int32), AX)
        for q in range(5):
            cells = rows + (j * BY - 4 + 8 * q)
            wy = weight(cells, AY)
            inv = 1.0 / (1.0 + 0.3 * (wx * wx + wy * wy))
            hit = (cells == sources[0, sh, 1]) & (lanes == sources[0, sh, 2])
            EY[sh, pl.ds(Y0 - 4 + 8 * q, 8)] = jnp.where(hit, inv, 0.0)

    rx = receivers[0] - i * BX
    ry = receivers[1] - j * BY
    here = (rx >= 0) & (rx < BX) & (ry >= 0) & (ry < BY)
    IDL[...] = jnp.where(here, rx * BY + ry, -1)
    deep = lax.broadcasted_iota(jnp.int32, (2 * BZ, RECS), 0) & (BZ - 1)
    OH[...] = jnp.where(deep == receivers[2], 1.0, 0.0).astype(jnp.bfloat16)

    for r in range(1, NS):
        off_copy(r).wait_send()
        shot = s ^ r
        send(OFS, OFR.at[shot], off_s.at[r], off_r.at[shot], (shot, i, j)).wait_recv()
    cp_now.wait()
    send_rows(E0, 0)
    send_sides(E0, 0)
    cp_prev.wait()
    pack(O, 2, PS)
    prev_ends = [pl.ds(X0, 2), pl.ds(X0 + BX - 2, 2)]
    prev_lands = [pl.ds(X0 + BX, 2), pl.ds(X0 - 2, 2)]
    prev_list = []
    for n, dx in ((0, -1), (1, 1)):
        prev_list.append((
            has[n], O.at[:, prev_ends[n], inner_y, :], O.at[:, prev_lands[n], inner_y, :],
            n, 1 - n, (s, i + dx, j),
        ))
    for n, dy in ((0, -1), (1, 1)):
        prev_list.append((has[2 + n], PS.at[n], PR.at[1 - n], 2 + n, 3 - n, (s, i, j + dy)))
    for ok, src, dst, n, m, dev in prev_list:
        @pl.when(ok)
        def _():
            send(src, dst, p_s.at[n], p_r.at[m], dev).start()

    cp_off = pltpu.make_async_copy(OFR, OFM, in_sem.at[0])
    cp_off.start()
    cp_off.wait()
    all_of(MT.at[pl.ds(0, GROUP - 1)], a_sem.at[0])
    all_of(R.at[pl.ds(0, GROUP - 1)], a_sem.at[1])

    send_corners(E0, 0)

    tail = me >= GROUP - 2
    head = me < 2
    shift = jnp.where(tail, -1, 1)
    firsts = [OFM[s ^ r, 0, 0] for r in range(NS)]
    columns = [firsts[r >> 2] + (i ^ (r & 3)) for r in range(GROUP)]
    for r in range(GROUP):
        plane = R[owner[columns[r]]]
        SEL[r] = plane
        EDGE[0, r] = plane[BY - 2 : BY]
        EDGE[1, r] = plane[0:2]
    halo_plane = jnp.where(tail, me - (GROUP - 2) + X0 - 2, X0 + BX + jnp.minimum(me, 1))
    halo_slot = jnp.where(tail, me - (GROUP - 2), 2 + jnp.minimum(me, 1))

    def bh_copy(r):
        return send(
            SELH.at[r], CO.at[halo_plane, inner_y, :], bh_s.at[r], bh_r.at[halo_slot], member(r)
        )

    def bh_ok(r):
        c = i ^ (r & 3)
        return (tail & (c > 0)) | (head & (c < NX - 1))

    for side, ok in ((0, has[3]), (1, has[2])):
        @pl.when(ok)
        def _():
            row = j + 1 if side == 0 else j - 1
            for r in range(GROUP):
                send(
                    EDGE.at[side, r], YM.at[side, me], e_sem.at[0, side], e_sem.at[1, side],
                    (s ^ (r >> 2), i ^ (r & 3), row),
                ).start()

    for r in ROW_ORDER:
        send(SEL.at[r], CO.at[X0 + me, inner_y, :], b_sem.at[0], b_sem.at[1], member(r)).start()

    @pl.when(tail | head)
    def _():
        for r in range(GROUP):
            SELH[r] = R[owner[jnp.clip(columns[r] + shift, 0, GROUP - 1)]]
        for r in range(1, GROUP):
            @pl.when(bh_ok(r))
            def _():
                bh_copy(r).start()

    CO[X0 + me, inner_y] = SEL[0]

    @pl.when(bh_ok(0))
    def _():
        CO[halo_plane, inner_y] = SELH[0]

    wait_some(E0, 0, range(2))
    wait_rest(E0, 0)
    for n in range(4):
        ok, src, dst, _, m, dev = prev_list[n]
        back = prev_list[[1, 0, 3, 2][n]]

        @pl.when(ok)
        def _():
            send(src, dst, p_s.at[n], p_r.at[m], dev).wait_send()
            send(back[1], back[2], p_s.at[n], p_r.at[n], dev).wait_recv()

    unpack(O, 2, PR)

    def advance(
        read, before, write, first, stride, blocks, wide, tiles, step, lift=(0, 0), beside=None,
        ahead=False,
    ):
        def planes(block):
            x_first = first + stride * block
            on = [
                [
                    jnp.where(
                        sources[0, sh, 0] == i * BX + x_first + k - X0, wavelet[0, sh, step], 0.0
                    )
                    for sh in range(SHOTS)
                ]
                for k in range(wide)
            ]
            for y in tiles:
                at = pl.ds(y, 8)
                line = [
                    {d: read[sh, x_first + d, at] for d in range(-2, wide + 2)} for sh in range(SHOTS)
                ]
                for k in range(wide):
                    x = x_first + k
                    if not ahead:
                        kc, ka, k2 = KC[x, at], KA[x, at], K2[x, at]
                    for sh in range(SHOTS):
                        c = line[sh][k]
                        a = (line[sh][k + 1] + line[sh][k - 1]) + (
                            read[sh, x, pl.ds(y + 1, 8)] + read[sh, x, pl.ds(y - 1, 8)]
                        )
                        b = (line[sh][k + 2] + line[sh][k - 2]) + (
                            read[sh, x, pl.ds(y + 2, 8)] + read[sh, x, pl.ds(y - 2, 8)]
                        )
                        a = a + (
                            pltpu.roll(c, 1, 1) * first_lane
                            + pltpu.roll(c, BZ - 1, 1) * last_lane
                        )
                        b = b + (
                            pltpu.roll(c, 2, 1) * second_lane
                            + pltpu.roll(c, BZ - 2, 1) * last_two
                        )
                        if ahead:
                            write[sh, x, at] = a - 0.0625 * b
                            continue
                        fresh = (kc * c - k2 * before[sh, x, at]) + ka * (a - 0.0625 * b)
                        fresh = fresh + EY[sh, at] * on[k][sh]
                        write[sh, x - lift[0], pl.ds(y - lift[1], 8)] = fresh
            if beside is not None:
                beside(block)

        loop(blocks, planes)

    wide_tiles = [Y0 - 4 + 8 * q for q in range(5)]
    own_tiles = [Y0 + 8 * q for q in range(4)]

    advance(E0, O, W, X0 - 2, 4, 5, 4, wide_tiles, 0, ahead=True)

    all_of(SEL.at[pl.ds(0, GROUP - 1)], b_sem.at[0])
    all_of(CO.at[pl.ds(0, GROUP - 1), inner_y, :], b_sem.at[1])

    @pl.when(tail | head)
    def _():
        for r in range(1, GROUP):
            @pl.when(bh_ok(r))
            def _():
                bh_copy(r).wait_send()

    for slot in range(4):
        source = GROUP - 2 + slot if slot < 2 else slot - 2
        plane = X0 - 2 + slot if slot < 2 else X0 + BX + slot - 2
        edge = has[0] if slot < 2 else has[1]

        @pl.when(edge & (me != source))
        def _():
            send(
                SELH.at[0], CO.at[plane, inner_y, :], bh_s.at[0], bh_r.at[slot],
                (source >> 2, source & 3, j),
            ).wait_recv()

    for side, to, back in ((0, has[3], has[2]), (1, has[2], has[3])):
        @pl.when(to)
        def _():
            all_of(EDGE.at[side], e_sem.at[0, side])

        @pl.when(back)
        def _():
            all_of(YM.at[side], e_sem.at[1, side])
            for x in range(BX):
                CO[X0 + x, pl.ds(Y0 - 2 if side == 0 else Y0 + BY, 2)] = YM[side, x]

    def first_step(x):
        on = [
            jnp.where(sources[0, sh, 0] == i * BX + x - X0, wavelet[0, sh, 0], 0.0)
            for sh in range(SHOTS)
        ]
        for y in wide_tiles:
            at = pl.ds(y, 8)
            speed = CO[x, at]
            inv = INV[x, at]
            scaled = speed * speed * inv
            kc = 2.0 * inv - 7.5 * scaled
            ka = (4.0 / 3.0) * scaled
            k2 = K2[x, at]
            KC[x, at] = kc
            KA[x, at] = ka
            for sh in range(SHOTS):
                fresh = (kc * E0[sh, x, at] - k2 * O[sh, x, at]) + ka * W[sh, x, at]
                O[sh, x, at] = fresh + EY[sh, at] * on[sh]

    loop(X0 + BX + 2, first_step, X0 - 2)

    ends = [wide_tiles[0], wide_tiles[4]]

    def outer_middle(even, step):
        advance(even, O, O, X0 + 2, 4, 3, 4, wide_tiles[1:4], step)

    def outer_sides(even, step):
        advance(even, O, O, X0 - 2, BX, 2, 4, wide_tiles[1:4], step)

    def outer_ends(even, step):
        advance(even, O, O, X0 - 2, 4, 5, 4, ends, step)

    row_ids = lax.broadcasted_iota(jnp.int32, (BX * BY, RECS), 0)

    def split(buf, block, corner):
        for sh in range(SHOTS):
            for k in range(4):
                x = 4 * block + k
                v = buf[sh, corner[0] + x, pl.ds(corner[1], BY)]
                high = v.astype(jnp.bfloat16)
                low = (v - high.astype(F32)).astype(jnp.bfloat16)
                at = pl.ds(pl.multiple_of((sh * BX + x) * BY, BY), BY)
                XB[at, 0:BZ] = high
                XB[at, BZ : 2 * BZ] = low

    def keep(pair, half, sh, got):
        row = 4 * half + 2 * sh
        TS[pair, row : row + 1] = got[:, 0:128]
        TS[pair, row + 1 : row + 2] = got[:, 128:256]

    def sample(buf, pair, half, corner=(X0, Y0)):
        loop(BX // 4, lambda block: split(buf, block, corner))
        for sh in range(SHOTS):
            picked = jnp.dot(
                XB[sh * BX * BY : (sh + 1) * BX * BY], OH[...], preferred_element_type=F32
            )
            got = jnp.sum(jnp.where(row_ids == IDL[...], picked, 0.0), axis=0, keepdims=True)
            keep(pair, half, sh, got)

    def sample_beside(buf):
        def some(block):
            split(buf, block, (X0, Y0))
            wanted = IDL[...] - 4 * BY * block
            for sh in range(SHOTS):
                at = pl.ds(pl.multiple_of((sh * BX + 4 * block) * BY, 4 * BY), 4 * BY)
                picked = jnp.dot(XB[at], OH[...], preferred_element_type=F32)
                hit = jnp.where(row_ids[: 4 * BY] == wanted, picked, 0.0)
                ACC[sh] += jnp.sum(hit.reshape(4 * BY // 8, 8, RECS), axis=0)

        return some

    def trace_gx(pair):
        for r in (2, 1, 3):
            send(
                TS.at[pair], TX.at[pair, i], x_sem.at[0, pair], x_sem.at[1, pair], (s, i ^ r, j)
            ).start()
        TX[pair, i] = TS[pair]

    def tree(parts):
        while len(parts) > 1:
            parts = [a + b for a, b in zip(parts[0::2], parts[1::2])]
        return parts[0]

    def trace_gy(pair):
        all_of(TX.at[pair, pl.ds(0, NX - 1)], x_sem.at[0, pair])
        all_of(TX.at[pair, pl.ds(0, NX - 1)], x_sem.at[1, pair])
        TG[pair] = tree([TX[pair, q] for q in range(NX)])
        for r in range(NY - 1, 0, -1):
            send(
                TG.at[pair], TY.at[pair, j], y_sem.at[0, pair], y_sem.at[1, pair], (s, i, j ^ r)
            ).start()
        TY[pair, j] = TG[pair]

    def put_traces(pair, total):
        for row in range(8):
            half, sh, part = row // 4, (row // 2) % 2, row % 2
            out_traces[sh, 2 * pair + half : 2 * pair + half + 1, 128 * part : 128 * part + 128] = (
                total[row : row + 1]
            )

    def trace_out(pair):
        all_of(TY.at[pair, pl.ds(0, NY - 1)], y_sem.at[0, pair])
        all_of(TY.at[pair, pl.ds(0, NY - 1)], y_sem.at[1, pair])
        put_traces(pair, tree([TY[pair, q] for q in range(NY)]))

    pairs = STEPS // 2
    for pair in range(pairs):
        even, later = ((E0, E1), (E1, E0))[pair % 2]
        slot = (pair + 1) % 2
        step = 2 * pair + 1
        if pair:
            outer_ends(even, step - 1)
        if pair < pairs - 1:
            advance(O, even, later, X0, 4, 4, 4, [own_tiles[0], own_tiles[3]], step)
            send_corners(later, slot)
            send_rows(later, slot)
            advance(O, even, later, X0, 12, 2, 4, own_tiles[1:3], step)
            send_sides(later, slot)
            advance(O, even, later, X0 + 4, 4, 2, 4, own_tiles[1:3], step)
            sample(O, pair, 0)
            sample(later, pair, 1)
            trace_gx(pair)
            if pair:
                trace_gy(pair - 1)
            outer_middle(later, step + 1)
            if pair > 1:
                trace_out(pair - 2)
            wait_some(later, slot, range(2))
            outer_sides(later, step + 1)
            wait_rest(later, slot)
        else:
            cp_last = pltpu.make_async_copy(
                O.at[:, inner_x, inner_y, :], out_prev.at[0], in_sem.at[2]
            )
            cp_last.start()
            final = out_now.at[0]
            ACC[...] = jnp.zeros_like(ACC)
            advance(
                O, even, final, X0, 4, 4, 4, own_tiles, step, (X0, Y0), sample_beside(O)
            )
            for sh in range(SHOTS):
                keep(pair, 0, sh, jnp.sum(ACC[sh], axis=0, keepdims=True))
            sample(final, pair, 1, (0, 0))
            for r in SHOT_ORDER:
                send(
                    TS.at[pair], TR.at[mine], t_sem.at[0], t_sem.at[1],
                    (s, i ^ (r >> 3), j ^ (r & 7)),
                ).start()
            TR[mine] = TS[pair]
            trace_gy(pair - 1)
            trace_out(pair - 2)
            cp_last.wait()
            trace_out(pair - 1)
            all_of(TR.at[pl.ds(0, PEERS - 1)], t_sem.at[0])
            all_of(TR.at[pl.ds(0, PEERS - 1)], t_sem.at[1])
            put_traces(pair, tree([TR[q] for q in range(PEERS)]))


def window(tiles, owner, offset, now, prev, sources, wavelet, receivers):
    any_spec = pl.BlockSpec(memory_space=pl.ANY)
    smem = pl.BlockSpec(memory_space=pltpu.SMEM)
    vmem = pl.BlockSpec(memory_space=pltpu.VMEM)
    buf = pltpu.VMEM
    dma = pltpu.SemaphoreType.DMA
    padded = (PX, PY, BZ)
    out_now, out_prev, traces = pl.pallas_call(
        kernel,
        out_shape=(
            pltpu.VMEM(now.shape, F32),
            pltpu.VMEM(prev.shape, F32),
            pltpu.VMEM((SHOTS, STEPS, RECS), F32),
        ),
        in_specs=[any_spec, smem, smem, any_spec, any_spec, smem, smem, vmem],
        out_specs=(vmem, vmem, vmem),
        scratch_shapes=[
            buf((SHOTS,) + padded, F32),
            buf((SHOTS,) + padded, F32),
            buf((SHOTS,) + padded, F32),
            buf((BX, BY, BZ), F32),
            buf((GROUP, BY, BZ), F32),
            buf((GROUP, BY, BZ), F32),
            buf((GROUP, BY, BZ), F32),
            buf((2, GROUP, 2, BZ), F32),
            buf((2, GROUP, 2, BZ), F32),
            buf(padded, F32),
            buf(padded, F32),
            buf(padded, F32),
            buf(padded, F32),
            buf(padded, F32),
            buf((SHOTS, PY, BZ), F32),
            buf((2, SHOTS * BX, 4, BZ), F32),
            buf((2, 2, SHOTS * BX, 4, BZ), F32),
            buf((4, 8, BZ), F32),
            buf((2, 4, 8, BZ), F32),
            buf((2, SHOTS * BX, 2, BZ), F32),
            buf((2, SHOTS * BX, 2, BZ), F32),
            buf((1, BZ), jnp.int32),
            buf((NS, 1, BZ), jnp.int32),
            pltpu.SMEM((NS, 1, BZ), jnp.int32),
            buf((2 * BZ, RECS), jnp.bfloat16),
            buf((1, RECS), jnp.int32),
            buf((SHOTS * BX * BY, 2 * BZ), jnp.bfloat16),
            buf((SHOTS, 8, RECS), F32),
            buf((STEPS // 2, 8, 128), F32),
            buf((PEERS, 8, 128), F32),
            buf((STEPS // 2 - 1, NX, 8, 128), F32),
            buf((STEPS // 2 - 1, NY, 8, 128), F32),
            buf((STEPS // 2 - 1, 8, 128), F32),
            buf((SHOTS,) + padded, F32),
            dma((3,)), dma((NS,)), dma((NS,)), dma((2,)), dma((2,)),
            dma((GROUP,)), dma((4,)), dma((2, 2)),
            dma((2, 8)), dma((2, 8)), dma((4,)), dma((4,)), dma((2,)),
            dma((2, STEPS // 2 - 1)), dma((2, STEPS // 2 - 1)),
        ],
        compiler_params=pltpu.CompilerParams(collective_id=0, has_side_effects=True),
    )(tiles, owner, offset, now, prev, sources, wavelet, jnp.transpose(receivers, (2, 0, 1)))
    return out_now, out_prev, jnp.transpose(traces, (0, 2, 1))[None]


def solution(mesh):
    return jax.shard_map(
        window,
        mesh=mesh,
        in_specs=(
            P(("shot", "gx"), "gy", None),
            P(),
            P("shot"),
            P("shot", None, "gx", "gy", None),
            P("shot", None, "gx", "gy", None),
            P("shot", None, None),
            P("shot", None, None),
            P("shot", None, None),
        ),
        out_specs=(
            P("shot", None, "gx", "gy", None),
            P("shot", None, "gx", "gy", None),
            P("shot", None, None, None),
        ),
        check_vma=False,
    )
```

```python
import jax
import jax.numpy as jnp
from jax import lax
from jax.experimental import pallas as pl
from jax.experimental.pallas import tpu as pltpu
from jax.sharding import PartitionSpec as P

STEPS = 8
SHOTS = 2
NS, NX, NY = 4, 4, 8
GROUP = NS * NX
PEERS = NX * NY
BX, BY, BZ = 16, 32, 128
AX, AY = NX * BX, NY * BY
RECS = 256
PX, PY = BX + 8, BY + 16
X0, Y0 = 4, 8
MESH = pl.DeviceIdType.MESH
F32 = jnp.float32


RING = (0, 1, 2, 1)
ROW_ORDER = sorted(range(1, GROUP), key=lambda r: -RING[r & 3] - (r >> 3))
SHOT_ORDER = sorted(
    range(1, PEERS), key=lambda r: -RING[r >> 3] - RING[(r & 7) >> 1] - 2 * (r & 1)
)


def loop(n, body, start=0):
    lax.fori_loop(start, n, lambda k, c: (body(k), c)[1], 0)


def kernel(
    tiles, owner, offset, now, prev, sources, wavelet, receivers,
    out_now, out_prev, out_traces,
    E0, E1, O, MT, R, SEL, SELH, EDGE, YM, CO, KC, KA, K2, INV, EY,
    YS, YR, CS, CR, PS, PR, OFS, OFR, OFM, OH, IDL, XB, ACC, TS, TR, TX, TY, TG, W,
    in_sem, off_s, off_r, a_sem, b_sem, bh_s, bh_r, e_sem,
    h_s, h_r, p_s, p_r, t_sem, x_sem, y_sem,
):
    s = lax.axis_index("shot")
    i = lax.axis_index("gx")
    j = lax.axis_index("gy")
    me = s * NX + i
    mine = i * NY + j

    def member(r):
        return (s ^ (r >> 2), i ^ (r & 3), j)

    def all_of(ref, sem):
        pltpu.make_async_copy(ref, ref, sem).wait()

    def send(src, dst, ssem, rsem, dev):
        return pltpu.make_async_remote_copy(
            src_ref=src, dst_ref=dst, send_sem=ssem, recv_sem=rsem,
            device_id=dev, device_id_type=MESH,
        )

    inner_x = pl.ds(X0, BX)
    inner_y = pl.ds(Y0, BY)
    has = [i > 0, i < NX - 1, j > 0, j < NY - 1]

    cp_mt = pltpu.make_async_copy(tiles, MT, in_sem.at[0])
    cp_now = pltpu.make_async_copy(now.at[0], E0.at[:, inner_x, inner_y, :], in_sem.at[1])
    cp_prev = pltpu.make_async_copy(prev.at[0], O.at[:, inner_x, inner_y, :], in_sem.at[2])
    cp_mt.start()
    cp_now.start()
    cp_prev.start()

    barrier = pltpu.get_barrier_semaphore()

    def greet(dev):
        pl.semaphore_signal(barrier, inc=1, device_id=dev, device_id_type=MESH)

    for r in range(1, NY):
        greet((s, i, j ^ r))
    for r in range(1, GROUP):
        greet(member(r))
    pl.semaphore_wait(barrier, GROUP + NY - 2)

    OFS[...] = jnp.full((1, BZ), offset[0], jnp.int32)

    def off_copy(r):
        return send(OFS, OFR.at[s], off_s.at[r], off_r.at[s], (s ^ r, i, j))

    for r in range(1, NS):
        off_copy(r).start()
    OFR[s] = jnp.full((1, BZ), offset[0], jnp.int32)

    cp_mt.wait()
    for r in ROW_ORDER:
        send(MT.at[me ^ r], R.at[me], a_sem.at[0], a_sem.at[1], member(r)).start()
    R[me] = MT[me]

    def pack(buf, depth, store):
        for x in range(BX):
            for sh in range(SHOTS):
                store[0, sh * BX + x] = buf[sh, X0 + x, pl.ds(Y0, depth)]
                store[1, sh * BX + x] = buf[sh, X0 + x, pl.ds(Y0 + BY - depth, depth)]

    def unpack(buf, depth, store):
        for side, y in ((0, Y0 - depth), (1, Y0 + BY)):
            @pl.when(has[2 + side])
            def _():
                for x in range(BX):
                    for sh in range(SHOTS):
                        buf[sh, X0 + x, pl.ds(y, depth)] = store[side, sh * BX + x]

    corners = [(-1, -1), (-1, 1), (1, -1), (1, 1)]

    def halo_list(buf, slot):
        ends = [pl.ds(X0, 4), pl.ds(X0 + BX - 4, 4)]
        lands = [pl.ds(X0 + BX, 4), pl.ds(X0 - 4, 4)]
        found = []
        for n, dx in ((0, -1), (1, 1)):
            found.append((
                has[n], buf.at[:, ends[n], inner_y, :], buf.at[:, lands[n], inner_y, :],
                n, 1 - n, (s, i + dx, j),
            ))
        for n, dy in ((0, -1), (1, 1)):
            found.append((
                has[2 + n], YS.at[n], YR.at[slot, 1 - n], 2 + n, 3 - n, (s, i, j + dy),
            ))
        for n, (dx, dy) in enumerate(corners):
            ok = has[0 if dx < 0 else 1] & has[2 if dy < 0 else 3]
            found.append((
                ok, CS.at[n], CR.at[slot, 3 - n], 4 + n, 7 - n, (s, i + dx, j + dy),
            ))
        return found

    def start_some(copies, slot):
        for ok, src, dst, n, m, dev in copies:
            @pl.when(ok)
            def _():
                send(src, dst, h_s.at[slot, n], h_r.at[slot, m], dev).start()

    def send_sides(buf, slot):
        start_some(halo_list(buf, slot)[0:2], slot)

    def send_rows(buf, slot):
        pack(buf, 4, YS)
        start_some(halo_list(buf, slot)[2:4], slot)

    def send_corners(buf, slot):
        for n, (dx, dy) in enumerate(corners):
            for sh in range(SHOTS):
                for k in range(2):
                    x = X0 + k if dx < 0 else X0 + BX - 2 + k
                    y = Y0 if dy < 0 else Y0 + BY - 2
                    CS[n, sh * 4 + k * 2 : sh * 4 + k * 2 + 2] = buf[sh, x, y : y + 2]
        start_some(halo_list(buf, slot)[4:8], slot)

    def wait_some(buf, slot, which):
        copies = halo_list(buf, slot)
        opposite = [1, 0, 3, 2, 7, 6, 5, 4]
        for n in which:
            ok, src, dst, _, m, dev = copies[n]
            back = copies[opposite[n]]

            @pl.when(ok)
            def _():
                send(src, dst, h_s.at[slot, n], h_r.at[slot, m], dev).wait_send()
                send(back[1], back[2], h_s.at[slot, n], h_r.at[slot, n], dev).wait_recv()

    def wait_rest(buf, slot):
        copies = halo_list(buf, slot)
        wait_some(buf, slot, range(2, 8))
        unpack(buf, 4, YR.at[slot])
        for n, (dx, dy) in enumerate(corners):
            @pl.when(copies[4 + n][0])
            def _():
                for sh in range(SHOTS):
                    for k in range(2):
                        x = X0 - 2 + k if dx < 0 else X0 + BX + k
                        y = Y0 - 2 if dy < 0 else Y0 + BY
                        buf[sh, x, y : y + 2] = CR[slot, n, sh * 4 + k * 2 : sh * 4 + k * 2 + 2]

    for n, first in ((0, 0), (1, PX - 4)):
        @pl.when(jnp.logical_not(has[n]))
        def _():
            blank = jnp.zeros((4, PY, BZ), F32)
            for buf in (E0, E1, O):
                for sh in range(SHOTS):
                    buf[sh, first : first + 4] = blank
            CO[first : first + 4] = blank

    for n, first in ((2, 0), (3, PY - 8)):
        @pl.when(jnp.logical_not(has[n]))
        def _():
            blank = jnp.zeros((8, BZ), F32)

            def one(x):
                for buf in (E0, E1, O):
                    for sh in range(SHOTS):
                        buf[sh, x, first : first + 8] = blank
                CO[x, first : first + 8] = blank

            loop(PX, one)

    rows = lax.broadcasted_iota(jnp.int32, (8, BZ), 0)
    lanes = lax.broadcasted_iota(jnp.int32, (8, BZ), 1)
    first_lane = (lanes > 0).astype(F32)
    second_lane = (lanes > 1).astype(F32)
    last_lane = (lanes < BZ - 1).astype(F32)
    last_two = (lanes < BZ - 2).astype(F32)

    def weight(cell, total):
        return jnp.maximum(16 - jnp.minimum(cell + 1, total - cell), 0).astype(F32) / 16.0

    def damping_tables(x):
        wx = weight(jnp.full((8, BZ), i * BX + x - X0, jnp.int32), AX)
        for q in range(5):
            at = pl.ds(Y0 - 4 + 8 * q, 8)
            wy = weight(rows + (j * BY - 4 + 8 * q), AY)
            d = 0.3 * (wx * wx + wy * wy)
            inv = 1.0 / (1.0 + d)
            INV[x, at] = inv
            K2[x, at] = (1.0 - d) * inv

    loop(X0 + BX + 2, damping_tables, X0 - 2)

    for sh in range(SHOTS):
        wx = weight(jnp.full((8, BZ), sources[0, sh, 0], jnp.int32), AX)
        for q in range(5):
            cells = rows + (j * BY - 4 + 8 * q)
            wy = weight(cells, AY)
            inv = 1.0 / (1.0 + 0.3 * (wx * wx + wy * wy))
            hit = (cells == sources[0, sh, 1]) & (lanes == sources[0, sh, 2])
            EY[sh, pl.ds(Y0 - 4 + 8 * q, 8)] = jnp.where(hit, inv, 0.0)

    rx = receivers[0] - i * BX
    ry = receivers[1] - j * BY
    here = (rx >= 0) & (rx < BX) & (ry >= 0) & (ry < BY)
    IDL[...] = jnp.where(here, rx * BY + ry, -1)
    deep = lax.broadcasted_iota(jnp.int32, (2 * BZ, RECS), 0) & (BZ - 1)
    OH[...] = jnp.where(deep == receivers[2], 1.0, 0.0).astype(jnp.bfloat16)

    for r in range(1, NS):
        off_copy(r).wait_send()
        shot = s ^ r
        send(OFS, OFR.at[shot], off_s.at[r], off_r.at[shot], (shot, i, j)).wait_recv()
    cp_now.wait()
    send_rows(E0, 0)
    send_sides(E0, 0)
    cp_prev.wait()
    pack(O, 2, PS)
    prev_ends = [pl.ds(X0, 2), pl.ds(X0 + BX - 2, 2)]
    prev_lands = [pl.ds(X0 + BX, 2), pl.ds(X0 - 2, 2)]
    prev_list = []
    for n, dx in ((0, -1), (1, 1)):
        prev_list.append((
            has[n], O.at[:, prev_ends[n], inner_y, :], O.at[:, prev_lands[n], inner_y, :],
            n, 1 - n, (s, i + dx, j),
        ))
    for n, dy in ((0, -1), (1, 1)):
        prev_list.append((has[2 + n], PS.at[n], PR.at[1 - n], 2 + n, 3 - n, (s, i, j + dy)))
    for ok, src, dst, n, m, dev in prev_list:
        @pl.when(ok)
        def _():
            send(src, dst, p_s.at[n], p_r.at[m], dev).start()

    cp_off = pltpu.make_async_copy(OFR, OFM, in_sem.at[0])
    cp_off.start()
    cp_off.wait()
    all_of(MT.at[pl.ds(0, GROUP - 1)], a_sem.at[0])
    all_of(R.at[pl.ds(0, GROUP - 1)], a_sem.at[1])

    send_corners(E0, 0)

    tail = me >= GROUP - 2
    head = me < 2
    shift = jnp.where(tail, -1, 1)
    firsts = [OFM[s ^ r, 0, 0] for r in range(NS)]
    columns = [firsts[r >> 2] + (i ^ (r & 3)) for r in range(GROUP)]
    for r in range(GROUP):
        plane = R[owner[columns[r]]]
        SEL[r] = plane
        EDGE[0, r] = plane[BY - 2 : BY]
        EDGE[1, r] = plane[0:2]
    halo_plane = jnp.where(tail, me - (GROUP - 2) + X0 - 2, X0 + BX + jnp.minimum(me, 1))
    halo_slot = jnp.where(tail, me - (GROUP - 2), 2 + jnp.minimum(me, 1))

    def bh_copy(r):
        return send(
            SELH.at[r], CO.at[halo_plane, inner_y, :], bh_s.at[r], bh_r.at[halo_slot], member(r)
        )

    def bh_ok(r):
        c = i ^ (r & 3)
        return (tail & (c > 0)) | (head & (c < NX - 1))

    for side, ok in ((0, has[3]), (1, has[2])):
        @pl.when(ok)
        def _():
            row = j + 1 if side == 0 else j - 1
            for r in range(GROUP):
                send(
                    EDGE.at[side, r], YM.at[side, me], e_sem.at[0, side], e_sem.at[1, side],
                    (s ^ (r >> 2), i ^ (r & 3), row),
                ).start()

    for r in ROW_ORDER:
        send(SEL.at[r], CO.at[X0 + me, inner_y, :], b_sem.at[0], b_sem.at[1], member(r)).start()

    @pl.when(tail | head)
    def _():
        for r in range(GROUP):
            SELH[r] = R[owner[jnp.clip(columns[r] + shift, 0, GROUP - 1)]]
        for r in range(1, GROUP):
            @pl.when(bh_ok(r))
            def _():
                bh_copy(r).start()

    CO[X0 + me, inner_y] = SEL[0]

    @pl.when(bh_ok(0))
    def _():
        CO[halo_plane, inner_y] = SELH[0]

    wait_some(E0, 0, range(2))
    wait_rest(E0, 0)
    for n in range(4):
        ok, src, dst, _, m, dev = prev_list[n]
        back = prev_list[[1, 0, 3, 2][n]]

        @pl.when(ok)
        def _():
            send(src, dst, p_s.at[n], p_r.at[m], dev).wait_send()
            send(back[1], back[2], p_s.at[n], p_r.at[n], dev).wait_recv()

    unpack(O, 2, PR)

    def advance(
        read, before, write, first, stride, blocks, wide, tiles, step, lift=(0, 0), beside=None,
        ahead=False,
    ):
        def planes(block):
            x_first = first + stride * block
            on = [
                [
                    jnp.where(
                        sources[0, sh, 0] == i * BX + x_first + k - X0, wavelet[0, sh, step], 0.0
                    )
                    for sh in range(SHOTS)
                ]
                for k in range(wide)
            ]
            for y in tiles:
                at = pl.ds(y, 8)
                line = [
                    {d: read[sh, x_first + d, at] for d in range(-2, wide + 2)} for sh in range(SHOTS)
                ]
                for k in range(wide):
                    x = x_first + k
                    if not ahead:
                        kc, ka, k2 = KC[x, at], KA[x, at], K2[x, at]
                    for sh in range(SHOTS):
                        c = line[sh][k]
                        a = (line[sh][k + 1] + line[sh][k - 1]) + (
                            read[sh, x, pl.ds(y + 1, 8)] + read[sh, x, pl.ds(y - 1, 8)]
                        )
                        b = (line[sh][k + 2] + line[sh][k - 2]) + (
                            read[sh, x, pl.ds(y + 2, 8)] + read[sh, x, pl.ds(y - 2, 8)]
                        )
                        a = a + (
                            pltpu.roll(c, 1, 1) * first_lane
                            + pltpu.roll(c, BZ - 1, 1) * last_lane
                        )
                        b = b + (
                            pltpu.roll(c, 2, 1) * second_lane
                            + pltpu.roll(c, BZ - 2, 1) * last_two
                        )
                        if ahead:
                            write[sh, x, at] = a - 0.0625 * b
                            continue
                        fresh = (kc * c - k2 * before[sh, x, at]) + ka * (a - 0.0625 * b)
                        fresh = fresh + EY[sh, at] * on[k][sh]
                        write[sh, x - lift[0], pl.ds(y - lift[1], 8)] = fresh
            if beside is not None:
                beside(block)

        loop(blocks, planes)

    wide_tiles = [Y0 - 4 + 8 * q for q in range(5)]
    own_tiles = [Y0 + 8 * q for q in range(4)]

    advance(E0, O, W, X0 - 2, 4, 5, 4, wide_tiles, 0, ahead=True)

    all_of(SEL.at[pl.ds(0, GROUP - 1)], b_sem.at[0])
    all_of(CO.at[pl.ds(0, GROUP - 1), inner_y, :], b_sem.at[1])

    @pl.when(tail | head)
    def _():
        for r in range(1, GROUP):
            @pl.when(bh_ok(r))
            def _():
                bh_copy(r).wait_send()

    for slot in range(4):
        source = GROUP - 2 + slot if slot < 2 else slot - 2
        plane = X0 - 2 + slot if slot < 2 else X0 + BX + slot - 2
        edge = has[0] if slot < 2 else has[1]

        @pl.when(edge & (me != source))
        def _():
            send(
                SELH.at[0], CO.at[plane, inner_y, :], bh_s.at[0], bh_r.at[slot],
                (source >> 2, source & 3, j),
            ).wait_recv()

    for side, to, back in ((0, has[3], has[2]), (1, has[2], has[3])):
        @pl.when(to)
        def _():
            all_of(EDGE.at[side], e_sem.at[0, side])

        @pl.when(back)
        def _():
            all_of(YM.at[side], e_sem.at[1, side])
            for x in range(BX):
                CO[X0 + x, pl.ds(Y0 - 2 if side == 0 else Y0 + BY, 2)] = YM[side, x]

    def first_step(x):
        on = [
            jnp.where(sources[0, sh, 0] == i * BX + x - X0, wavelet[0, sh, 0], 0.0)
            for sh in range(SHOTS)
        ]
        for y in wide_tiles:
            at = pl.ds(y, 8)
            speed = CO[x, at]
            inv = INV[x, at]
            scaled = speed * speed * inv
            kc = 2.0 * inv - 7.5 * scaled
            ka = (4.0 / 3.0) * scaled
            k2 = K2[x, at]
            KC[x, at] = kc
            KA[x, at] = ka
            for sh in range(SHOTS):
                fresh = (kc * E0[sh, x, at] - k2 * O[sh, x, at]) + ka * W[sh, x, at]
                O[sh, x, at] = fresh + EY[sh, at] * on[sh]

    loop(X0 + BX + 2, first_step, X0 - 2)

    ends = [wide_tiles[0], wide_tiles[4]]

    def outer_middle(even, step):
        advance(even, O, O, X0 + 2, 4, 3, 4, wide_tiles[1:4], step)

    def outer_sides(even, step):
        advance(even, O, O, X0 - 2, BX, 2, 4, wide_tiles[1:4], step)

    def outer_ends(even, step):
        advance(even, O, O, X0 - 2, 4, 5, 4, ends, step)

    row_ids = lax.broadcasted_iota(jnp.int32, (BX * BY, RECS), 0)

    def split(buf, block, corner):
        for sh in range(SHOTS):
            for k in range(4):
                x = 4 * block + k
                v = buf[sh, corner[0] + x, pl.ds(corner[1], BY)]
                high = v.astype(jnp.bfloat16)
                low = (v - high.astype(F32)).astype(jnp.bfloat16)
                at = pl.ds(pl.multiple_of((sh * BX + x) * BY, BY), BY)
                XB[at, 0:BZ] = high
                XB[at, BZ : 2 * BZ] = low

    def keep(pair, half, sh, got):
        row = 4 * half + 2 * sh
        TS[pair, row : row + 1] = got[:, 0:128]
        TS[pair, row + 1 : row + 2] = got[:, 128:256]

    def sample(buf, pair, half, corner=(X0, Y0)):
        loop(BX // 4, lambda block: split(buf, block, corner))
        for sh in range(SHOTS):
            picked = jnp.dot(
                XB[sh * BX * BY : (sh + 1) * BX * BY], OH[...], preferred_element_type=F32
            )
            got = jnp.sum(jnp.where(row_ids == IDL[...], picked, 0.0), axis=0, keepdims=True)
            keep(pair, half, sh, got)

    def sample_beside(buf):
        def some(block):
            split(buf, block, (X0, Y0))
            wanted = IDL[...] - 4 * BY * block
            for sh in range(SHOTS):
                at = pl.ds(pl.multiple_of((sh * BX + 4 * block) * BY, 4 * BY), 4 * BY)
                picked = jnp.dot(XB[at], OH[...], preferred_element_type=F32)
                hit = jnp.where(row_ids[: 4 * BY] == wanted, picked, 0.0)
                ACC[sh] += jnp.sum(hit.reshape(4 * BY // 8, 8, RECS), axis=0)

        return some

    def trace_gx(pair):
        for r in (2, 1, 3):
            send(
                TS.at[pair], TX.at[pair, i], x_sem.at[0, pair], x_sem.at[1, pair], (s, i ^ r, j)
            ).start()
        TX[pair, i] = TS[pair]

    def tree(parts):
        while len(parts) > 1:
            parts = [a + b for a, b in zip(parts[0::2], parts[1::2])]
        return parts[0]

    def trace_gy(pair):
        all_of(TX.at[pair, pl.ds(0, NX - 1)], x_sem.at[0, pair])
        all_of(TX.at[pair, pl.ds(0, NX - 1)], x_sem.at[1, pair])
        TG[pair] = tree([TX[pair, q] for q in range(NX)])
        for r in range(NY - 1, 0, -1):
            send(
                TG.at[pair], TY.at[pair, j], y_sem.at[0, pair], y_sem.at[1, pair], (s, i, j ^ r)
            ).start()
        TY[pair, j] = TG[pair]

    def put_traces(pair, total):
        for row in range(8):
            half, sh, part = row // 4, (row // 2) % 2, row % 2
            out_traces[sh, 2 * pair + half : 2 * pair + half + 1, 128 * part : 128 * part + 128] = (
                total[row : row + 1]
            )

    def trace_out(pair):
        all_of(TY.at[pair, pl.ds(0, NY - 1)], y_sem.at[0, pair])
        all_of(TY.at[pair, pl.ds(0, NY - 1)], y_sem.at[1, pair])
        put_traces(pair, tree([TY[pair, q] for q in range(NY)]))

    pairs = STEPS // 2
    for pair in range(pairs):
        even, later = ((E0, E1), (E1, E0))[pair % 2]
        slot = (pair + 1) % 2
        step = 2 * pair + 1
        if pair:
            outer_ends(even, step - 1)
        if pair < pairs - 1:
            advance(O, even, later, X0, 4, 4, 4, [own_tiles[0], own_tiles[3]], step)
            send_corners(later, slot)
            send_rows(later, slot)
            advance(O, even, later, X0, 12, 2, 4, own_tiles[1:3], step)
            send_sides(later, slot)
            advance(O, even, later, X0 + 4, 4, 2, 4, own_tiles[1:3], step)
            sample(O, pair, 0)
            sample(later, pair, 1)
            trace_gx(pair)
            if pair:
                trace_gy(pair - 1)
            outer_middle(later, step + 1)
            if pair > 1:
                trace_out(pair - 2)
            wait_some(later, slot, range(2))
            outer_sides(later, step + 1)
            wait_rest(later, slot)
        else:
            cp_last = pltpu.make_async_copy(
                O.at[:, inner_x, inner_y, :], out_prev.at[0], in_sem.at[2]
            )
            cp_last.start()
            final = out_now.at[0]
            ACC[...] = jnp.zeros_like(ACC)
            advance(
                O, even, final, X0, 4, 4, 4, own_tiles, step, (X0, Y0), sample_beside(O)
            )
            for sh in range(SHOTS):
                keep(pair, 0, sh, jnp.sum(ACC[sh], axis=0, keepdims=True))
            sample(final, pair, 1, (0, 0))
            for r in SHOT_ORDER:
                send(
                    TS.at[pair], TR.at[mine], t_sem.at[0], t_sem.at[1],
                    (s, i ^ (r >> 3), j ^ (r & 7)),
                ).start()
            TR[mine] = TS[pair]
            trace_gy(pair - 1)
            trace_out(pair - 2)
            cp_last.wait()
            trace_out(pair - 1)
            all_of(TR.at[pl.ds(0, PEERS - 1)], t_sem.at[0])
            all_of(TR.at[pl.ds(0, PEERS - 1)], t_sem.at[1])
            put_traces(pair, tree([TR[q] for q in range(PEERS)]))


def store(a, b, c, to_a, to_b, to_c, sem):
    copies = [
        pltpu.make_async_copy(x, y, sem.at[n])
        for n, (x, y) in enumerate(((a, to_a), (b, to_b), (c, to_c)))
    ]
    for copy in copies:
        copy.start()
    for copy in copies:
        copy.wait()


def window(tiles, owner, offset, now, prev, sources, wavelet, receivers):
    any_spec = pl.BlockSpec(memory_space=pl.ANY)
    smem = pl.BlockSpec(memory_space=pltpu.SMEM)
    vmem = pl.BlockSpec(memory_space=pltpu.VMEM)
    buf = pltpu.VMEM
    dma = pltpu.SemaphoreType.DMA
    padded = (PX, PY, BZ)
    out_now, out_prev, traces = pl.pallas_call(
        kernel,
        out_shape=(
            pltpu.VMEM(now.shape, F32),
            pltpu.VMEM(prev.shape, F32),
            pltpu.VMEM((SHOTS, STEPS, RECS), F32),
        ),
        in_specs=[any_spec, smem, smem, any_spec, any_spec, smem, smem, vmem],
        out_specs=(vmem, vmem, vmem),
        scratch_shapes=[
            buf((SHOTS,) + padded, F32),
            buf((SHOTS,) + padded, F32),
            buf((SHOTS,) + padded, F32),
            buf((BX, BY, BZ), F32),
            buf((GROUP, BY, BZ), F32),
            buf((GROUP, BY, BZ), F32),
            buf((GROUP, BY, BZ), F32),
            buf((2, GROUP, 2, BZ), F32),
            buf((2, GROUP, 2, BZ), F32),
            buf(padded, F32),
            buf(padded, F32),
            buf(padded, F32),
            buf(padded, F32),
            buf(padded, F32),
            buf((SHOTS, PY, BZ), F32),
            buf((2, SHOTS * BX, 4, BZ), F32),
            buf((2, 2, SHOTS * BX, 4, BZ), F32),
            buf((4, 8, BZ), F32),
            buf((2, 4, 8, BZ), F32),
            buf((2, SHOTS * BX, 2, BZ), F32),
            buf((2, SHOTS * BX, 2, BZ), F32),
            buf((1, BZ), jnp.int32),
            buf((NS, 1, BZ), jnp.int32),
            pltpu.SMEM((NS, 1, BZ), jnp.int32),
            buf((2 * BZ, RECS), jnp.bfloat16),
            buf((1, RECS), jnp.int32),
            buf((SHOTS * BX * BY, 2 * BZ), jnp.bfloat16),
            buf((SHOTS, 8, RECS), F32),
            buf((STEPS // 2, 8, 128), F32),
            buf((PEERS, 8, 128), F32),
            buf((STEPS // 2 - 1, NX, 8, 128), F32),
            buf((STEPS // 2 - 1, NY, 8, 128), F32),
            buf((STEPS // 2 - 1, 8, 128), F32),
            buf((SHOTS,) + padded, F32),
            dma((3,)), dma((NS,)), dma((NS,)), dma((2,)), dma((2,)),
            dma((GROUP,)), dma((4,)), dma((2, 2)),
            dma((2, 8)), dma((2, 8)), dma((4,)), dma((4,)), dma((2,)),
            dma((2, STEPS // 2 - 1)), dma((2, STEPS // 2 - 1)),
        ],
        compiler_params=pltpu.CompilerParams(collective_id=0, has_side_effects=True),
    )(tiles, owner, offset, now, prev, sources, wavelet, jnp.transpose(receivers, (2, 0, 1)))
    hbm = pl.BlockSpec(memory_space=pltpu.HBM)
    out_now, out_prev, traces = pl.pallas_call(
        store,
        out_shape=(
            jax.ShapeDtypeStruct(now.shape, F32),
            jax.ShapeDtypeStruct(prev.shape, F32),
            jax.ShapeDtypeStruct((SHOTS, STEPS, RECS), F32),
        ),
        in_specs=[any_spec] * 3,
        out_specs=(hbm, hbm, hbm),
        scratch_shapes=[dma((3,))],
    )(*[pltpu.with_memory_space_constraint(x, pltpu.VMEM) for x in (out_now, out_prev, traces)])
    return out_now, out_prev, jnp.transpose(traces, (0, 2, 1))[None]


def solution(mesh):
    return jax.shard_map(
        window,
        mesh=mesh,
        in_specs=(
            P(("shot", "gx"), "gy", None),
            P(),
            P("shot"),
            P("shot", None, "gx", "gy", None),
            P("shot", None, "gx", "gy", None),
            P("shot", None, None),
            P("shot", None, None),
            P("shot", None, None),
        ),
        out_specs=(
            P("shot", None, "gx", "gy", None),
            P("shot", None, "gx", "gy", None),
            P("shot", None, None, None),
        ),
        check_vma=False,
    )
```

```python
import jax
import jax.numpy as jnp
from jax import lax
from jax.experimental import pallas as pl
from jax.experimental.pallas import tpu as pltpu
from jax.sharding import PartitionSpec as P

STEPS = 8
SHOTS = 2
NS, NX, NY = 4, 4, 8
GROUP = NS * NX
PEERS = NX * NY
BX, BY, BZ = 16, 32, 128
AX, AY = NX * BX, NY * BY
RECS = 256
PX, PY = BX + 8, BY + 16
X0, Y0 = 4, 8
MESH = pl.DeviceIdType.MESH
MATMUL_SHOTS = (1,)
F32 = jnp.float32


RING = (0, 1, 2, 1)
ROW_ORDER = sorted(range(1, GROUP), key=lambda r: -RING[r & 3] - (r >> 3))
SHOT_ORDER = sorted(
    range(1, PEERS), key=lambda r: -RING[r >> 3] - RING[(r & 7) >> 1] - 2 * (r & 1)
)


def loop(n, body, start=0):
    lax.fori_loop(start, n, lambda k, c: (body(k), c)[1], 0)


def kernel(
    tiles, owner, offset, now, prev, sources, wavelet, receivers,
    out_now, out_prev, out_traces,
    E0, E1, O, MT, R, SEL, SELH, EDGE, YM, CO, KC, KA, K2, INV, EY,
    YS, YR, CS, CR, PS, PR, OFS, OFR, OFM, OH, IDL, XB, ACC, TS, TR, TX, TY, TG, W, BAND,
    in_sem, off_s, off_r, a_sem, b_sem, bh_s, bh_r, e_sem,
    h_s, h_r, p_s, p_r, t_sem, x_sem, y_sem,
):
    s = lax.axis_index("shot")
    i = lax.axis_index("gx")
    j = lax.axis_index("gy")
    me = s * NX + i
    mine = i * NY + j

    def member(r):
        return (s ^ (r >> 2), i ^ (r & 3), j)

    def all_of(ref, sem):
        pltpu.make_async_copy(ref, ref, sem).wait()

    def send(src, dst, ssem, rsem, dev):
        return pltpu.make_async_remote_copy(
            src_ref=src, dst_ref=dst, send_sem=ssem, recv_sem=rsem,
            device_id=dev, device_id_type=MESH,
        )

    inner_x = pl.ds(X0, BX)
    inner_y = pl.ds(Y0, BY)
    has = [i > 0, i < NX - 1, j > 0, j < NY - 1]

    cp_mt = pltpu.make_async_copy(tiles, MT, in_sem.at[0])
    cp_now = pltpu.make_async_copy(now.at[0], E0.at[:, inner_x, inner_y, :], in_sem.at[1])
    cp_prev = pltpu.make_async_copy(prev.at[0], O.at[:, inner_x, inner_y, :], in_sem.at[2])
    cp_mt.start()
    cp_now.start()
    cp_prev.start()

    barrier = pltpu.get_barrier_semaphore()

    def greet(dev):
        pl.semaphore_signal(barrier, inc=1, device_id=dev, device_id_type=MESH)

    for r in range(1, NY):
        greet((s, i, j ^ r))
    for r in range(1, GROUP):
        greet(member(r))
    pl.semaphore_wait(barrier, GROUP + NY - 2)

    OFS[...] = jnp.full((1, BZ), offset[0], jnp.int32)

    def off_copy(r):
        return send(OFS, OFR.at[s], off_s.at[r], off_r.at[s], (s ^ r, i, j))

    for r in range(1, NS):
        off_copy(r).start()
    OFR[s] = jnp.full((1, BZ), offset[0], jnp.int32)

    cp_mt.wait()
    for r in ROW_ORDER:
        send(MT.at[me ^ r], R.at[me], a_sem.at[0], a_sem.at[1], member(r)).start()
    R[me] = MT[me]

    def pack(buf, depth, store):
        for x in range(BX):
            for sh in range(SHOTS):
                store[0, sh * BX + x] = buf[sh, X0 + x, pl.ds(Y0, depth)]
                store[1, sh * BX + x] = buf[sh, X0 + x, pl.ds(Y0 + BY - depth, depth)]

    def unpack(buf, depth, store):
        for side, y in ((0, Y0 - depth), (1, Y0 + BY)):
            @pl.when(has[2 + side])
            def _():
                for x in range(BX):
                    for sh in range(SHOTS):
                        buf[sh, X0 + x, pl.ds(y, depth)] = store[side, sh * BX + x]

    corners = [(-1, -1), (-1, 1), (1, -1), (1, 1)]

    def halo_list(buf, slot):
        ends = [pl.ds(X0, 4), pl.ds(X0 + BX - 4, 4)]
        lands = [pl.ds(X0 + BX, 4), pl.ds(X0 - 4, 4)]
        found = []
        for n, dx in ((0, -1), (1, 1)):
            found.append((
                has[n], buf.at[:, ends[n], inner_y, :], buf.at[:, lands[n], inner_y, :],
                n, 1 - n, (s, i + dx, j),
            ))
        for n, dy in ((0, -1), (1, 1)):
            found.append((
                has[2 + n], YS.at[n], YR.at[slot, 1 - n], 2 + n, 3 - n, (s, i, j + dy),
            ))
        for n, (dx, dy) in enumerate(corners):
            ok = has[0 if dx < 0 else 1] & has[2 if dy < 0 else 3]
            found.append((
                ok, CS.at[n], CR.at[slot, 3 - n], 4 + n, 7 - n, (s, i + dx, j + dy),
            ))
        return found

    def start_some(copies, slot):
        for ok, src, dst, n, m, dev in copies:
            @pl.when(ok)
            def _():
                send(src, dst, h_s.at[slot, n], h_r.at[slot, m], dev).start()

    def send_sides(buf, slot):
        start_some(halo_list(buf, slot)[0:2], slot)

    def send_rows(buf, slot):
        pack(buf, 4, YS)
        start_some(halo_list(buf, slot)[2:4], slot)

    def send_corners(buf, slot):
        for n, (dx, dy) in enumerate(corners):
            for sh in range(SHOTS):
                for k in range(2):
                    x = X0 + k if dx < 0 else X0 + BX - 2 + k
                    y = Y0 if dy < 0 else Y0 + BY - 2
                    CS[n, sh * 4 + k * 2 : sh * 4 + k * 2 + 2] = buf[sh, x, y : y + 2]
        start_some(halo_list(buf, slot)[4:8], slot)

    def wait_some(buf, slot, which):
        copies = halo_list(buf, slot)
        opposite = [1, 0, 3, 2, 7, 6, 5, 4]
        for n in which:
            ok, src, dst, _, m, dev = copies[n]
            back = copies[opposite[n]]

            @pl.when(ok)
            def _():
                send(src, dst, h_s.at[slot, n], h_r.at[slot, m], dev).wait_send()
                send(back[1], back[2], h_s.at[slot, n], h_r.at[slot, n], dev).wait_recv()

    def wait_rest(buf, slot):
        copies = halo_list(buf, slot)
        wait_some(buf, slot, range(2, 8))
        unpack(buf, 4, YR.at[slot])
        for n, (dx, dy) in enumerate(corners):
            @pl.when(copies[4 + n][0])
            def _():
                for sh in range(SHOTS):
                    for k in range(2):
                        x = X0 - 2 + k if dx < 0 else X0 + BX + k
                        y = Y0 - 2 if dy < 0 else Y0 + BY
                        buf[sh, x, y : y + 2] = CR[slot, n, sh * 4 + k * 2 : sh * 4 + k * 2 + 2]

    for n, first in ((0, 0), (1, PX - 4)):
        @pl.when(jnp.logical_not(has[n]))
        def _():
            blank = jnp.zeros((4, PY, BZ), F32)
            for buf in (E0, E1, O):
                for sh in range(SHOTS):
                    buf[sh, first : first + 4] = blank
            CO[first : first + 4] = blank

    for n, first in ((2, 0), (3, PY - 8)):
        @pl.when(jnp.logical_not(has[n]))
        def _():
            blank = jnp.zeros((8, BZ), F32)

            def one(x):
                for buf in (E0, E1, O):
                    for sh in range(SHOTS):
                        buf[sh, x, first : first + 8] = blank
                CO[x, first : first + 8] = blank

            loop(PX, one)

    rows = lax.broadcasted_iota(jnp.int32, (8, BZ), 0)
    lanes = lax.broadcasted_iota(jnp.int32, (8, BZ), 1)
    first_lane = (lanes > 0).astype(F32)
    second_lane = (lanes > 1).astype(F32)
    last_lane = (lanes < BZ - 1).astype(F32)
    last_two = (lanes < BZ - 2).astype(F32)

    def weight(cell, total):
        return jnp.maximum(16 - jnp.minimum(cell + 1, total - cell), 0).astype(F32) / 16.0

    def damping_tables(x):
        wx = weight(jnp.full((8, BZ), i * BX + x - X0, jnp.int32), AX)
        for q in range(5):
            at = pl.ds(Y0 - 4 + 8 * q, 8)
            wy = weight(rows + (j * BY - 4 + 8 * q), AY)
            d = 0.3 * (wx * wx + wy * wy)
            inv = 1.0 / (1.0 + d)
            INV[x, at] = inv
            K2[x, at] = (1.0 - d) * inv

    loop(X0 + BX + 2, damping_tables, X0 - 2)

    for sh in range(SHOTS):
        wx = weight(jnp.full((8, BZ), sources[0, sh, 0], jnp.int32), AX)
        for q in range(5):
            cells = rows + (j * BY - 4 + 8 * q)
            wy = weight(cells, AY)
            inv = 1.0 / (1.0 + 0.3 * (wx * wx + wy * wy))
            hit = (cells == sources[0, sh, 1]) & (lanes == sources[0, sh, 2])
            EY[sh, pl.ds(Y0 - 4 + 8 * q, 8)] = jnp.where(hit, inv, 0.0)

    gap = jnp.abs(
        (lax.broadcasted_iota(jnp.int32, (2 * BZ, BZ), 0) & (BZ - 1))
        - lax.broadcasted_iota(jnp.int32, (2 * BZ, BZ), 1)
    )
    BAND[...] = jnp.where(gap == 1, 1.0, jnp.where(gap == 2, -0.0625, 0.0)).astype(jnp.bfloat16)

    rx = receivers[0] - i * BX
    ry = receivers[1] - j * BY
    here = (rx >= 0) & (rx < BX) & (ry >= 0) & (ry < BY)
    IDL[...] = jnp.where(here, rx * BY + ry, -1)
    deep = lax.broadcasted_iota(jnp.int32, (2 * BZ, RECS), 0) & (BZ - 1)
    OH[...] = jnp.where(deep == receivers[2], 1.0, 0.0).astype(jnp.bfloat16)

    for r in range(1, NS):
        off_copy(r).wait_send()
        shot = s ^ r
        send(OFS, OFR.at[shot], off_s.at[r], off_r.at[shot], (shot, i, j)).wait_recv()
    cp_now.wait()
    send_rows(E0, 0)
    send_sides(E0, 0)
    cp_prev.wait()
    pack(O, 2, PS)
    prev_ends = [pl.ds(X0, 2), pl.ds(X0 + BX - 2, 2)]
    prev_lands = [pl.ds(X0 + BX, 2), pl.ds(X0 - 2, 2)]
    prev_list = []
    for n, dx in ((0, -1), (1, 1)):
        prev_list.append((
            has[n], O.at[:, prev_ends[n], inner_y, :], O.at[:, prev_lands[n], inner_y, :],
            n, 1 - n, (s, i + dx, j),
        ))
    for n, dy in ((0, -1), (1, 1)):
        prev_list.append((has[2 + n], PS.at[n], PR.at[1 - n], 2 + n, 3 - n, (s, i, j + dy)))
    for ok, src, dst, n, m, dev in prev_list:
        @pl.when(ok)
        def _():
            send(src, dst, p_s.at[n], p_r.at[m], dev).start()

    cp_off = pltpu.make_async_copy(OFR, OFM, in_sem.at[0])
    cp_off.start()
    cp_off.wait()
    all_of(MT.at[pl.ds(0, GROUP - 1)], a_sem.at[0])
    all_of(R.at[pl.ds(0, GROUP - 1)], a_sem.at[1])

    send_corners(E0, 0)

    tail = me >= GROUP - 2
    head = me < 2
    shift = jnp.where(tail, -1, 1)
    firsts = [OFM[s ^ r, 0, 0] for r in range(NS)]
    columns = [firsts[r >> 2] + (i ^ (r & 3)) for r in range(GROUP)]
    for r in range(GROUP):
        plane = R[owner[columns[r]]]
        SEL[r] = plane
        EDGE[0, r] = plane[BY - 2 : BY]
        EDGE[1, r] = plane[0:2]
    halo_plane = jnp.where(tail, me - (GROUP - 2) + X0 - 2, X0 + BX + jnp.minimum(me, 1))
    halo_slot = jnp.where(tail, me - (GROUP - 2), 2 + jnp.minimum(me, 1))

    def bh_copy(r):
        return send(
            SELH.at[r], CO.at[halo_plane, inner_y, :], bh_s.at[r], bh_r.at[halo_slot], member(r)
        )

    def bh_ok(r):
        c = i ^ (r & 3)
        return (tail & (c > 0)) | (head & (c < NX - 1))

    for side, ok in ((0, has[3]), (1, has[2])):
        @pl.when(ok)
        def _():
            row = j + 1 if side == 0 else j - 1
            for r in range(GROUP):
                send(
                    EDGE.at[side, r], YM.at[side, me], e_sem.at[0, side], e_sem.at[1, side],
                    (s ^ (r >> 2), i ^ (r & 3), row),
                ).start()

    for r in ROW_ORDER:
        send(SEL.at[r], CO.at[X0 + me, inner_y, :], b_sem.at[0], b_sem.at[1], member(r)).start()

    @pl.when(tail | head)
    def _():
        for r in range(GROUP):
            SELH[r] = R[owner[jnp.clip(columns[r] + shift, 0, GROUP - 1)]]
        for r in range(1, GROUP):
            @pl.when(bh_ok(r))
            def _():
                bh_copy(r).start()

    CO[X0 + me, inner_y] = SEL[0]

    @pl.when(bh_ok(0))
    def _():
        CO[halo_plane, inner_y] = SELH[0]

    wait_some(E0, 0, range(2))
    wait_rest(E0, 0)
    for n in range(4):
        ok, src, dst, _, m, dev = prev_list[n]
        back = prev_list[[1, 0, 3, 2][n]]

        @pl.when(ok)
        def _():
            send(src, dst, p_s.at[n], p_r.at[m], dev).wait_send()
            send(back[1], back[2], p_s.at[n], p_r.at[n], dev).wait_recv()

    unpack(O, 2, PR)

    def advance(
        read, before, write, first, stride, blocks, wide, tiles, step, lift=(0, 0), beside=None,
        ahead=False,
    ):
        def planes(block):
            x_first = first + stride * block
            on = [
                [
                    jnp.where(
                        sources[0, sh, 0] == i * BX + x_first + k - X0, wavelet[0, sh, step], 0.0
                    )
                    for sh in range(SHOTS)
                ]
                for k in range(wide)
            ]
            lines = [
                [
                    {d: read[sh, x_first + d, pl.ds(y, 8)] for d in range(-2, wide + 2)}
                    for sh in range(SHOTS)
                ]
                for y in tiles
            ]
            deep = {}
            for sh in MATMUL_SHOTS:
                v = jnp.concatenate([ln[sh][k] for ln in lines for k in range(wide)], axis=0)
                high = v.astype(jnp.bfloat16)
                low = (v - high.astype(F32)).astype(jnp.bfloat16)
                deep[sh] = jnp.dot(
                    jnp.concatenate([high, low], axis=1), BAND[...], preferred_element_type=F32
                )
            for n, y in enumerate(tiles):
                at = pl.ds(y, 8)
                line = lines[n]
                for k in range(wide):
                    x = x_first + k
                    if not ahead:
                        kc, ka, k2 = KC[x, at], KA[x, at], K2[x, at]
                    for sh in range(SHOTS):
                        c = line[sh][k]
                        a = (line[sh][k + 1] + line[sh][k - 1]) + (
                            read[sh, x, pl.ds(y + 1, 8)] + read[sh, x, pl.ds(y - 1, 8)]
                        )
                        b = (line[sh][k + 2] + line[sh][k - 2]) + (
                            read[sh, x, pl.ds(y + 2, 8)] + read[sh, x, pl.ds(y - 2, 8)]
                        )
                        if sh in deep:
                            m = 8 * (n * wide + k)
                            near = (a - 0.0625 * b) + deep[sh][m : m + 8]
                        else:
                            a = a + (
                                pltpu.roll(c, 1, 1) * first_lane
                                + pltpu.roll(c, BZ - 1, 1) * last_lane
                            )
                            b = b + (
                                pltpu.roll(c, 2, 1) * second_lane
                                + pltpu.roll(c, BZ - 2, 1) * last_two
                            )
                            near = a - 0.0625 * b
                        if ahead:
                            write[sh, x, at] = near
                            continue
                        fresh = (kc * c - k2 * before[sh, x, at]) + ka * near
                        fresh = fresh + EY[sh, at] * on[k][sh]
                        write[sh, x - lift[0], pl.ds(y - lift[1], 8)] = fresh
            if beside is not None:
                beside(block)

        loop(blocks, planes)

    wide_tiles = [Y0 - 4 + 8 * q for q in range(5)]
    own_tiles = [Y0 + 8 * q for q in range(4)]

    advance(E0, O, W, X0 - 2, 4, 5, 4, wide_tiles, 0, ahead=True)

    all_of(SEL.at[pl.ds(0, GROUP - 1)], b_sem.at[0])
    all_of(CO.at[pl.ds(0, GROUP - 1), inner_y, :], b_sem.at[1])

    @pl.when(tail | head)
    def _():
        for r in range(1, GROUP):
            @pl.when(bh_ok(r))
            def _():
                bh_copy(r).wait_send()

    for slot in range(4):
        source = GROUP - 2 + slot if slot < 2 else slot - 2
        plane = X0 - 2 + slot if slot < 2 else X0 + BX + slot - 2
        edge = has[0] if slot < 2 else has[1]

        @pl.when(edge & (me != source))
        def _():
            send(
                SELH.at[0], CO.at[plane, inner_y, :], bh_s.at[0], bh_r.at[slot],
                (source >> 2, source & 3, j),
            ).wait_recv()

    for side, to, back in ((0, has[3], has[2]), (1, has[2], has[3])):
        @pl.when(to)
        def _():
            all_of(EDGE.at[side], e_sem.at[0, side])

        @pl.when(back)
        def _():
            all_of(YM.at[side], e_sem.at[1, side])
            for x in range(BX):
                CO[X0 + x, pl.ds(Y0 - 2 if side == 0 else Y0 + BY, 2)] = YM[side, x]

    def first_step(x):
        on = [
            jnp.where(sources[0, sh, 0] == i * BX + x - X0, wavelet[0, sh, 0], 0.0)
            for sh in range(SHOTS)
        ]
        for y in wide_tiles:
            at = pl.ds(y, 8)
            speed = CO[x, at]
            inv = INV[x, at]
            scaled = speed * speed * inv
            kc = 2.0 * inv - 7.5 * scaled
            ka = (4.0 / 3.0) * scaled
            k2 = K2[x, at]
            KC[x, at] = kc
            KA[x, at] = ka
            for sh in range(SHOTS):
                fresh = (kc * E0[sh, x, at] - k2 * O[sh, x, at]) + ka * W[sh, x, at]
                O[sh, x, at] = fresh + EY[sh, at] * on[sh]

    loop(X0 + BX + 2, first_step, X0 - 2)

    ends = [wide_tiles[0], wide_tiles[4]]

    def outer_middle(even, step):
        advance(even, O, O, X0 + 2, 4, 3, 4, wide_tiles[1:4], step)

    def outer_sides(even, step):
        advance(even, O, O, X0 - 2, BX, 2, 4, wide_tiles[1:4], step)

    def outer_ends(even, step):
        advance(even, O, O, X0 - 2, 20, 1, 20, ends, step)

    row_ids = lax.broadcasted_iota(jnp.int32, (BX * BY, RECS), 0)

    def split(buf, block, corner):
        for sh in range(SHOTS):
            for k in range(4):
                x = 4 * block + k
                v = buf[sh, corner[0] + x, pl.ds(corner[1], BY)]
                high = v.astype(jnp.bfloat16)
                low = (v - high.astype(F32)).astype(jnp.bfloat16)
                at = pl.ds(pl.multiple_of((sh * BX + x) * BY, BY), BY)
                XB[at, 0:BZ] = high
                XB[at, BZ : 2 * BZ] = low

    def keep(pair, half, sh, got):
        row = 4 * half + 2 * sh
        TS[pair, row : row + 1] = got[:, 0:128]
        TS[pair, row + 1 : row + 2] = got[:, 128:256]

    def sample(buf, pair, half, corner=(X0, Y0)):
        loop(BX // 4, lambda block: split(buf, block, corner))
        for sh in range(SHOTS):
            picked = jnp.dot(
                XB[sh * BX * BY : (sh + 1) * BX * BY], OH[...], preferred_element_type=F32
            )
            got = jnp.sum(jnp.where(row_ids == IDL[...], picked, 0.0), axis=0, keepdims=True)
            keep(pair, half, sh, got)

    def sample_beside(buf):
        def some(block):
            split(buf, block, (X0, Y0))
            wanted = IDL[...] - 4 * BY * block
            for sh in range(SHOTS):
                at = pl.ds(pl.multiple_of((sh * BX + 4 * block) * BY, 4 * BY), 4 * BY)
                picked = jnp.dot(XB[at], OH[...], preferred_element_type=F32)
                hit = jnp.where(row_ids[: 4 * BY] == wanted, picked, 0.0)
                ACC[sh] += jnp.sum(hit.reshape(4 * BY // 8, 8, RECS), axis=0)

        return some

    def trace_gx(pair):
        for r in (2, 1, 3):
            send(
                TS.at[pair], TX.at[pair, i], x_sem.at[0, pair], x_sem.at[1, pair], (s, i ^ r, j)
            ).start()
        TX[pair, i] = TS[pair]

    def tree(parts):
        while len(parts) > 1:
            parts = [a + b for a, b in zip(parts[0::2], parts[1::2])]
        return parts[0]

    def trace_gy(pair):
        all_of(TX.at[pair, pl.ds(0, NX - 1)], x_sem.at[0, pair])
        all_of(TX.at[pair, pl.ds(0, NX - 1)], x_sem.at[1, pair])
        TG[pair] = tree([TX[pair, q] for q in range(NX)])
        for r in range(NY - 1, 0, -1):
            send(
                TG.at[pair], TY.at[pair, j], y_sem.at[0, pair], y_sem.at[1, pair], (s, i, j ^ r)
            ).start()
        TY[pair, j] = TG[pair]

    def put_traces(pair, total):
        for row in range(8):
            half, sh, part = row // 4, (row // 2) % 2, row % 2
            out_traces[sh, 2 * pair + half : 2 * pair + half + 1, 128 * part : 128 * part + 128] = (
                total[row : row + 1]
            )

    def trace_out(pair):
        all_of(TY.at[pair, pl.ds(0, NY - 1)], y_sem.at[0, pair])
        all_of(TY.at[pair, pl.ds(0, NY - 1)], y_sem.at[1, pair])
        put_traces(pair, tree([TY[pair, q] for q in range(NY)]))

    pairs = STEPS // 2
    for pair in range(pairs):
        even, later = ((E0, E1), (E1, E0))[pair % 2]
        slot = (pair + 1) % 2
        step = 2 * pair + 1
        if pair:
            outer_ends(even, step - 1)
        if pair < pairs - 1:
            advance(O, even, later, X0, 16, 1, 16, [own_tiles[0], own_tiles[3]], step)
            send_corners(later, slot)
            send_rows(later, slot)
            advance(O, even, later, X0, 12, 2, 4, own_tiles[1:3], step)
            send_sides(later, slot)
            advance(O, even, later, X0 + 4, 4, 2, 4, own_tiles[1:3], step)
            sample(O, pair, 0)
            sample(later, pair, 1)
            trace_gx(pair)
            if pair:
                trace_gy(pair - 1)
            outer_middle(later, step + 1)
            if pair > 1:
                trace_out(pair - 2)
            wait_some(later, slot, range(2))
            outer_sides(later, step + 1)
            wait_rest(later, slot)
        else:
            cp_last = pltpu.make_async_copy(
                O.at[:, inner_x, inner_y, :], out_prev.at[0], in_sem.at[2]
            )
            cp_last.start()
            final = out_now.at[0]
            ACC[...] = jnp.zeros_like(ACC)
            advance(
                O, even, final, X0, 4, 4, 4, own_tiles, step, (X0, Y0), sample_beside(O)
            )
            for sh in range(SHOTS):
                keep(pair, 0, sh, jnp.sum(ACC[sh], axis=0, keepdims=True))
            sample(final, pair, 1, (0, 0))
            for r in SHOT_ORDER:
                send(
                    TS.at[pair], TR.at[mine], t_sem.at[0], t_sem.at[1],
                    (s, i ^ (r >> 3), j ^ (r & 7)),
                ).start()
            TR[mine] = TS[pair]
            trace_gy(pair - 1)
            trace_out(pair - 2)
            cp_last.wait()
            trace_out(pair - 1)
            all_of(TR.at[pl.ds(0, PEERS - 1)], t_sem.at[0])
            all_of(TR.at[pl.ds(0, PEERS - 1)], t_sem.at[1])
            put_traces(pair, tree([TR[q] for q in range(PEERS)]))


def store(a, b, c, to_a, to_b, to_c, sem):
    copies = [
        pltpu.make_async_copy(x, y, sem.at[n])
        for n, (x, y) in enumerate(((a, to_a), (b, to_b), (c, to_c)))
    ]
    for copy in copies:
        copy.start()
    for copy in copies:
        copy.wait()


def window(tiles, owner, offset, now, prev, sources, wavelet, receivers):
    any_spec = pl.BlockSpec(memory_space=pl.ANY)
    smem = pl.BlockSpec(memory_space=pltpu.SMEM)
    vmem = pl.BlockSpec(memory_space=pltpu.VMEM)
    buf = pltpu.VMEM
    dma = pltpu.SemaphoreType.DMA
    padded = (PX, PY, BZ)
    out_now, out_prev, traces = pl.pallas_call(
        kernel,
        out_shape=(
            pltpu.VMEM(now.shape, F32),
            pltpu.VMEM(prev.shape, F32),
            pltpu.VMEM((SHOTS, STEPS, RECS), F32),
        ),
        in_specs=[any_spec, smem, smem, any_spec, any_spec, smem, smem, vmem],
        out_specs=(vmem, vmem, vmem),
        scratch_shapes=[
            buf((SHOTS,) + padded, F32),
            buf((SHOTS,) + padded, F32),
            buf((SHOTS,) + padded, F32),
            buf((BX, BY, BZ), F32),
            buf((GROUP, BY, BZ), F32),
            buf((GROUP, BY, BZ), F32),
            buf((GROUP, BY, BZ), F32),
            buf((2, GROUP, 2, BZ), F32),
            buf((2, GROUP, 2, BZ), F32),
            buf(padded, F32),
            buf(padded, F32),
            buf(padded, F32),
            buf(padded, F32),
            buf(padded, F32),
            buf((SHOTS, PY, BZ), F32),
            buf((2, SHOTS * BX, 4, BZ), F32),
            buf((2, 2, SHOTS * BX, 4, BZ), F32),
            buf((4, 8, BZ), F32),
            buf((2, 4, 8, BZ), F32),
            buf((2, SHOTS * BX, 2, BZ), F32),
            buf((2, SHOTS * BX, 2, BZ), F32),
            buf((1, BZ), jnp.int32),
            buf((NS, 1, BZ), jnp.int32),
            pltpu.SMEM((NS, 1, BZ), jnp.int32),
            buf((2 * BZ, RECS), jnp.bfloat16),
            buf((1, RECS), jnp.int32),
            buf((SHOTS * BX * BY, 2 * BZ), jnp.bfloat16),
            buf((SHOTS, 8, RECS), F32),
            buf((STEPS // 2, 8, 128), F32),
            buf((PEERS, 8, 128), F32),
            buf((STEPS // 2 - 1, NX, 8, 128), F32),
            buf((STEPS // 2 - 1, NY, 8, 128), F32),
            buf((STEPS // 2 - 1, 8, 128), F32),
            buf((SHOTS,) + padded, F32),
            buf((2 * BZ, BZ), jnp.bfloat16),
            dma((3,)), dma((NS,)), dma((NS,)), dma((2,)), dma((2,)),
            dma((GROUP,)), dma((4,)), dma((2, 2)),
            dma((2, 8)), dma((2, 8)), dma((4,)), dma((4,)), dma((2,)),
            dma((2, STEPS // 2 - 1)), dma((2, STEPS // 2 - 1)),
        ],
        compiler_params=pltpu.CompilerParams(collective_id=0, has_side_effects=True),
    )(tiles, owner, offset, now, prev, sources, wavelet, jnp.transpose(receivers, (2, 0, 1)))
    hbm = pl.BlockSpec(memory_space=pltpu.HBM)
    out_now, out_prev, traces = pl.pallas_call(
        store,
        out_shape=(
            jax.ShapeDtypeStruct(now.shape, F32),
            jax.ShapeDtypeStruct(prev.shape, F32),
            jax.ShapeDtypeStruct((SHOTS, STEPS, RECS), F32),
        ),
        in_specs=[any_spec] * 3,
        out_specs=(hbm, hbm, hbm),
        scratch_shapes=[dma((3,))],
    )(*[pltpu.with_memory_space_constraint(x, pltpu.VMEM) for x in (out_now, out_prev, traces)])
    return out_now, out_prev, jnp.transpose(traces, (0, 2, 1))[None]


def solution(mesh):
    return jax.shard_map(
        window,
        mesh=mesh,
        in_specs=(
            P(("shot", "gx"), "gy", None),
            P(),
            P("shot"),
            P("shot", None, "gx", "gy", None),
            P("shot", None, "gx", "gy", None),
            P("shot", None, None),
            P("shot", None, None),
            P("shot", None, None),
        ),
        out_specs=(
            P("shot", None, "gx", "gy", None),
            P("shot", None, "gx", "gy", None),
            P("shot", None, None, None),
        ),
        check_vma=False,
    )
```

```python
import jax
import jax.numpy as jnp
from jax import lax
from jax.experimental import pallas as pl
from jax.experimental.pallas import tpu as pltpu
from jax.sharding import PartitionSpec as P

STEPS = 8
SHOTS = 2
NS, NX, NY = 4, 4, 8
GROUP = NS * NX
PEERS = NX * NY
BX, BY, BZ = 16, 32, 128
AX, AY = NX * BX, NY * BY
RECS = 256
PX, PY = BX + 8, BY + 16
X0, Y0 = 4, 8
MESH = pl.DeviceIdType.MESH
MATMUL_SHOTS = (0, 1)
F32 = jnp.float32


RING = (0, 1, 2, 1)
ROW_ORDER = sorted(range(1, GROUP), key=lambda r: -RING[r & 3] - (r >> 3))
SHOT_ORDER = sorted(
    range(1, PEERS), key=lambda r: -RING[r >> 3] - RING[(r & 7) >> 1] - 2 * (r & 1)
)


def loop(n, body, start=0):
    lax.fori_loop(start, n, lambda k, c: (body(k), c)[1], 0)


def kernel(
    tiles, owner, offset, now, prev, sources, wavelet, receivers,
    out_now, out_prev, out_traces,
    E0, E1, O, MT, R, SEL, SELH, EDGE, YM, CO, KC, KA, K2, INV, EY,
    YS, YR, CS, CR, PS, PR, OFS, OFR, OFM, OH, IDL, XB, ACC, TS, TR, TX, TY, TG, W, BAND,
    in_sem, off_s, off_r, a_sem, b_sem, bh_s, bh_r, e_sem,
    h_s, h_r, p_s, p_r, t_sem, x_sem, y_sem,
):
    s = lax.axis_index("shot")
    i = lax.axis_index("gx")
    j = lax.axis_index("gy")
    me = s * NX + i
    mine = i * NY + j

    def member(r):
        return (s ^ (r >> 2), i ^ (r & 3), j)

    def all_of(ref, sem):
        pltpu.make_async_copy(ref, ref, sem).wait()

    def send(src, dst, ssem, rsem, dev):
        return pltpu.make_async_remote_copy(
            src_ref=src, dst_ref=dst, send_sem=ssem, recv_sem=rsem,
            device_id=dev, device_id_type=MESH,
        )

    inner_x = pl.ds(X0, BX)
    inner_y = pl.ds(Y0, BY)
    has = [i > 0, i < NX - 1, j > 0, j < NY - 1]

    cp_mt = pltpu.make_async_copy(tiles, MT, in_sem.at[0])
    cp_now = pltpu.make_async_copy(now.at[0], E0.at[:, inner_x, inner_y, :], in_sem.at[1])
    cp_prev = pltpu.make_async_copy(prev.at[0], O.at[:, inner_x, inner_y, :], in_sem.at[2])
    cp_mt.start()
    cp_now.start()
    cp_prev.start()

    barrier = pltpu.get_barrier_semaphore()

    def greet(dev):
        pl.semaphore_signal(barrier, inc=1, device_id=dev, device_id_type=MESH)

    for r in range(1, NY):
        greet((s, i, j ^ r))
    for r in range(1, GROUP):
        greet(member(r))
    pl.semaphore_wait(barrier, GROUP + NY - 2)

    OFS[...] = jnp.full((1, BZ), offset[0], jnp.int32)

    def off_copy(r):
        return send(OFS, OFR.at[s], off_s.at[r], off_r.at[s], (s ^ r, i, j))

    for r in range(1, NS):
        off_copy(r).start()
    OFR[s] = jnp.full((1, BZ), offset[0], jnp.int32)

    cp_mt.wait()
    for r in ROW_ORDER:
        send(MT.at[me ^ r], R.at[me], a_sem.at[0], a_sem.at[1], member(r)).start()
    R[me] = MT[me]

    def pack(buf, depth, store):
        for x in range(BX):
            for sh in range(SHOTS):
                store[0, sh * BX + x] = buf[sh, X0 + x, pl.ds(Y0, depth)]
                store[1, sh * BX + x] = buf[sh, X0 + x, pl.ds(Y0 + BY - depth, depth)]

    def unpack(buf, depth, store):
        for side, y in ((0, Y0 - depth), (1, Y0 + BY)):
            @pl.when(has[2 + side])
            def _():
                for x in range(BX):
                    for sh in range(SHOTS):
                        buf[sh, X0 + x, pl.ds(y, depth)] = store[side, sh * BX + x]

    corners = [(-1, -1), (-1, 1), (1, -1), (1, 1)]

    def halo_list(buf, slot):
        ends = [pl.ds(X0, 4), pl.ds(X0 + BX - 4, 4)]
        lands = [pl.ds(X0 + BX, 4), pl.ds(X0 - 4, 4)]
        found = []
        for n, dx in ((0, -1), (1, 1)):
            found.append((
                has[n], buf.at[:, ends[n], inner_y, :], buf.at[:, lands[n], inner_y, :],
                n, 1 - n, (s, i + dx, j),
            ))
        for n, dy in ((0, -1), (1, 1)):
            found.append((
                has[2 + n], YS.at[n], YR.at[slot, 1 - n], 2 + n, 3 - n, (s, i, j + dy),
            ))
        for n, (dx, dy) in enumerate(corners):
            ok = has[0 if dx < 0 else 1] & has[2 if dy < 0 else 3]
            found.append((
                ok, CS.at[n], CR.at[slot, 3 - n], 4 + n, 7 - n, (s, i + dx, j + dy),
            ))
        return found

    def start_some(copies, slot):
        for ok, src, dst, n, m, dev in copies:
            @pl.when(ok)
            def _():
                send(src, dst, h_s.at[slot, n], h_r.at[slot, m], dev).start()

    def send_sides(buf, slot):
        start_some(halo_list(buf, slot)[0:2], slot)

    def send_rows(buf, slot):
        pack(buf, 4, YS)
        start_some(halo_list(buf, slot)[2:4], slot)

    def send_corners(buf, slot):
        for n, (dx, dy) in enumerate(corners):
            for sh in range(SHOTS):
                for k in range(2):
                    x = X0 + k if dx < 0 else X0 + BX - 2 + k
                    y = Y0 if dy < 0 else Y0 + BY - 2
                    CS[n, sh * 4 + k * 2 : sh * 4 + k * 2 + 2] = buf[sh, x, y : y + 2]
        start_some(halo_list(buf, slot)[4:8], slot)

    def wait_some(buf, slot, which):
        copies = halo_list(buf, slot)
        opposite = [1, 0, 3, 2, 7, 6, 5, 4]
        for n in which:
            ok, src, dst, _, m, dev = copies[n]
            back = copies[opposite[n]]

            @pl.when(ok)
            def _():
                send(src, dst, h_s.at[slot, n], h_r.at[slot, m], dev).wait_send()
                send(back[1], back[2], h_s.at[slot, n], h_r.at[slot, n], dev).wait_recv()

    def wait_rest(buf, slot):
        copies = halo_list(buf, slot)
        wait_some(buf, slot, range(2, 8))
        unpack(buf, 4, YR.at[slot])
        for n, (dx, dy) in enumerate(corners):
            @pl.when(copies[4 + n][0])
            def _():
                for sh in range(SHOTS):
                    for k in range(2):
                        x = X0 - 2 + k if dx < 0 else X0 + BX + k
                        y = Y0 - 2 if dy < 0 else Y0 + BY
                        buf[sh, x, y : y + 2] = CR[slot, n, sh * 4 + k * 2 : sh * 4 + k * 2 + 2]

    for n, first in ((0, 0), (1, PX - 4)):
        @pl.when(jnp.logical_not(has[n]))
        def _():
            blank = jnp.zeros((4, PY, BZ), F32)
            for buf in (E0, E1, O):
                for sh in range(SHOTS):
                    buf[sh, first : first + 4] = blank
            CO[first : first + 4] = blank

    for n, first in ((2, 0), (3, PY - 8)):
        @pl.when(jnp.logical_not(has[n]))
        def _():
            blank = jnp.zeros((8, BZ), F32)

            def one(x):
                for buf in (E0, E1, O):
                    for sh in range(SHOTS):
                        buf[sh, x, first : first + 8] = blank
                CO[x, first : first + 8] = blank

            loop(PX, one)

    rows = lax.broadcasted_iota(jnp.int32, (8, BZ), 0)
    lanes = lax.broadcasted_iota(jnp.int32, (8, BZ), 1)
    first_lane = (lanes > 0).astype(F32)
    second_lane = (lanes > 1).astype(F32)
    last_lane = (lanes < BZ - 1).astype(F32)
    last_two = (lanes < BZ - 2).astype(F32)

    def weight(cell, total):
        return jnp.maximum(16 - jnp.minimum(cell + 1, total - cell), 0).astype(F32) / 16.0

    def damping_tables(x):
        wx = weight(jnp.full((8, BZ), i * BX + x - X0, jnp.int32), AX)
        for q in range(5):
            at = pl.ds(Y0 - 4 + 8 * q, 8)
            wy = weight(rows + (j * BY - 4 + 8 * q), AY)
            d = 0.3 * (wx * wx + wy * wy)
            inv = 1.0 / (1.0 + d)
            INV[x, at] = inv
            K2[x, at] = (1.0 - d) * inv

    loop(X0 + BX + 2, damping_tables, X0 - 2)

    for sh in range(SHOTS):
        wx = weight(jnp.full((8, BZ), sources[0, sh, 0], jnp.int32), AX)
        for q in range(5):
            cells = rows + (j * BY - 4 + 8 * q)
            wy = weight(cells, AY)
            inv = 1.0 / (1.0 + 0.3 * (wx * wx + wy * wy))
            hit = (cells == sources[0, sh, 1]) & (lanes == sources[0, sh, 2])
            EY[sh, pl.ds(Y0 - 4 + 8 * q, 8)] = jnp.where(hit, inv, 0.0)

    gap = jnp.abs(
        (lax.broadcasted_iota(jnp.int32, (2 * BZ, BZ), 0) & (BZ - 1))
        - lax.broadcasted_iota(jnp.int32, (2 * BZ, BZ), 1)
    )
    BAND[...] = jnp.where(gap == 1, 1.0, jnp.where(gap == 2, -0.0625, 0.0)).astype(jnp.bfloat16)

    rx = receivers[0] - i * BX
    ry = receivers[1] - j * BY
    here = (rx >= 0) & (rx < BX) & (ry >= 0) & (ry < BY)
    IDL[...] = jnp.where(here, rx * BY + ry, -1)
    deep = lax.broadcasted_iota(jnp.int32, (2 * BZ, RECS), 0) & (BZ - 1)
    OH[...] = jnp.where(deep == receivers[2], 1.0, 0.0).astype(jnp.bfloat16)

    for r in range(1, NS):
        off_copy(r).wait_send()
        shot = s ^ r
        send(OFS, OFR.at[shot], off_s.at[r], off_r.at[shot], (shot, i, j)).wait_recv()
    cp_now.wait()
    send_rows(E0, 0)
    send_sides(E0, 0)
    cp_prev.wait()
    pack(O, 2, PS)
    prev_ends = [pl.ds(X0, 2), pl.ds(X0 + BX - 2, 2)]
    prev_lands = [pl.ds(X0 + BX, 2), pl.ds(X0 - 2, 2)]
    prev_list = []
    for n, dx in ((0, -1), (1, 1)):
        prev_list.append((
            has[n], O.at[:, prev_ends[n], inner_y, :], O.at[:, prev_lands[n], inner_y, :],
            n, 1 - n, (s, i + dx, j),
        ))
    for n, dy in ((0, -1), (1, 1)):
        prev_list.append((has[2 + n], PS.at[n], PR.at[1 - n], 2 + n, 3 - n, (s, i, j + dy)))
    for ok, src, dst, n, m, dev in prev_list:
        @pl.when(ok)
        def _():
            send(src, dst, p_s.at[n], p_r.at[m], dev).start()

    cp_off = pltpu.make_async_copy(OFR, OFM, in_sem.at[0])
    cp_off.start()
    cp_off.wait()
    all_of(MT.at[pl.ds(0, GROUP - 1)], a_sem.at[0])
    all_of(R.at[pl.ds(0, GROUP - 1)], a_sem.at[1])

    send_corners(E0, 0)

    tail = me >= GROUP - 2
    head = me < 2
    shift = jnp.where(tail, -1, 1)
    firsts = [OFM[s ^ r, 0, 0] for r in range(NS)]
    columns = [firsts[r >> 2] + (i ^ (r & 3)) for r in range(GROUP)]
    for r in range(GROUP):
        plane = R[owner[columns[r]]]
        SEL[r] = plane
        EDGE[0, r] = plane[BY - 2 : BY]
        EDGE[1, r] = plane[0:2]
    halo_plane = jnp.where(tail, me - (GROUP - 2) + X0 - 2, X0 + BX + jnp.minimum(me, 1))
    halo_slot = jnp.where(tail, me - (GROUP - 2), 2 + jnp.minimum(me, 1))

    def bh_copy(r):
        return send(
            SELH.at[r], CO.at[halo_plane, inner_y, :], bh_s.at[r], bh_r.at[halo_slot], member(r)
        )

    def bh_ok(r):
        c = i ^ (r & 3)
        return (tail & (c > 0)) | (head & (c < NX - 1))

    for side, ok in ((0, has[3]), (1, has[2])):
        @pl.when(ok)
        def _():
            row = j + 1 if side == 0 else j - 1
            for r in range(GROUP):
                send(
                    EDGE.at[side, r], YM.at[side, me], e_sem.at[0, side], e_sem.at[1, side],
                    (s ^ (r >> 2), i ^ (r & 3), row),
                ).start()

    for r in ROW_ORDER:
        send(SEL.at[r], CO.at[X0 + me, inner_y, :], b_sem.at[0], b_sem.at[1], member(r)).start()

    @pl.when(tail | head)
    def _():
        for r in range(GROUP):
            SELH[r] = R[owner[jnp.clip(columns[r] + shift, 0, GROUP - 1)]]
        for r in range(1, GROUP):
            @pl.when(bh_ok(r))
            def _():
                bh_copy(r).start()

    CO[X0 + me, inner_y] = SEL[0]

    @pl.when(bh_ok(0))
    def _():
        CO[halo_plane, inner_y] = SELH[0]

    wait_some(E0, 0, range(2))
    wait_rest(E0, 0)
    for n in range(4):
        ok, src, dst, _, m, dev = prev_list[n]
        back = prev_list[[1, 0, 3, 2][n]]

        @pl.when(ok)
        def _():
            send(src, dst, p_s.at[n], p_r.at[m], dev).wait_send()
            send(back[1], back[2], p_s.at[n], p_r.at[n], dev).wait_recv()

    unpack(O, 2, PR)

    def advance(
        read, before, write, first, stride, blocks, wide, tiles, step, lift=(0, 0), beside=None,
        ahead=False,
    ):
        def planes(block):
            x_first = first + stride * block
            on = [
                [
                    jnp.where(
                        sources[0, sh, 0] == i * BX + x_first + k - X0, wavelet[0, sh, step], 0.0
                    )
                    for sh in range(SHOTS)
                ]
                for k in range(wide)
            ]
            lines = [
                [
                    {d: read[sh, x_first + d, pl.ds(y, 8)] for d in range(-2, wide + 2)}
                    for sh in range(SHOTS)
                ]
                for y in tiles
            ]
            deep = {}
            for sh in MATMUL_SHOTS:
                v = jnp.concatenate([ln[sh][k] for ln in lines for k in range(wide)], axis=0)
                high = v.astype(jnp.bfloat16)
                low = (v - high.astype(F32)).astype(jnp.bfloat16)
                deep[sh] = jnp.dot(
                    jnp.concatenate([high, low], axis=1), BAND[...], preferred_element_type=F32
                )
            for n, y in enumerate(tiles):
                at = pl.ds(y, 8)
                line = lines[n]
                for k in range(wide):
                    x = x_first + k
                    if not ahead:
                        kc, ka, k2 = KC[x, at], KA[x, at], K2[x, at]
                    for sh in range(SHOTS):
                        c = line[sh][k]
                        a = (line[sh][k + 1] + line[sh][k - 1]) + (
                            read[sh, x, pl.ds(y + 1, 8)] + read[sh, x, pl.ds(y - 1, 8)]
                        )
                        b = (line[sh][k + 2] + line[sh][k - 2]) + (
                            read[sh, x, pl.ds(y + 2, 8)] + read[sh, x, pl.ds(y - 2, 8)]
                        )
                        if sh in deep:
                            m = 8 * (n * wide + k)
                            near = (a - 0.0625 * b) + deep[sh][m : m + 8]
                        else:
                            a = a + (
                                pltpu.roll(c, 1, 1) * first_lane
                                + pltpu.roll(c, BZ - 1, 1) * last_lane
                            )
                            b = b + (
                                pltpu.roll(c, 2, 1) * second_lane
                                + pltpu.roll(c, BZ - 2, 1) * last_two
                            )
                            near = a - 0.0625 * b
                        if ahead:
                            write[sh, x, at] = near
                            continue
                        fresh = (kc * c - k2 * before[sh, x, at]) + ka * near
                        fresh = fresh + EY[sh, at] * on[k][sh]
                        write[sh, x - lift[0], pl.ds(y - lift[1], 8)] = fresh
            if beside is not None:
                beside(block)

        loop(blocks, planes)

    wide_tiles = [Y0 - 4 + 8 * q for q in range(5)]
    own_tiles = [Y0 + 8 * q for q in range(4)]

    advance(E0, O, W, X0 - 2, 10, 2, 10, wide_tiles, 0, ahead=True)

    all_of(SEL.at[pl.ds(0, GROUP - 1)], b_sem.at[0])
    all_of(CO.at[pl.ds(0, GROUP - 1), inner_y, :], b_sem.at[1])

    @pl.when(tail | head)
    def _():
        for r in range(1, GROUP):
            @pl.when(bh_ok(r))
            def _():
                bh_copy(r).wait_send()

    for slot in range(4):
        source = GROUP - 2 + slot if slot < 2 else slot - 2
        plane = X0 - 2 + slot if slot < 2 else X0 + BX + slot - 2
        edge = has[0] if slot < 2 else has[1]

        @pl.when(edge & (me != source))
        def _():
            send(
                SELH.at[0], CO.at[plane, inner_y, :], bh_s.at[0], bh_r.at[slot],
                (source >> 2, source & 3, j),
            ).wait_recv()

    for side, to, back in ((0, has[3], has[2]), (1, has[2], has[3])):
        @pl.when(to)
        def _():
            all_of(EDGE.at[side], e_sem.at[0, side])

        @pl.when(back)
        def _():
            all_of(YM.at[side], e_sem.at[1, side])
            for x in range(BX):
                CO[X0 + x, pl.ds(Y0 - 2 if side == 0 else Y0 + BY, 2)] = YM[side, x]

    def first_step(x):
        on = [
            jnp.where(sources[0, sh, 0] == i * BX + x - X0, wavelet[0, sh, 0], 0.0)
            for sh in range(SHOTS)
        ]
        for y in wide_tiles:
            at = pl.ds(y, 8)
            speed = CO[x, at]
            inv = INV[x, at]
            scaled = speed * speed * inv
            kc = 2.0 * inv - 7.5 * scaled
            ka = (4.0 / 3.0) * scaled
            k2 = K2[x, at]
            KC[x, at] = kc
            KA[x, at] = ka
            for sh in range(SHOTS):
                fresh = (kc * E0[sh, x, at] - k2 * O[sh, x, at]) + ka * W[sh, x, at]
                O[sh, x, at] = fresh + EY[sh, at] * on[sh]

    loop(X0 + BX + 2, first_step, X0 - 2)

    ends = [wide_tiles[0], wide_tiles[4]]

    def outer_middle(even, step):
        advance(even, O, O, X0 + 2, 4, 3, 4, wide_tiles[1:4], step)

    def outer_sides(even, step):
        advance(even, O, O, X0 - 2, BX, 2, 4, wide_tiles[1:4], step)

    def outer_ends(even, step):
        advance(even, O, O, X0 - 2, 20, 1, 20, ends, step)

    row_ids = lax.broadcasted_iota(jnp.int32, (BX * BY, RECS), 0)

    def split(buf, block, corner):
        for sh in range(SHOTS):
            for k in range(4):
                x = 4 * block + k
                v = buf[sh, corner[0] + x, pl.ds(corner[1], BY)]
                high = v.astype(jnp.bfloat16)
                low = (v - high.astype(F32)).astype(jnp.bfloat16)
                at = pl.ds(pl.multiple_of((sh * BX + x) * BY, BY), BY)
                XB[at, 0:BZ] = high
                XB[at, BZ : 2 * BZ] = low

    def keep(pair, half, sh, got):
        row = 4 * half + 2 * sh
        TS[pair, row : row + 1] = got[:, 0:128]
        TS[pair, row + 1 : row + 2] = got[:, 128:256]

    def sample(buf, pair, half, corner=(X0, Y0)):
        loop(BX // 4, lambda block: split(buf, block, corner))
        for sh in range(SHOTS):
            picked = jnp.dot(
                XB[sh * BX * BY : (sh + 1) * BX * BY], OH[...], preferred_element_type=F32
            )
            got = jnp.sum(jnp.where(row_ids == IDL[...], picked, 0.0), axis=0, keepdims=True)
            keep(pair, half, sh, got)

    def sample_beside(buf):
        def four(block):
            split(buf, block, (X0, Y0))
            wanted = IDL[...] - 4 * BY * block
            for sh in range(SHOTS):
                at = pl.ds(pl.multiple_of((sh * BX + 4 * block) * BY, 4 * BY), 4 * BY)
                picked = jnp.dot(XB[at], OH[...], preferred_element_type=F32)
                hit = jnp.where(row_ids[: 4 * BY] == wanted, picked, 0.0)
                ACC[sh] += jnp.sum(hit.reshape(4 * BY // 8, 8, RECS), axis=0)

        def some(block):
            four(2 * block)
            four(2 * block + 1)

        return some

    def trace_gx(pair):
        for r in (2, 1, 3):
            send(
                TS.at[pair], TX.at[pair, i], x_sem.at[0, pair], x_sem.at[1, pair], (s, i ^ r, j)
            ).start()
        TX[pair, i] = TS[pair]

    def tree(parts):
        while len(parts) > 1:
            parts = [a + b for a, b in zip(parts[0::2], parts[1::2])]
        return parts[0]

    def trace_gy(pair):
        all_of(TX.at[pair, pl.ds(0, NX - 1)], x_sem.at[0, pair])
        all_of(TX.at[pair, pl.ds(0, NX - 1)], x_sem.at[1, pair])
        TG[pair] = tree([TX[pair, q] for q in range(NX)])
        for r in range(NY - 1, 0, -1):
            send(
                TG.at[pair], TY.at[pair, j], y_sem.at[0, pair], y_sem.at[1, pair], (s, i, j ^ r)
            ).start()
        TY[pair, j] = TG[pair]

    def put_traces(pair, total):
        for row in range(8):
            half, sh, part = row // 4, (row // 2) % 2, row % 2
            out_traces[sh, 2 * pair + half : 2 * pair + half + 1, 128 * part : 128 * part + 128] = (
                total[row : row + 1]
            )

    def trace_out(pair):
        all_of(TY.at[pair, pl.ds(0, NY - 1)], y_sem.at[0, pair])
        all_of(TY.at[pair, pl.ds(0, NY - 1)], y_sem.at[1, pair])
        put_traces(pair, tree([TY[pair, q] for q in range(NY)]))

    pairs = STEPS // 2
    for pair in range(pairs):
        even, later = ((E0, E1), (E1, E0))[pair % 2]
        slot = (pair + 1) % 2
        step = 2 * pair + 1
        if pair:
            outer_ends(even, step - 1)
        if pair < pairs - 1:
            advance(O, even, later, X0, 16, 1, 16, [own_tiles[0], own_tiles[3]], step)
            send_corners(later, slot)
            send_rows(later, slot)
            advance(O, even, later, X0, 12, 2, 4, own_tiles[1:3], step)
            send_sides(later, slot)
            advance(O, even, later, X0 + 4, 4, 2, 4, own_tiles[1:3], step)
            sample(O, pair, 0)
            sample(later, pair, 1)
            trace_gx(pair)
            if pair:
                trace_gy(pair - 1)
            outer_middle(later, step + 1)
            if pair > 1:
                trace_out(pair - 2)
            wait_some(later, slot, range(2))
            outer_sides(later, step + 1)
            wait_rest(later, slot)
        else:
            cp_last = pltpu.make_async_copy(
                O.at[:, inner_x, inner_y, :], out_prev.at[0], in_sem.at[2]
            )
            cp_last.start()
            final = out_now.at[0]
            ACC[...] = jnp.zeros_like(ACC)
            advance(
                O, even, final, X0, 8, 2, 8, own_tiles, step, (X0, Y0), sample_beside(O)
            )
            for sh in range(SHOTS):
                keep(pair, 0, sh, jnp.sum(ACC[sh], axis=0, keepdims=True))
            sample(final, pair, 1, (0, 0))
            for r in SHOT_ORDER:
                send(
                    TS.at[pair], TR.at[mine], t_sem.at[0], t_sem.at[1],
                    (s, i ^ (r >> 3), j ^ (r & 7)),
                ).start()
            TR[mine] = TS[pair]
            trace_gy(pair - 1)
            trace_out(pair - 2)
            cp_last.wait()
            trace_out(pair - 1)
            all_of(TR.at[pl.ds(0, PEERS - 1)], t_sem.at[0])
            all_of(TR.at[pl.ds(0, PEERS - 1)], t_sem.at[1])
            put_traces(pair, tree([TR[q] for q in range(PEERS)]))


def store(a, b, c, to_a, to_b, to_c, sem):
    copies = [
        pltpu.make_async_copy(x, y, sem.at[n])
        for n, (x, y) in enumerate(((a, to_a), (b, to_b), (c, to_c)))
    ]
    for copy in copies:
        copy.start()
    for copy in copies:
        copy.wait()


def window(tiles, owner, offset, now, prev, sources, wavelet, receivers):
    any_spec = pl.BlockSpec(memory_space=pl.ANY)
    smem = pl.BlockSpec(memory_space=pltpu.SMEM)
    vmem = pl.BlockSpec(memory_space=pltpu.VMEM)
    buf = pltpu.VMEM
    dma = pltpu.SemaphoreType.DMA
    padded = (PX, PY, BZ)
    out_now, out_prev, traces = pl.pallas_call(
        kernel,
        out_shape=(
            pltpu.VMEM(now.shape, F32),
            pltpu.VMEM(prev.shape, F32),
            pltpu.VMEM((SHOTS, STEPS, RECS), F32),
        ),
        in_specs=[any_spec, smem, smem, any_spec, any_spec, smem, smem, vmem],
        out_specs=(vmem, vmem, vmem),
        scratch_shapes=[
            buf((SHOTS,) + padded, F32),
            buf((SHOTS,) + padded, F32),
            buf((SHOTS,) + padded, F32),
            buf((BX, BY, BZ), F32),
            buf((GROUP, BY, BZ), F32),
            buf((GROUP, BY, BZ), F32),
            buf((GROUP, BY, BZ), F32),
            buf((2, GROUP, 2, BZ), F32),
            buf((2, GROUP, 2, BZ), F32),
            buf(padded, F32),
            buf(padded, F32),
            buf(padded, F32),
            buf(padded, F32),
            buf(padded, F32),
            buf((SHOTS, PY, BZ), F32),
            buf((2, SHOTS * BX, 4, BZ), F32),
            buf((2, 2, SHOTS * BX, 4, BZ), F32),
            buf((4, 8, BZ), F32),
            buf((2, 4, 8, BZ), F32),
            buf((2, SHOTS * BX, 2, BZ), F32),
            buf((2, SHOTS * BX, 2, BZ), F32),
            buf((1, BZ), jnp.int32),
            buf((NS, 1, BZ), jnp.int32),
            pltpu.SMEM((NS, 1, BZ), jnp.int32),
            buf((2 * BZ, RECS), jnp.bfloat16),
            buf((1, RECS), jnp.int32),
            buf((SHOTS * BX * BY, 2 * BZ), jnp.bfloat16),
            buf((SHOTS, 8, RECS), F32),
            buf((STEPS // 2, 8, 128), F32),
            buf((PEERS, 8, 128), F32),
            buf((STEPS // 2 - 1, NX, 8, 128), F32),
            buf((STEPS // 2 - 1, NY, 8, 128), F32),
            buf((STEPS // 2 - 1, 8, 128), F32),
            buf((SHOTS,) + padded, F32),
            buf((2 * BZ, BZ), jnp.bfloat16),
            dma((3,)), dma((NS,)), dma((NS,)), dma((2,)), dma((2,)),
            dma((GROUP,)), dma((4,)), dma((2, 2)),
            dma((2, 8)), dma((2, 8)), dma((4,)), dma((4,)), dma((2,)),
            dma((2, STEPS // 2 - 1)), dma((2, STEPS // 2 - 1)),
        ],
        compiler_params=pltpu.CompilerParams(collective_id=0, has_side_effects=True),
    )(tiles, owner, offset, now, prev, sources, wavelet, jnp.transpose(receivers, (2, 0, 1)))
    hbm = pl.BlockSpec(memory_space=pltpu.HBM)
    out_now, out_prev, traces = pl.pallas_call(
        store,
        out_shape=(
            jax.ShapeDtypeStruct(now.shape, F32),
            jax.ShapeDtypeStruct(prev.shape, F32),
            jax.ShapeDtypeStruct((SHOTS, STEPS, RECS), F32),
        ),
        in_specs=[any_spec] * 3,
        out_specs=(hbm, hbm, hbm),
        scratch_shapes=[dma((3,))],
    )(*[pltpu.with_memory_space_constraint(x, pltpu.VMEM) for x in (out_now, out_prev, traces)])
    return out_now, out_prev, jnp.transpose(traces, (0, 2, 1))[None]


def solution(mesh):
    return jax.shard_map(
        window,
        mesh=mesh,
        in_specs=(
            P(("shot", "gx"), "gy", None),
            P(),
            P("shot"),
            P("shot", None, "gx", "gy", None),
            P("shot", None, "gx", "gy", None),
            P("shot", None, None),
            P("shot", None, None),
            P("shot", None, None),
        ),
        out_specs=(
            P("shot", None, "gx", "gy", None),
            P("shot", None, "gx", "gy", None),
            P("shot", None, None, None),
        ),
        check_vma=False,
    )
```
